256 devices in a mesh: gz: 64 (over x, z, core), gy: 4 (over y).
Axes of the slice: x: 4, y: 4, z: 8, core: 2. Of those that a mesh axis runs over, the one named last changes fastest.
Arguments:
- populations: float32 [19, 64, 128, 256], P(None, 'gz', 'gy'), may hold values from 0 to 0.5, as said below
- solid_fraction: float32 [64, 128, 256], P('gz', 'gy'), may hold values from 0 to 1
- labels: int32 [64, 128, 256], P('gz', 'gy'), may hold values from 0 to 4, as said below
Outputs:
- sensitivity: float32 [64, 128, 256], P('gz', 'gy')
- adjoint_populations: float32 [19, 64, 128, 256], P(None, 'gz', 'gy')
The draws below stay inside these ranges and needn't reach their ends.
Inputs may be any that keep to these rules, and one draw needn't show every extreme that they name: `populations`: each population is w_q times a factor between 0.7 and 1.3. labels 3 appear only in the first plane along the feeding direction and 4 only in the last, in voxels that are not solid.
All inputs are finite; a program needn't handle non-finite values.
Results may differ from the reference program's by a relative error of at most 0.00028.
Values sent between devices are 32-bit elements; how exact they have to be, the bound alone decides.
A program may use at most 64 MiB of HBM per device.

```python
import jax
import jax.numpy as jnp
from jax import lax

X = 256
STEPS = 2
NZ = 64
NY = 128


def draw_populations(key, part):
    weights = jnp.array([1.0 / 3.0] + [1.0 / 18.0] * 6 + [1.0 / 36.0] * 12, jnp.float32).reshape(19, 1, 1, 1)
    shape = (19, NZ, NY, X)
    zpos = lax.broadcasted_iota(jnp.float32, shape, 1)
    amplitude = 0.1 + 0.2 * zpos / max(NZ - 1, 1)
    noise = jax.random.uniform(key, shape, jnp.float32, -1.0, 1.0)
    return weights * (1.0 + amplitude * noise)


def draw_labels(key, part):
    shape = (NZ, NY, X)
    draws = jax.random.randint(key, shape, 0, 20)
    base = jnp.where(draws < 9, 0, jnp.where(draws < 15, 1, 2))
    zpos = lax.broadcasted_iota(jnp.int32, shape, 0)
    marked = jnp.where((zpos == 0) & (base != 2), 3, base)
    marked = jnp.where((zpos == NZ - 1) & (base != 2), 4, marked)
    return marked.astype(jnp.int32)


def shard_levels(rng, dims, cuts, least, top_value):
    gain, own = 1.0, jax.random.fold_in(rng, 6)
    for position, blocks in cuts:
        steps = jnp.exp(jax.random.uniform(jax.random.fold_in(own, position), (blocks,), jnp.float32, least / len(cuts), top_value / len(cuts)))
        gain = gain * jnp.repeat(steps, dims[position] // blocks).reshape([-1 if axis == position else 1 for axis in range(len(dims))])
    return gain


def setup_inputs(seed: int = 0) -> dict:
    streams_of = jax.random.split(jax.random.key(seed), 4)
    return {
        "populations": draw_populations(jax.random.fold_in(streams_of[3], 71), 0),
        "solid_fraction": jnp.clip(1.0 * jax.random.uniform(streams_of[1], (NZ, NY, X), jnp.float32) ** shard_levels(streams_of[1], (NZ, NY, X), ((0, 64), (1, 4)), -0.2, 0.2), 0.0, 1.0),
        "labels": draw_labels(jax.random.fold_in(streams_of[3], 71), 0),
    }


OMEGA = 0.9
INLET_SPEED = 0.05

def velocity_table():
    velocities = [(0, 0, 0)]
    for axis in range(3):
        for sign in (1, -1):
            vector = [0, 0, 0]
            vector[axis] = sign
            velocities.append(tuple(vector))
    for first in range(3):
        for second in range(first + 1, 3):
            for sign_a in (1, -1):
                for sign_b in (1, -1):
                    vector = [0, 0, 0]
                    vector[first] = sign_a
                    vector[second] = sign_b
                    velocities.append(tuple(vector))
    weights = [1.0 / 3.0] + [1.0 / 18.0] * 6 + [1.0 / 36.0] * 12
    opposite = [velocities.index(tuple((-e for e in vector))) for vector in velocities]
    return (velocities, weights, opposite)

def equilibrium(density, vel_x, vel_y, vel_z):
    velocities, weights, opposite = velocity_table()
    rows = []
    speed = vel_x * vel_x + vel_y * vel_y + vel_z * vel_z
    for index in range(19):
        cx, cy, cz = velocities[index]
        along = cx * vel_x + cy * vel_y + cz * vel_z
        rows.append(weights[index] * density * (1.0 + 3.0 * along + 4.5 * along * along - 1.5 * speed))
    return jnp.stack(rows)

def moments(field):
    velocities, weights, opposite = velocity_table()
    density = lax.optimization_barrier(jnp.sum(field, axis=0))
    mom_x = sum((velocities[q][0] * field[q] for q in range(19) if velocities[q][0] != 0))
    mom_y = sum((velocities[q][1] * field[q] for q in range(19) if velocities[q][1] != 0))
    mom_z = sum((velocities[q][2] * field[q] for q in range(19) if velocities[q][2] != 0))
    return (density, mom_x, mom_y, mom_z)

def collide(field, s_eff, labels):
    velocities, weights, opposite = velocity_table()
    density, mom_x, mom_y, mom_z = moments(field)
    feq = equilibrium(density, mom_x / density, mom_y / density, mom_z / density)
    rate = jnp.where(labels == 4, jnp.ones_like(density), OMEGA * jnp.ones_like(density))
    relaxed = field - rate * (field - feq)
    flipped = jnp.stack([field[opposite[q]] for q in range(19)])
    mixed = (1.0 - s_eff) * relaxed + s_eff * flipped
    ones = jnp.ones_like(density)
    inlet = equilibrium(ones, 0.0 * ones, 0.0 * ones, INLET_SPEED * ones)
    return jnp.where(labels == 3, inlet, mixed)

def energy(field, s_eff):
    density, mom_x, mom_y, mom_z = moments(field)
    return jnp.sum((1.0 - s_eff) * (mom_x * mom_x + mom_y * mom_y + mom_z * mom_z) / density)

def stream(field):
    velocities, weights, opposite = velocity_table()
    rows = []
    for q in range(19):
        cx, cy, cz = velocities[q]
        rows.append(jnp.roll(field[q], (cz, cy, cx), axis=(0, 1, 2)))
    return jnp.stack(rows)

def reference(populations, solid_fraction, labels):

    def total_energy(start, fraction):
        s_eff = jnp.where(labels == 1, fraction, jnp.where(labels == 2, jnp.ones_like(fraction), jnp.zeros_like(fraction)))

        def advance(carry, unused):
            field, result = carry
            field = stream(collide(field, s_eff, labels))
            result = result + energy(field, s_eff)
            return ((field, result), None)
        advance = jax.checkpoint(advance)
        carry, unused = lax.scan(advance, (start, jnp.zeros((), start.dtype)), jnp.arange(STEPS, dtype=jnp.int32))
        return carry[1]
    value, grads = jax.value_and_grad(total_energy, argnums=(0, 1))(populations, solid_fraction)
    mean_energy = value / (STEPS * NZ * NY * X)
    return (grads[1] / mean_energy, grads[0] / mean_energy)
```

```python
import functools

import jax
import jax.numpy as jnp
from jax import lax
from jax.experimental import pallas as pl
from jax.experimental.pallas import tpu as pltpu
from jax.sharding import PartitionSpec as P

STEPS = 2
OMEGA = 0.9
INLET_SPEED = 0.05
ROWS = 8
TOP = 8
MESH = pl.DeviceIdType.MESH


def velocity_table():
    velocities = [(0, 0, 0)]
    for axis in range(3):
        for sign in (1, -1):
            vector = [0, 0, 0]
            vector[axis] = sign
            velocities.append(tuple(vector))
    for first in range(3):
        for second in range(first + 1, 3):
            for sign_a in (1, -1):
                for sign_b in (1, -1):
                    vector = [0, 0, 0]
                    vector[first] = sign_a
                    vector[second] = sign_b
                    velocities.append(tuple(vector))
    weights = [1.0 / 3.0] + [1.0 / 18.0] * 6 + [1.0 / 36.0] * 12
    opposite = [velocities.index(tuple((-e for e in vector))) for vector in velocities]
    return (velocities, weights, opposite)


VEL, WEIGHT, OPP = velocity_table()
INDEX = {v: q for q, v in enumerate(VEL)}
PAIRS = [(q, OPP[q]) for q in range(19) if q < OPP[q]]
UP = [(0, 0, 1), (1, 0, 1), (-1, 0, 1), (0, 1, 1), (0, -1, 1)]
DOWN = [(0, 0, -1), (1, 0, -1), (-1, 0, -1), (0, 1, -1), (0, -1, -1)]
FLAT = [v for v in VEL if v[2] == 0]
FLAT_UP = [(0, 1, 0), (1, 1, 0), (-1, 1, 0)]
FLAT_DOWN = [(0, -1, 0), (1, -1, 0), (-1, -1, 0)]


def inlet_value(q):
    along = VEL[q][2] * INLET_SPEED
    return WEIGHT[q] * (1.0 + 3.0 * along + 4.5 * along * along - 1.5 * INLET_SPEED * INLET_SPEED)


def roll_x(value, shift):
    if shift == 0:
        return value
    return pltpu.roll(value, shift % value.shape[1], 1)


def signed(terms):
    total = None
    for sign, value in terms:
        if sign == 0:
            continue
        if total is None:
            total = value if sign > 0 else -value
        else:
            total = total + value if sign > 0 else total - value
    return total


def dot_c(c, vector):
    return signed([(c[i], vector[i]) for i in range(3)])


def collide(f, a, b, s, k):
    rho = functools.reduce(lambda p, q: p + q, f)
    m = [signed([(VEL[q][i], f[q]) for q in range(19)]) for i in range(3)]
    inv = 1.0 / rho
    u = [m[i] * inv for i in range(3)]
    speed = u[0] * u[0] + u[1] * u[1] + u[2] * u[2]
    brho = b * rho
    base = brho * (1.0 - 1.5 * speed)
    post = [None] * 19
    post[0] = (a + s) * f[0] + WEIGHT[0] * base + k * inlet_value(0)
    for q, o in PAIRS:
        w = WEIGHT[q]
        along = dot_c(VEL[q], u)
        even = w * base + (4.5 * w) * (brho * along) * along
        odd = (3.0 * w) * (brho * along)
        post[q] = a * f[q] + s * f[o] + (even + odd) + k * inlet_value(q)
        post[o] = a * f[o] + s * f[q] + (even - odd) + k * inlet_value(o)
    return rho, u, speed, post


def collide_adjoint(mu, f, rho, u, speed, a, b, s):
    plus = {q: mu[q] + mu[o] for q, o in PAIRS}
    minus = {q: mu[q] - mu[o] for q, o in PAIRS}

    def weighted(table, first, second=None):
        axial, diagonal = [], []
        for q, o in PAIRS:
            c = VEL[q]
            sign = c[first] if second is None else c[first] * c[second]
            (axial if WEIGHT[q] == WEIGHT[1] else diagonal).append((sign, table[q]))
        one, two = signed(axial), signed(diagonal)
        two = two * WEIGHT[7]
        return two if one is None else one * WEIGHT[1] + two

    axial = functools.reduce(lambda p, q: p + q, [plus[q] for q, o in PAIRS if WEIGHT[q] == WEIGHT[1]])
    diagonal = functools.reduce(lambda p, q: p + q, [plus[q] for q, o in PAIRS if WEIGHT[q] != WEIGHT[1]])
    big_a = WEIGHT[0] * mu[0] + WEIGHT[1] * axial + WEIGHT[7] * diagonal
    big_b = [3.0 * weighted(minus, i) for i in range(3)]
    big_c = {}
    for i in range(3):
        for j in range(i, 3):
            big_c[i, j] = big_c[j, i] = 4.5 * weighted(plus, i, j)
    cu = [sum(big_c[i, j] * u[j] for j in range(3)) for i in range(3)]
    quad = cu[0] * u[0] + cu[1] * u[1] + cu[2] * u[2] - 1.5 * speed * big_a
    by_rho = b * (big_a - quad)
    by_m = [b * (big_b[i] + 2.0 * cu[i] - 3.0 * big_a * u[i]) for i in range(3)]
    lam = [None] * 19
    lam[0] = (a + s) * mu[0] + by_rho
    same = mu[0] * f[0]
    cross = same
    for q, o in PAIRS:
        along = dot_c(VEL[q], by_m)
        lam[q] = a * mu[q] + s * mu[o] + (by_rho + along)
        lam[o] = a * mu[o] + s * mu[q] + (by_rho - along)
        same = same + (mu[q] * f[q] + mu[o] * f[o])
        cross = cross + (mu[q] * f[o] + mu[o] * f[q])
    total = rho * (big_a + big_b[0] * u[0] + big_b[1] * u[1] + big_b[2] * u[2] + quad)
    by_s = cross - ((1.0 - OMEGA) * same + OMEGA * total)
    return lam, by_s


def scratch_list(rows, cols, n_ar):
    f32 = jnp.float32
    padded = rows + 16
    names = {
        "f0": pltpu.VMEM((19, 1, rows, cols), f32),
        "sol": pltpu.VMEM((1, rows, cols), f32),
        "lab": pltpu.VMEM((1, rows, cols), jnp.int32),
        "coef": pltpu.VMEM((3, rows, cols), f32),
        "mom0": pltpu.VMEM((4, rows, cols), f32),
        "mom1": pltpu.VMEM((4, rows, cols), f32),
        "f1": pltpu.VMEM((19, rows, cols), f32),
        "ds": pltpu.VMEM((rows, cols), f32),
        "acc": pltpu.VMEM((ROWS, cols), f32),
        "lam": pltpu.VMEM((19, 1, rows, cols), f32),
        "sens": pltpu.VMEM((1, rows, cols), f32),
        "en": pltpu.VMEM((8, 128), f32),
        "in_sem": pltpu.SemaphoreType.DMA((3,)),
        "out_sem": pltpu.SemaphoreType.DMA((3,)),
        "ssem": pltpu.SemaphoreType.DMA((4, 14)),
        "rsem": pltpu.SemaphoreType.DMA((4, 14)),
        "part": pltpu.VMEM((6, padded, cols), f32),
        "grad": pltpu.VMEM((4, padded, cols), f32),
    }
    for r, fields, edge in ((0, 5, 3), (1, 4, 2), (2, 3, 2), (3, 5, 3)):
        names[f"up{r}"] = pltpu.VMEM((fields, rows, cols), f32)
        names[f"dn{r}"] = pltpu.VMEM((fields, rows, cols), f32)
        names[f"rup{r}"] = pltpu.VMEM((fields, padded, cols), f32)
        names[f"rdn{r}"] = pltpu.VMEM((fields, padded, cols), f32)
        for name in ("yu", "yd", "ryu", "ryd"):
            names[f"{name}{r}"] = pltpu.VMEM((edge, cols), f32)
        for i in range(4):
            names[f"dg{r}{i}"] = pltpu.VMEM((1, cols), f32)
            names[f"rdg{r}{i}"] = pltpu.VMEM((1, cols), f32)
    for r in (0, 3):
        names[f"flat{r}"] = pltpu.VMEM((9, padded, cols), f32)
    for stage, count in enumerate(n_ar):
        names[f"ar{stage}"] = pltpu.VMEM((1, 128), f32)
        names[f"ras{stage}"] = pltpu.SemaphoreType.DMA((count,))
        names[f"rar{stage}"] = pltpu.SemaphoreType.DMA((count,))
        for i in range(count):
            names[f"arr{stage}_{i}"] = pltpu.VMEM((1, 128), f32)
    return names


def kernel(names, sizes, pop_ref, sol_ref, lab_ref, lam_ref, sens_ref, en_ref, *refs):
    S = dict(zip(names, refs))
    n_gz, n_gy, n_x, n_z, n_core = sizes
    rows, cols = S["ds"].shape
    chunks = rows // ROWS
    last = TOP + rows
    gz = lax.axis_index("gz")
    gy = lax.axis_index("gy")

    loads = [
        pltpu.make_async_copy(pop_ref, S["f0"], S["in_sem"].at[0]),
        pltpu.make_async_copy(sol_ref, S["sol"], S["in_sem"].at[1]),
        pltpu.make_async_copy(lab_ref, S["lab"], S["in_sem"].at[2]),
    ]
    for load in loads:
        load.start()

    def at(dz, dy):
        return (lax.rem(gz + dz + n_gz, n_gz), lax.rem(gy + dy + n_gy, n_gy))

    core = lax.rem(gz, n_core)
    zpos = lax.rem(gz // n_core, n_z)
    xpos = gz // (n_core * n_z)

    def place(dx, dz, dcore, dy):
        x = lax.rem(xpos + dx, n_x)
        z = lax.rem(zpos + dz, n_z)
        c = lax.rem(core + dcore, n_core)
        return ((x * n_z + z) * n_core + c, lax.rem(gy + dy, n_gy))

    stages = [
        [place(0, 0, dc, dy) for dc in range(n_core) for dy in range(n_gy) if (dc, dy) != (0, 0)],
        [place(0, dz, 0, 0) for dz in range(1, n_z)],
        [place(dx, 0, 0, 0) for dx in range(1, n_x)],
    ]
    near = [at(dz, dy) for dz, dy in ((1, 0), (-1, 0), (0, 1), (0, -1), (1, 1), (1, -1), (-1, 1), (-1, -1))]
    barrier = pltpu.get_barrier_semaphore()
    greeted = near + [d for stage in stages for d in stage]
    for device in greeted:
        pl.semaphore_signal(barrier, inc=1, device_id=device, device_id_type=MESH)

    def send(src, dst, r, i, device):
        copy = pltpu.make_async_remote_copy(
            src_ref=src,
            dst_ref=dst,
            send_sem=S["ssem"].at[r, i],
            recv_sem=S["rsem"].at[r, i],
            device_id=device,
            device_id_type=MESH,
        )
        copy.start()
        started[r].append(copy)

    started = [[], [], [], []]

    def send_bulk(r, k):
        src, dst = pl.ds(k * ROWS, ROWS), pl.ds(TOP + k * ROWS, ROWS)
        send(S[f"up{r}"].at[:, src, :], S[f"rup{r}"].at[:, dst, :], r, k, at(1, 0))
        send(S[f"dn{r}"].at[:, src, :], S[f"rdn{r}"].at[:, dst, :], r, chunks + k, at(-1, 0))

    def send_edges(r):
        base = 2 * chunks
        send(S[f"yu{r}"], S[f"ryu{r}"], r, base, at(0, 1))
        send(S[f"yd{r}"], S[f"ryd{r}"], r, base + 1, at(0, -1))
        for i, (dz, dy) in enumerate(((1, 1), (1, -1), (-1, 1), (-1, -1))):
            send(S[f"dg{r}{i}"], S[f"rdg{r}{i}"], r, base + 2 + i, at(dz, dy))

    def receive(r):
        for copy in started[r]:
            copy.wait_recv()

    def interior(k):
        return pl.ds(TOP + k * ROWS, ROWS)

    def moved(k, dy):
        return pl.ds(TOP + k * ROWS - dy, ROWS)

    def emit_populations(r, k, values, sense):
        here = pl.ds(k * ROWS, ROWS)
        for name, table in (("up", UP), ("dn", DOWN)):
            for i, d in enumerate(table):
                q = INDEX[tuple(sense * e for e in d)]
                value = roll_x(values[q], d[0])
                S[f"{name}{r}"][i, here, :] = value
                slot = {("up", 1): 0, ("up", -1): 1, ("dn", 1): 2, ("dn", -1): 3}.get((name, d[1]))
                if d[1] == 1 and k == chunks - 1:
                    S[f"dg{r}{slot}"][...] = value[ROWS - 1 :, :]
                if d[1] == -1 and k == 0:
                    S[f"dg{r}{slot}"][...] = value[:1, :]
        for i, d in enumerate(FLAT):
            q = INDEX[tuple(sense * e for e in d)]
            value = roll_x(values[q], d[0])
            S[f"flat{r}"][i, interior(k), :] = value
            if d[1] == 1 and k == chunks - 1:
                j = FLAT_UP.index(d)
                S[f"yu{r}"][j : j + 1, :] = value[ROWS - 1 :, :]
            if d[1] == -1 and k == 0:
                j = FLAT_DOWN.index(d)
                S[f"yd{r}"][j : j + 1, :] = value[:1, :]

    def place_edges(r):
        for i, name, row in ((0, "rup", TOP - 1), (1, "rup", last), (2, "rdn", TOP - 1), (3, "rdn", last)):
            slot = 3 if i % 2 == 0 else 4
            S[f"{name}{r}"][slot, pl.ds(row, 1), :] = S[f"rdg{r}{i}"][...]
        for j in range(3):
            S[f"flat{r}"][FLAT.index(FLAT_UP[j]), pl.ds(TOP - 1, 1), :] = S[f"ryu{r}"][j : j + 1, :]
            S[f"flat{r}"][FLAT.index(FLAT_DOWN[j]), pl.ds(last, 1), :] = S[f"ryd{r}"][j : j + 1, :]

    def gather_populations(r, k, sense):
        values = [None] * 19
        for name, table in (("rup", UP), ("rdn", DOWN), ("flat", FLAT)):
            for i, d in enumerate(table):
                q = INDEX[tuple(sense * e for e in d)]
                values[q] = S[f"{name}{r}"][i, moved(k, d[1]), :]
        return values

    def coefficients(k):
        here = pl.ds(k * ROWS, ROWS)
        return [S["coef"][i, here, :] for i in range(3)]

    def inlet(k):
        return jnp.where(S["lab"][0, pl.ds(k * ROWS, ROWS), :] == 3, 1.0, 0.0)

    for load in loads:
        load.wait()
    pl.semaphore_wait(barrier, len(greeted))
    for k in range(chunks):
        here = pl.ds(k * ROWS, ROWS)
        label = S["lab"][0, here, :]
        s = jnp.where(label == 1, S["sol"][0, here, :], jnp.where(label == 2, 1.0, 0.0))
        free = jnp.where(label == 3, 0.0, 1.0 - s)
        b = jnp.where(label == 4, free, OMEGA * free)
        a = jnp.where(label == 4, 0.0, (1.0 - OMEGA) * free)
        for i, value in enumerate((a, b, s)):
            S["coef"][i, here, :] = value
        f = [S["f0"][q, 0, here, :] for q in range(19)]
        rho, u, speed, post = collide(f, a, b, s, inlet(k))
        for i, value in enumerate((rho, *u)):
            S["mom0"][i, here, :] = value
        emit_populations(0, k, post, 1)
        send_bulk(0, k)
    send_edges(0)

    receive(0)
    place_edges(0)
    for k in range(chunks):
        here = pl.ds(k * ROWS, ROWS)
        a, b, s = coefficients(k)
        f = gather_populations(0, k, 1)
        for q in range(19):
            S["f1"][q, here, :] = f[q]
        rho, u, speed, post = collide(f, a, b, s, inlet(k))
        for i, value in enumerate((rho, *u)):
            S["mom1"][i, here, :] = value
        flow = rho * speed
        S["ds"][here, :] = -flow
        energy = (1.0 - s) * flow
        S["acc"][...] = energy if k == 0 else S["acc"][...] + energy

        def three(cy, cz):
            mid = post[INDEX[0, cy, cz]]
            right = roll_x(post[INDEX[1, cy, cz]], 1)
            left = roll_x(post[INDEX[-1, cy, cz]], -1)
            return mid + right + left, right - left

        for name, cz, slot in (("up", 1, 0), ("dn", -1, 2)):
            total, along = three(0, cz)
            ahead, behind = post[INDEX[0, 1, cz]], post[INDEX[0, -1, cz]]
            for i, value in enumerate((total, along, ahead, behind)):
                S[f"{name}1"][i, here, :] = value
            if k == chunks - 1:
                S[f"dg1{slot}"][...] = ahead[ROWS - 1 :, :]
            if k == 0:
                S[f"dg1{slot + 1}"][...] = behind[:1, :]
        send_bulk(1, k)
        for j, cy in enumerate((0, 1, -1)):
            total, along = three(cy, 0)
            S["part"][2 * j, interior(k), :] = total
            S["part"][2 * j + 1, interior(k), :] = along
            if cy == 1 and k == chunks - 1:
                S["yu1"][0:1, :] = total[ROWS - 1 :, :]
                S["yu1"][1:2, :] = along[ROWS - 1 :, :]
            if cy == -1 and k == 0:
                S["yd1"][0:1, :] = total[:1, :]
                S["yd1"][1:2, :] = along[:1, :]
    send_edges(1)

    receive(1)
    for i, name, row in ((0, "rup1", TOP - 1), (1, "rup1", last), (2, "rdn1", TOP - 1), (3, "rdn1", last)):
        S[name][2 + i % 2, pl.ds(row, 1), :] = S[f"rdg1{i}"][...]
    for j in range(2):
        S["part"][2 + j, pl.ds(TOP - 1, 1), :] = S["ryu1"][j : j + 1, :]
        S["part"][4 + j, pl.ds(last, 1), :] = S["ryd1"][j : j + 1, :]
    for k in range(chunks):
        here = pl.ds(k * ROWS, ROWS)
        s = S["coef"][2, here, :]
        above, below = {}, {}
        for table, name in ((above, "rup1"), (below, "rdn1")):
            table["sum"] = S[name][0, interior(k), :]
            table["x"] = S[name][1, interior(k), :]
            table["ahead"] = S[name][2, moved(k, 1), :]
            table["behind"] = S[name][3, moved(k, -1), :]
            table["all"] = table["sum"] + (table["ahead"] + table["behind"])
        mid, mid_x = S["part"][0, interior(k), :], S["part"][1, interior(k), :]
        ahead, ahead_x = S["part"][2, moved(k, 1), :], S["part"][3, moved(k, 1), :]
        behind, behind_x = S["part"][4, moved(k, -1), :], S["part"][5, moved(k, -1), :]
        rho = above["all"] + below["all"] + (mid + (ahead + behind))
        inv = 1.0 / rho
        ux = (above["x"] + below["x"] + (mid_x + (ahead_x + behind_x))) * inv
        uy = ((above["ahead"] - above["behind"]) + (below["ahead"] - below["behind"]) + (ahead - behind)) * inv
        uz = (above["all"] - below["all"]) * inv
        speed = ux * ux + uy * uy + uz * uz
        flow = rho * speed
        S["ds"][here, :] = S["ds"][here, :] - flow
        S["acc"][...] = S["acc"][...] + (1.0 - s) * flow
        e = (1.0 - s) * speed
        twice = 2.0 * (1.0 - s)
        x, y, z = twice * ux, twice * uy, twice * uz
        for name, w, slot in (("up", -z - e, 0), ("dn", z - e, 2)):
            for i, value in enumerate((x, y, w)):
                S[f"{name}2"][i, here, :] = value
            if k == chunks - 1:
                S[f"dg2{slot}"][...] = (w - y)[ROWS - 1 :, :]
            if k == 0:
                S[f"dg2{slot + 1}"][...] = (w + y)[:1, :]
        send_bulk(2, k)
        for i, value in enumerate((x, y - e, -y - e, e)):
            S["grad"][i, interior(k), :] = value
        if k == chunks - 1:
            S["yu2"][0:1, :] = x[ROWS - 1 :, :]
            S["yu2"][1:2, :] = (-y - e)[ROWS - 1 :, :]
        if k == 0:
            S["yd2"][0:1, :] = x[:1, :]
            S["yd2"][1:2, :] = (y - e)[:1, :]
    send_edges(2)

    sums = []

    def reduce_send(stage, value):
        S[f"ar{stage}"][...] = value
        for i, device in enumerate(stages[stage]):
            copy = pltpu.make_async_remote_copy(
                src_ref=S[f"ar{stage}"],
                dst_ref=S[f"arr{stage}_{i}"],
                send_sem=S[f"ras{stage}"].at[i],
                recv_sem=S[f"rar{stage}"].at[i],
                device_id=device,
                device_id_type=MESH,
            )
            copy.start()
            sums.append((stage, copy))

    def reduce_receive(stage):
        value = S[f"ar{stage}"][...]
        for which, copy in sums:
            if which == stage:
                copy.wait_recv()
        for i in range(len(stages[stage])):
            value = value + S[f"arr{stage}_{i}"][...]
        return value

    acc = S["acc"][...]
    acc = functools.reduce(lambda p, q: p + q, [acc[:, i : i + 128] for i in range(0, cols, 128)])
    reduce_send(0, jnp.sum(acc, axis=0, keepdims=True))

    zero_row = jnp.zeros((1, cols), jnp.float32)
    reduce_send(1, reduce_receive(0))
    receive(2)
    for i, name, row in ((0, "rup2", TOP - 1), (1, "rup2", last), (2, "rdn2", TOP - 1), (3, "rdn2", last)):
        S[name][2, pl.ds(row, 1), :] = S[f"rdg2{i}"][...]
        S[name][1, pl.ds(row, 1), :] = zero_row
    for j, slot in ((0, 0), (1, 2)):
        S["grad"][slot, pl.ds(TOP - 1, 1), :] = S["ryu2"][j : j + 1, :]
    for j, slot in ((0, 0), (1, 1)):
        S["grad"][slot, pl.ds(last, 1), :] = S["ryd2"][j : j + 1, :]
    for k in range(chunks):
        here = pl.ds(k * ROWS, ROWS)
        a, b, s = coefficients(k)
        mu = [None] * 19
        for name, cz in (("rup2", -1), ("rdn2", 1)):
            x, w = S[name][0, interior(k), :], S[name][2, interior(k), :]
            mu[INDEX[0, 0, cz]] = w
            mu[INDEX[1, 0, cz]] = roll_x(w + x, -1)
            mu[INDEX[-1, 0, cz]] = roll_x(w - x, 1)
            mu[INDEX[0, 1, cz]] = S[name][2, moved(k, -1), :] + S[name][1, moved(k, -1), :]
            mu[INDEX[0, -1, cz]] = S[name][2, moved(k, 1), :] - S[name][1, moved(k, 1), :]
        for cy, slot in ((0, 3), (1, 1), (-1, 2)):
            x, w = S["grad"][0, moved(k, -cy), :], S["grad"][slot, moved(k, -cy), :]
            w = -w if cy == 0 else w
            mu[INDEX[0, cy, 0]] = w
            mu[INDEX[1, cy, 0]] = roll_x(w + x, -1)
            mu[INDEX[-1, cy, 0]] = roll_x(w - x, 1)
        f = [S["f1"][q, here, :] for q in range(19)]
        rho, u = S["mom1"][0, here, :], [S["mom1"][i, here, :] for i in (1, 2, 3)]
        speed = u[0] * u[0] + u[1] * u[1] + u[2] * u[2]
        lam, by_s = collide_adjoint(mu, f, rho, u, speed, a, b, s)
        S["ds"][here, :] = S["ds"][here, :] + by_s
        twice = 2.0 * (1.0 - s)
        twice_u = [twice * u[i] for i in range(3)]
        e = (1.0 - s) * speed
        lam[0] = lam[0] - e
        for q, o in PAIRS:
            along = dot_c(VEL[q], twice_u)
            lam[q] = lam[q] + (along - e)
            lam[o] = lam[o] - (along + e)
        emit_populations(3, k, lam, -1)
        send_bulk(3, k)
    send_edges(3)

    reduce_send(2, reduce_receive(1))
    receive(3)
    place_edges(3)
    for k in range(chunks):
        here = pl.ds(k * ROWS, ROWS)
        a, b, s = coefficients(k)
        mu = gather_populations(3, k, -1)
        f = [S["f0"][q, 0, here, :] for q in range(19)]
        rho, u = S["mom0"][0, here, :], [S["mom0"][i, here, :] for i in (1, 2, 3)]
        speed = u[0] * u[0] + u[1] * u[1] + u[2] * u[2]
        lam, by_s = collide_adjoint(mu, f, rho, u, speed, a, b, s)
        for q in range(19):
            S["lam"][q, 0, here, :] = lam[q]
        S["sens"][0, here, :] = jnp.where(S["lab"][0, here, :] == 1, S["ds"][here, :] + by_s, 0.0)
    stores = [
        pltpu.make_async_copy(S["lam"], lam_ref, S["out_sem"].at[0]),
        pltpu.make_async_copy(S["sens"], sens_ref, S["out_sem"].at[1]),
        pltpu.make_async_copy(S["en"], en_ref, S["out_sem"].at[2]),
    ]
    stores[0].start()
    stores[1].start()
    total = jnp.sum(reduce_receive(2), axis=1, keepdims=True)
    S["en"][...] = jnp.broadcast_to(total, (8, 128))
    stores[2].start()
    for copies in started:
        for copy in copies:
            copy.wait_send()
    for stage, copy in sums:
        copy.wait_send()
    for store in stores:
        store.wait()


def on_device(sizes, populations, solid_fraction, labels):
    rows, cols = solid_fraction.shape[1:]
    n_gz, n_gy, n_x, n_z, n_core = sizes
    names = scratch_list(rows, cols, (n_core * n_gy - 1, n_z - 1, n_x - 1))
    f32 = jnp.float32
    anywhere = pl.BlockSpec(memory_space=pl.ANY)
    lam, sens, total = pl.pallas_call(
        functools.partial(kernel, tuple(names), sizes),
        out_shape=(
            jax.ShapeDtypeStruct(populations.shape, f32),
            jax.ShapeDtypeStruct(solid_fraction.shape, f32),
            jax.ShapeDtypeStruct((8, 128), f32),
        ),
        in_specs=[anywhere] * 3,
        out_specs=(anywhere,) * 3,
        scratch_shapes=list(names.values()),
        compiler_params=pltpu.CompilerParams(
            collective_id=0, has_side_effects=True, vmem_limit_bytes=24 * 1024 * 1024
        ),
        name="lattice",
    )(populations, solid_fraction, labels)
    cells = n_gz * n_gy * rows * cols
    mean_energy = total[0, 0] / (STEPS * cells)
    return (sens / mean_energy, lam / mean_energy)


def solution(mesh):
    n_gz, n_gy = mesh.shape["gz"], mesh.shape["gy"]
    n_core = 2
    n_z = 8 if n_gz % 16 == 0 else n_gz // 2
    n_x = n_gz // (n_core * n_z)
    in_specs = (P(None, "gz", "gy", None), P("gz", "gy", None), P("gz", "gy", None))
    out_specs = (P("gz", "gy", None), P(None, "gz", "gy", None))
    return jax.shard_map(
        functools.partial(on_device, (n_gz, n_gy, n_x, n_z, n_core)),
        mesh=mesh,
        in_specs=in_specs,
        out_specs=out_specs,
        check_vma=False,
    )
```

```python
import functools

import jax
import jax.numpy as jnp
from jax import lax
from jax.experimental import pallas as pl
from jax.experimental.pallas import tpu as pltpu
from jax.sharding import PartitionSpec as P

STEPS = 2
OMEGA = 0.9
INLET_SPEED = 0.05
ROWS = 8
TOP = 8
MESH = pl.DeviceIdType.MESH


def velocity_table():
    velocities = [(0, 0, 0)]
    for axis in range(3):
        for sign in (1, -1):
            vector = [0, 0, 0]
            vector[axis] = sign
            velocities.append(tuple(vector))
    for first in range(3):
        for second in range(first + 1, 3):
            for sign_a in (1, -1):
                for sign_b in (1, -1):
                    vector = [0, 0, 0]
                    vector[first] = sign_a
                    vector[second] = sign_b
                    velocities.append(tuple(vector))
    weights = [1.0 / 3.0] + [1.0 / 18.0] * 6 + [1.0 / 36.0] * 12
    opposite = [velocities.index(tuple((-e for e in vector))) for vector in velocities]
    return (velocities, weights, opposite)


VEL, WEIGHT, OPP = velocity_table()
INDEX = {v: q for q, v in enumerate(VEL)}
PAIRS = [(q, OPP[q]) for q in range(19) if q < OPP[q]]
UP = [(0, 0, 1), (1, 0, 1), (-1, 0, 1), (0, 1, 1), (0, -1, 1)]
DOWN = [(0, 0, -1), (1, 0, -1), (-1, 0, -1), (0, 1, -1), (0, -1, -1)]
FLAT = [v for v in VEL if v[2] == 0]
FLAT_UP = [(0, 1, 0), (1, 1, 0), (-1, 1, 0)]
FLAT_DOWN = [(0, -1, 0), (1, -1, 0), (-1, -1, 0)]


def inlet_value(q):
    along = VEL[q][2] * INLET_SPEED
    return WEIGHT[q] * (1.0 + 3.0 * along + 4.5 * along * along - 1.5 * INLET_SPEED * INLET_SPEED)


def roll_x(value, shift):
    if shift == 0:
        return value
    return pltpu.roll(value, shift % value.shape[1], 1)


def signed(terms):
    total = None
    for sign, value in terms:
        if sign == 0:
            continue
        if total is None:
            total = value if sign > 0 else -value
        else:
            total = total + value if sign > 0 else total - value
    return total


def dot_c(c, vector):
    return signed([(c[i], vector[i]) for i in range(3)])


def collide(f, a, b, s, k):
    rho = functools.reduce(lambda p, q: p + q, f)
    m = [signed([(VEL[q][i], f[q]) for q in range(19)]) for i in range(3)]
    inv = 1.0 / rho
    u = [m[i] * inv for i in range(3)]
    speed = u[0] * u[0] + u[1] * u[1] + u[2] * u[2]
    brho = b * rho
    base = brho * (1.0 - 1.5 * speed)
    post = [None] * 19
    post[0] = (a + s) * f[0] + WEIGHT[0] * base + k * inlet_value(0)
    for q, o in PAIRS:
        w = WEIGHT[q]
        along = dot_c(VEL[q], u)
        even = w * base + (4.5 * w) * (brho * along) * along
        odd = (3.0 * w) * (brho * along)
        post[q] = a * f[q] + s * f[o] + (even + odd) + k * inlet_value(q)
        post[o] = a * f[o] + s * f[q] + (even - odd) + k * inlet_value(o)
    return rho, u, speed, post


def collide_adjoint(mu, f, rho, u, speed, a, b, s):
    plus = {q: mu[q] + mu[o] for q, o in PAIRS}
    minus = {q: mu[q] - mu[o] for q, o in PAIRS}

    def weighted(table, first, second=None):
        axial, diagonal = [], []
        for q, o in PAIRS:
            c = VEL[q]
            sign = c[first] if second is None else c[first] * c[second]
            (axial if WEIGHT[q] == WEIGHT[1] else diagonal).append((sign, table[q]))
        one, two = signed(axial), signed(diagonal)
        two = two * WEIGHT[7]
        return two if one is None else one * WEIGHT[1] + two

    axial = functools.reduce(lambda p, q: p + q, [plus[q] for q, o in PAIRS if WEIGHT[q] == WEIGHT[1]])
    diagonal = functools.reduce(lambda p, q: p + q, [plus[q] for q, o in PAIRS if WEIGHT[q] != WEIGHT[1]])
    big_a = WEIGHT[0] * mu[0] + WEIGHT[1] * axial + WEIGHT[7] * diagonal
    big_b = [3.0 * weighted(minus, i) for i in range(3)]
    big_c = {}
    for i in range(3):
        for j in range(i, 3):
            big_c[i, j] = big_c[j, i] = 4.5 * weighted(plus, i, j)
    cu = [sum(big_c[i, j] * u[j] for j in range(3)) for i in range(3)]
    quad = cu[0] * u[0] + cu[1] * u[1] + cu[2] * u[2] - 1.5 * speed * big_a
    by_rho = b * (big_a - quad)
    by_m = [b * (big_b[i] + 2.0 * cu[i] - 3.0 * big_a * u[i]) for i in range(3)]
    lam = [None] * 19
    lam[0] = (a + s) * mu[0] + by_rho
    same = mu[0] * f[0]
    cross = same
    for q, o in PAIRS:
        along = dot_c(VEL[q], by_m)
        lam[q] = a * mu[q] + s * mu[o] + (by_rho + along)
        lam[o] = a * mu[o] + s * mu[q] + (by_rho - along)
        same = same + (mu[q] * f[q] + mu[o] * f[o])
        cross = cross + (mu[q] * f[o] + mu[o] * f[q])
    total = rho * (big_a + big_b[0] * u[0] + big_b[1] * u[1] + big_b[2] * u[2] + quad)
    by_s = cross - ((1.0 - OMEGA) * same + OMEGA * total)
    return lam, by_s


def scratch_list(rows, cols, n_ar):
    f32 = jnp.float32
    padded = rows + 16
    names = {
        "f0": pltpu.VMEM((19, 1, rows, cols), f32),
        "sol": pltpu.VMEM((1, rows, cols), f32),
        "lab": pltpu.VMEM((1, rows, cols), jnp.int32),
        "coef": pltpu.VMEM((3, rows, cols), f32),
        "mom0": pltpu.VMEM((4, rows, cols), f32),
        "mom1": pltpu.VMEM((4, rows, cols), f32),
        "f1": pltpu.VMEM((19, rows, cols), f32),
        "ds": pltpu.VMEM((rows, cols), f32),
        "acc": pltpu.VMEM((ROWS, cols), f32),
        "in_sem": pltpu.SemaphoreType.DMA((3,)),
        "ssem": pltpu.SemaphoreType.DMA((4, 14)),
        "rsem": pltpu.SemaphoreType.DMA((4, 14)),
        "part": pltpu.VMEM((6, padded, cols), f32),
        "grad": pltpu.VMEM((4, padded, cols), f32),
    }
    for r, fields, edge in ((0, 5, 3), (1, 4, 2), (2, 3, 2), (3, 5, 3)):
        names[f"up{r}"] = pltpu.VMEM((fields, rows, cols), f32)
        names[f"dn{r}"] = pltpu.VMEM((fields, rows, cols), f32)
        names[f"rup{r}"] = pltpu.VMEM((fields, padded, cols), f32)
        names[f"rdn{r}"] = pltpu.VMEM((fields, padded, cols), f32)
        for name in ("yu", "yd", "ryu", "ryd"):
            names[f"{name}{r}"] = pltpu.VMEM((edge, cols), f32)
        for i in range(4):
            names[f"dg{r}{i}"] = pltpu.VMEM((1, cols), f32)
            names[f"rdg{r}{i}"] = pltpu.VMEM((1, cols), f32)
    for r in (0, 3):
        names[f"flat{r}"] = pltpu.VMEM((9, padded, cols), f32)
    for stage, count in enumerate(n_ar):
        names[f"ar{stage}"] = pltpu.VMEM((1, 128), f32)
        names[f"ras{stage}"] = pltpu.SemaphoreType.DMA((count,))
        names[f"rar{stage}"] = pltpu.SemaphoreType.DMA((count,))
        for i in range(count):
            names[f"arr{stage}_{i}"] = pltpu.VMEM((1, 128), f32)
    return names


def kernel(names, sizes, pop_ref, sol_ref, lab_ref, lam_ref, sens_ref, en_ref, *refs):
    S = dict(zip(names, refs))
    n_gz, n_gy, n_x, n_z, n_core = sizes
    rows, cols = S["ds"].shape
    chunks = rows // ROWS
    order = [0, chunks - 1, *range(1, chunks - 1)]
    last = TOP + rows
    gz = lax.axis_index("gz")
    gy = lax.axis_index("gy")

    loads = [
        pltpu.make_async_copy(pop_ref, S["f0"], S["in_sem"].at[0]),
        pltpu.make_async_copy(sol_ref, S["sol"], S["in_sem"].at[1]),
        pltpu.make_async_copy(lab_ref, S["lab"], S["in_sem"].at[2]),
    ]
    for load in loads:
        load.start()

    def at(dz, dy):
        return (lax.rem(gz + dz + n_gz, n_gz), lax.rem(gy + dy + n_gy, n_gy))

    core = lax.rem(gz, n_core)
    zpos = lax.rem(gz // n_core, n_z)
    xpos = gz // (n_core * n_z)

    def place(dx, dz, dcore, dy):
        x = lax.rem(xpos + dx, n_x)
        z = lax.rem(zpos + dz, n_z)
        c = lax.rem(core + dcore, n_core)
        return ((x * n_z + z) * n_core + c, lax.rem(gy + dy, n_gy))

    stages = [
        [place(0, 0, dc, dy) for dc in range(n_core) for dy in range(n_gy) if (dc, dy) != (0, 0)],
        [place(0, dz, 0, 0) for dz in range(1, n_z)],
        [place(dx, 0, 0, 0) for dx in range(1, n_x)],
    ]
    near = [at(dz, dy) for dz, dy in ((1, 0), (-1, 0), (0, 1), (0, -1), (1, 1), (1, -1), (-1, 1), (-1, -1))]
    barrier = pltpu.get_barrier_semaphore()
    greeted = near + [d for stage in stages for d in stage]
    for device in greeted:
        pl.semaphore_signal(barrier, inc=1, device_id=device, device_id_type=MESH)

    def send(src, dst, r, i, device):
        copy = pltpu.make_async_remote_copy(
            src_ref=src,
            dst_ref=dst,
            send_sem=S["ssem"].at[r, i],
            recv_sem=S["rsem"].at[r, i],
            device_id=device,
            device_id_type=MESH,
        )
        copy.start()
        started[r].append(copy)

    started = [[], [], [], []]

    def send_bulk(r, k):
        src, dst = pl.ds(k * ROWS, ROWS), pl.ds(TOP + k * ROWS, ROWS)
        send(S[f"up{r}"].at[:, src, :], S[f"rup{r}"].at[:, dst, :], r, k, at(1, 0))
        send(S[f"dn{r}"].at[:, src, :], S[f"rdn{r}"].at[:, dst, :], r, chunks + k, at(-1, 0))

    def send_edges(r):
        base = 2 * chunks
        send(S[f"yu{r}"], S[f"ryu{r}"], r, base, at(0, 1))
        send(S[f"yd{r}"], S[f"ryd{r}"], r, base + 1, at(0, -1))
        for i, (dz, dy) in enumerate(((1, 1), (1, -1), (-1, 1), (-1, -1))):
            send(S[f"dg{r}{i}"], S[f"rdg{r}{i}"], r, base + 2 + i, at(dz, dy))

    def send_chunk(r, k):
        if k == chunks - 1:
            send_edges(r)
        send_bulk(r, k)

    def receive(r):
        for copy in started[r]:
            copy.wait_recv()

    def interior(k):
        return pl.ds(TOP + k * ROWS, ROWS)

    def moved(k, dy):
        return pl.ds(TOP + k * ROWS - dy, ROWS)

    def emit_populations(r, k, values, sense):
        here = pl.ds(k * ROWS, ROWS)
        for name, table in (("up", UP), ("dn", DOWN)):
            for i, d in enumerate(table):
                q = INDEX[tuple(sense * e for e in d)]
                value = roll_x(values[q], d[0])
                S[f"{name}{r}"][i, here, :] = value
                slot = {("up", 1): 0, ("up", -1): 1, ("dn", 1): 2, ("dn", -1): 3}.get((name, d[1]))
                if d[1] == 1 and k == chunks - 1:
                    S[f"dg{r}{slot}"][...] = value[ROWS - 1 :, :]
                if d[1] == -1 and k == 0:
                    S[f"dg{r}{slot}"][...] = value[:1, :]
        for i, d in enumerate(FLAT):
            q = INDEX[tuple(sense * e for e in d)]
            value = roll_x(values[q], d[0])
            S[f"flat{r}"][i, interior(k), :] = value
            if d[1] == 1 and k == chunks - 1:
                j = FLAT_UP.index(d)
                S[f"yu{r}"][j : j + 1, :] = value[ROWS - 1 :, :]
            if d[1] == -1 and k == 0:
                j = FLAT_DOWN.index(d)
                S[f"yd{r}"][j : j + 1, :] = value[:1, :]

    def place_edges(r):
        for i, name, row in ((0, "rup", TOP - 1), (1, "rup", last), (2, "rdn", TOP - 1), (3, "rdn", last)):
            slot = 3 if i % 2 == 0 else 4
            S[f"{name}{r}"][slot, pl.ds(row, 1), :] = S[f"rdg{r}{i}"][...]
        for j in range(3):
            S[f"flat{r}"][FLAT.index(FLAT_UP[j]), pl.ds(TOP - 1, 1), :] = S[f"ryu{r}"][j : j + 1, :]
            S[f"flat{r}"][FLAT.index(FLAT_DOWN[j]), pl.ds(last, 1), :] = S[f"ryd{r}"][j : j + 1, :]

    def gather_populations(r, k, sense):
        values = [None] * 19
        for name, table in (("rup", UP), ("rdn", DOWN), ("flat", FLAT)):
            for i, d in enumerate(table):
                q = INDEX[tuple(sense * e for e in d)]
                values[q] = S[f"{name}{r}"][i, moved(k, d[1]), :]
        return values

    def coefficients(k):
        here = pl.ds(k * ROWS, ROWS)
        return [S["coef"][i, here, :] for i in range(3)]

    def inlet(k):
        return jnp.where(S["lab"][0, pl.ds(k * ROWS, ROWS), :] == 3, 1.0, 0.0)

    for load in loads:
        load.wait()
    pl.semaphore_wait(barrier, len(greeted))
    for k in order:
        here = pl.ds(k * ROWS, ROWS)
        label = S["lab"][0, here, :]
        s = jnp.where(label == 1, S["sol"][0, here, :], jnp.where(label == 2, 1.0, 0.0))
        free = jnp.where(label == 3, 0.0, 1.0 - s)
        b = jnp.where(label == 4, free, OMEGA * free)
        a = jnp.where(label == 4, 0.0, (1.0 - OMEGA) * free)
        for i, value in enumerate((a, b, s)):
            S["coef"][i, here, :] = value
        f = [S["f0"][q, 0, here, :] for q in range(19)]
        rho, u, speed, post = collide(f, a, b, s, inlet(k))
        for i, value in enumerate((rho, *u)):
            S["mom0"][i, here, :] = value
        emit_populations(0, k, post, 1)
        send_chunk(0, k)

    receive(0)
    place_edges(0)
    for k in order:
        here = pl.ds(k * ROWS, ROWS)
        a, b, s = coefficients(k)
        f = gather_populations(0, k, 1)
        for q in range(19):
            S["f1"][q, here, :] = f[q]
        rho, u, speed, post = collide(f, a, b, s, inlet(k))
        for i, value in enumerate((rho, *u)):
            S["mom1"][i, here, :] = value
        flow = rho * speed
        S["ds"][here, :] = -flow
        energy = (1.0 - s) * flow
        S["acc"][...] = energy if k == 0 else S["acc"][...] + energy

        def three(cy, cz):
            mid = post[INDEX[0, cy, cz]]
            right = roll_x(post[INDEX[1, cy, cz]], 1)
            left = roll_x(post[INDEX[-1, cy, cz]], -1)
            return mid + right + left, right - left

        for name, cz, slot in (("up", 1, 0), ("dn", -1, 2)):
            total, along = three(0, cz)
            ahead, behind = post[INDEX[0, 1, cz]], post[INDEX[0, -1, cz]]
            for i, value in enumerate((total, along, ahead, behind)):
                S[f"{name}1"][i, here, :] = value
            if k == chunks - 1:
                S[f"dg1{slot}"][...] = ahead[ROWS - 1 :, :]
            if k == 0:
                S[f"dg1{slot + 1}"][...] = behind[:1, :]
        for j, cy in enumerate((0, 1, -1)):
            total, along = three(cy, 0)
            S["part"][2 * j, interior(k), :] = total
            S["part"][2 * j + 1, interior(k), :] = along
            if cy == 1 and k == chunks - 1:
                S["yu1"][0:1, :] = total[ROWS - 1 :, :]
                S["yu1"][1:2, :] = along[ROWS - 1 :, :]
            if cy == -1 and k == 0:
                S["yd1"][0:1, :] = total[:1, :]
                S["yd1"][1:2, :] = along[:1, :]
        send_chunk(1, k)

    receive(1)
    for i, name, row in ((0, "rup1", TOP - 1), (1, "rup1", last), (2, "rdn1", TOP - 1), (3, "rdn1", last)):
        S[name][2 + i % 2, pl.ds(row, 1), :] = S[f"rdg1{i}"][...]
    for j in range(2):
        S["part"][2 + j, pl.ds(TOP - 1, 1), :] = S["ryu1"][j : j + 1, :]
        S["part"][4 + j, pl.ds(last, 1), :] = S["ryd1"][j : j + 1, :]
    for k in order:
        here = pl.ds(k * ROWS, ROWS)
        s = S["coef"][2, here, :]
        above, below = {}, {}
        for table, name in ((above, "rup1"), (below, "rdn1")):
            table["sum"] = S[name][0, interior(k), :]
            table["x"] = S[name][1, interior(k), :]
            table["ahead"] = S[name][2, moved(k, 1), :]
            table["behind"] = S[name][3, moved(k, -1), :]
            table["all"] = table["sum"] + (table["ahead"] + table["behind"])
        mid, mid_x = S["part"][0, interior(k), :], S["part"][1, interior(k), :]
        ahead, ahead_x = S["part"][2, moved(k, 1), :], S["part"][3, moved(k, 1), :]
        behind, behind_x = S["part"][4, moved(k, -1), :], S["part"][5, moved(k, -1), :]
        rho = above["all"] + below["all"] + (mid + (ahead + behind))
        inv = 1.0 / rho
        ux = (above["x"] + below["x"] + (mid_x + (ahead_x + behind_x))) * inv
        uy = ((above["ahead"] - above["behind"]) + (below["ahead"] - below["behind"]) + (ahead - behind)) * inv
        uz = (above["all"] - below["all"]) * inv
        speed = ux * ux + uy * uy + uz * uz
        flow = rho * speed
        S["ds"][here, :] = S["ds"][here, :] - flow
        S["acc"][...] = S["acc"][...] + (1.0 - s) * flow
        e = (1.0 - s) * speed
        twice = 2.0 * (1.0 - s)
        x, y, z = twice * ux, twice * uy, twice * uz
        for name, w, slot in (("up", -z - e, 0), ("dn", z - e, 2)):
            for i, value in enumerate((x, y, w)):
                S[f"{name}2"][i, here, :] = value
            if k == chunks - 1:
                S[f"dg2{slot}"][...] = (w - y)[ROWS - 1 :, :]
            if k == 0:
                S[f"dg2{slot + 1}"][...] = (w + y)[:1, :]
        for i, value in enumerate((x, y - e, -y - e, e)):
            S["grad"][i, interior(k), :] = value
        if k == chunks - 1:
            S["yu2"][0:1, :] = x[ROWS - 1 :, :]
            S["yu2"][1:2, :] = (-y - e)[ROWS - 1 :, :]
        if k == 0:
            S["yd2"][0:1, :] = x[:1, :]
            S["yd2"][1:2, :] = (y - e)[:1, :]
        send_chunk(2, k)

    sums = []

    def reduce_send(stage, value):
        S[f"ar{stage}"][...] = value
        for i, device in enumerate(stages[stage]):
            copy = pltpu.make_async_remote_copy(
                src_ref=S[f"ar{stage}"],
                dst_ref=S[f"arr{stage}_{i}"],
                send_sem=S[f"ras{stage}"].at[i],
                recv_sem=S[f"rar{stage}"].at[i],
                device_id=device,
                device_id_type=MESH,
            )
            copy.start()
            sums.append((stage, copy))

    def reduce_receive(stage):
        value = S[f"ar{stage}"][...]
        for which, copy in sums:
            if which == stage:
                copy.wait_recv()
        for i in range(len(stages[stage])):
            value = value + S[f"arr{stage}_{i}"][...]
        return value

    acc = S["acc"][...]
    acc = functools.reduce(lambda p, q: p + q, [acc[:, i : i + 128] for i in range(0, cols, 128)])
    reduce_send(0, jnp.sum(acc, axis=0, keepdims=True))

    zero_row = jnp.zeros((1, cols), jnp.float32)
    reduce_send(1, reduce_receive(0))
    receive(2)
    for i, name, row in ((0, "rup2", TOP - 1), (1, "rup2", last), (2, "rdn2", TOP - 1), (3, "rdn2", last)):
        S[name][2, pl.ds(row, 1), :] = S[f"rdg2{i}"][...]
        S[name][1, pl.ds(row, 1), :] = zero_row
    for j, slot in ((0, 0), (1, 2)):
        S["grad"][slot, pl.ds(TOP - 1, 1), :] = S["ryu2"][j : j + 1, :]
    for j, slot in ((0, 0), (1, 1)):
        S["grad"][slot, pl.ds(last, 1), :] = S["ryd2"][j : j + 1, :]
    for k in order:
        here = pl.ds(k * ROWS, ROWS)
        a, b, s = coefficients(k)
        mu = [None] * 19
        for name, cz in (("rup2", -1), ("rdn2", 1)):
            x, w = S[name][0, interior(k), :], S[name][2, interior(k), :]
            mu[INDEX[0, 0, cz]] = w
            mu[INDEX[1, 0, cz]] = roll_x(w + x, -1)
            mu[INDEX[-1, 0, cz]] = roll_x(w - x, 1)
            mu[INDEX[0, 1, cz]] = S[name][2, moved(k, -1), :] + S[name][1, moved(k, -1), :]
            mu[INDEX[0, -1, cz]] = S[name][2, moved(k, 1), :] - S[name][1, moved(k, 1), :]
        for cy, slot in ((0, 3), (1, 1), (-1, 2)):
            x, w = S["grad"][0, moved(k, -cy), :], S["grad"][slot, moved(k, -cy), :]
            w = -w if cy == 0 else w
            mu[INDEX[0, cy, 0]] = w
            mu[INDEX[1, cy, 0]] = roll_x(w + x, -1)
            mu[INDEX[-1, cy, 0]] = roll_x(w - x, 1)
        f = [S["f1"][q, here, :] for q in range(19)]
        rho, u = S["mom1"][0, here, :], [S["mom1"][i, here, :] for i in (1, 2, 3)]
        speed = u[0] * u[0] + u[1] * u[1] + u[2] * u[2]
        lam, by_s = collide_adjoint(mu, f, rho, u, speed, a, b, s)
        S["ds"][here, :] = S["ds"][here, :] + by_s
        twice = 2.0 * (1.0 - s)
        twice_u = [twice * u[i] for i in range(3)]
        e = (1.0 - s) * speed
        lam[0] = lam[0] - e
        for q, o in PAIRS:
            along = dot_c(VEL[q], twice_u)
            lam[q] = lam[q] + (along - e)
            lam[o] = lam[o] - (along + e)
        emit_populations(3, k, lam, -1)
        send_chunk(3, k)

    reduce_send(2, reduce_receive(1))
    receive(3)
    place_edges(3)
    for k in order:
        here = pl.ds(k * ROWS, ROWS)
        a, b, s = coefficients(k)
        mu = gather_populations(3, k, -1)
        f = [S["f0"][q, 0, here, :] for q in range(19)]
        rho, u = S["mom0"][0, here, :], [S["mom0"][i, here, :] for i in (1, 2, 3)]
        speed = u[0] * u[0] + u[1] * u[1] + u[2] * u[2]
        lam, by_s = collide_adjoint(mu, f, rho, u, speed, a, b, s)
        for q in range(19):
            lam_ref[q, 0, here, :] = lam[q]
        sens_ref[0, here, :] = jnp.where(S["lab"][0, here, :] == 1, S["ds"][here, :] + by_s, 0.0)
    total = jnp.sum(reduce_receive(2), axis=1, keepdims=True)
    en_ref[...] = jnp.broadcast_to(total, en_ref.shape)
    for copies in started:
        for copy in copies:
            copy.wait_send()
    for stage, copy in sums:
        copy.wait_send()


def finish(scale, lam_ref, sens_ref, en_ref, out_sens, out_lam, lam, sens, sems):
    inv = 1.0 / (en_ref[...] * scale)
    rows = sens.shape[1]
    stores = [
        pltpu.make_async_copy(lam.at[pl.ds(q, 1)], out_lam.at[pl.ds(q, 1)], sems.at[q]) for q in range(19)
    ] + [pltpu.make_async_copy(sens, out_sens, sems.at[19])]
    for q in range(19):
        for k in range(rows // ROWS):
            here = pl.ds(k * ROWS, ROWS)
            lam[q, 0, here, :] = lam_ref[q, 0, here, :] * inv
        stores[q].start()
    for k in range(rows // ROWS):
        here = pl.ds(k * ROWS, ROWS)
        sens[0, here, :] = sens_ref[0, here, :] * inv
    stores[19].start()
    for store in stores:
        store.wait()


def on_device(sizes, populations, solid_fraction, labels):
    rows, cols = solid_fraction.shape[1:]
    n_gz, n_gy, n_x, n_z, n_core = sizes
    names = scratch_list(rows, cols, (n_core * n_gy - 1, n_z - 1, n_x - 1))
    f32 = jnp.float32
    in_hbm = pl.BlockSpec(memory_space=pltpu.HBM)
    in_vmem = pl.BlockSpec(memory_space=pltpu.VMEM)
    lam_type = jax.ShapeDtypeStruct(populations.shape, f32)
    sens_type = jax.ShapeDtypeStruct(solid_fraction.shape, f32)
    limit = 24 * 1024 * 1024
    lam, sens, total = pl.pallas_call(
        functools.partial(kernel, tuple(names), sizes),
        out_shape=(lam_type, sens_type, jax.ShapeDtypeStruct((ROWS, cols), f32)),
        in_specs=[in_hbm] * 3,
        out_specs=(in_vmem,) * 3,
        scratch_shapes=list(names.values()),
        compiler_params=pltpu.CompilerParams(collective_id=0, has_side_effects=True, vmem_limit_bytes=limit),
        name="lattice",
    )(*[pltpu.with_memory_space_constraint(v, pltpu.HBM) for v in (populations, solid_fraction, labels)])
    scale = 1.0 / (STEPS * n_gz * n_gy * rows * cols)
    return pl.pallas_call(
        functools.partial(finish, scale),
        out_shape=(sens_type, lam_type),
        in_specs=[in_vmem] * 3,
        out_specs=(in_hbm,) * 2,
        scratch_shapes=[
            pltpu.VMEM(populations.shape, f32),
            pltpu.VMEM(solid_fraction.shape, f32),
            pltpu.SemaphoreType.DMA((20,)),
        ],
        compiler_params=pltpu.CompilerParams(vmem_limit_bytes=4 * 1024 * 1024),
        name="finish",
    )(lam, sens, total)


def solution(mesh):
    n_gz, n_gy = mesh.shape["gz"], mesh.shape["gy"]
    n_core = 2
    n_z = 8 if n_gz % 16 == 0 else n_gz // 2
    n_x = n_gz // (n_core * n_z)
    in_specs = (P(None, "gz", "gy", None), P("gz", "gy", None), P("gz", "gy", None))
    out_specs = (P("gz", "gy", None), P(None, "gz", "gy", None))
    return jax.shard_map(
        functools.partial(on_device, (n_gz, n_gy, n_x, n_z, n_core)),
        mesh=mesh,
        in_specs=in_specs,
        out_specs=out_specs,
        check_vma=False,
    )
```

```python
import functools

import jax
import jax.numpy as jnp
from jax import lax
from jax.experimental import pallas as pl
from jax.experimental.pallas import tpu as pltpu
from jax.sharding import PartitionSpec as P

STEPS = 2
OMEGA = 0.9
INLET_SPEED = 0.05
ROWS = 8
TOP = 8
MESH = pl.DeviceIdType.MESH


def velocity_table():
    velocities = [(0, 0, 0)]
    for axis in range(3):
        for sign in (1, -1):
            vector = [0, 0, 0]
            vector[axis] = sign
            velocities.append(tuple(vector))
    for first in range(3):
        for second in range(first + 1, 3):
            for sign_a in (1, -1):
                for sign_b in (1, -1):
                    vector = [0, 0, 0]
                    vector[first] = sign_a
                    vector[second] = sign_b
                    velocities.append(tuple(vector))
    weights = [1.0 / 3.0] + [1.0 / 18.0] * 6 + [1.0 / 36.0] * 12
    opposite = [velocities.index(tuple((-e for e in vector))) for vector in velocities]
    return (velocities, weights, opposite)


VEL, WEIGHT, OPP = velocity_table()
INDEX = {v: q for q, v in enumerate(VEL)}
PAIRS = [(q, OPP[q]) for q in range(19) if q < OPP[q]]
UP = [(0, 0, 1), (1, 0, 1), (-1, 0, 1), (0, 1, 1), (0, -1, 1)]
DOWN = [(0, 0, -1), (1, 0, -1), (-1, 0, -1), (0, 1, -1), (0, -1, -1)]
FLAT = [v for v in VEL if v[2] == 0]
FLAT_UP = [(0, 1, 0), (1, 1, 0), (-1, 1, 0)]
FLAT_DOWN = [(0, -1, 0), (1, -1, 0), (-1, -1, 0)]


def inlet_value(q):
    along = VEL[q][2] * INLET_SPEED
    return WEIGHT[q] * (1.0 + 3.0 * along + 4.5 * along * along - 1.5 * INLET_SPEED * INLET_SPEED)


def roll_x(value, shift):
    if shift == 0:
        return value
    return pltpu.roll(value, shift % value.shape[1], 1)


def signed(terms):
    total = None
    for sign, value in terms:
        if sign == 0:
            continue
        if total is None:
            total = value if sign > 0 else -value
        else:
            total = total + value if sign > 0 else total - value
    return total


def dot_c(c, vector):
    return signed([(c[i], vector[i]) for i in range(3)])


def collide(f, a, b, s, k):
    rho = functools.reduce(lambda p, q: p + q, f)
    m = [signed([(VEL[q][i], f[q]) for q in range(19)]) for i in range(3)]
    inv = 1.0 / rho
    u = [m[i] * inv for i in range(3)]
    speed = u[0] * u[0] + u[1] * u[1] + u[2] * u[2]
    brho = b * rho
    base = brho * (1.0 - 1.5 * speed)
    post = [None] * 19
    post[0] = (a + s) * f[0] + WEIGHT[0] * base + k * inlet_value(0)
    for q, o in PAIRS:
        w = WEIGHT[q]
        along = dot_c(VEL[q], u)
        even = w * base + (4.5 * w) * (brho * along) * along
        odd = (3.0 * w) * (brho * along)
        post[q] = a * f[q] + s * f[o] + (even + odd) + k * inlet_value(q)
        post[o] = a * f[o] + s * f[q] + (even - odd) + k * inlet_value(o)
    return rho, u, speed, post


def collide_adjoint(mu, f, rho, u, speed, a, b, s):
    plus = {q: mu[q] + mu[o] for q, o in PAIRS}
    minus = {q: mu[q] - mu[o] for q, o in PAIRS}

    def weighted(table, first, second=None):
        axial, diagonal = [], []
        for q, o in PAIRS:
            c = VEL[q]
            sign = c[first] if second is None else c[first] * c[second]
            (axial if WEIGHT[q] == WEIGHT[1] else diagonal).append((sign, table[q]))
        one, two = signed(axial), signed(diagonal)
        two = two * WEIGHT[7]
        return two if one is None else one * WEIGHT[1] + two

    axial = functools.reduce(lambda p, q: p + q, [plus[q] for q, o in PAIRS if WEIGHT[q] == WEIGHT[1]])
    diagonal = functools.reduce(lambda p, q: p + q, [plus[q] for q, o in PAIRS if WEIGHT[q] != WEIGHT[1]])
    big_a = WEIGHT[0] * mu[0] + WEIGHT[1] * axial + WEIGHT[7] * diagonal
    big_b = [3.0 * weighted(minus, i) for i in range(3)]
    big_c = {}
    for i in range(3):
        for j in range(i, 3):
            big_c[i, j] = big_c[j, i] = 4.5 * weighted(plus, i, j)
    cu = [sum(big_c[i, j] * u[j] for j in range(3)) for i in range(3)]
    quad = cu[0] * u[0] + cu[1] * u[1] + cu[2] * u[2] - 1.5 * speed * big_a
    by_rho = b * (big_a - quad)
    by_m = [b * (big_b[i] + 2.0 * cu[i] - 3.0 * big_a * u[i]) for i in range(3)]
    lam = [None] * 19
    lam[0] = (a + s) * mu[0] + by_rho
    same = mu[0] * f[0]
    cross = same
    for q, o in PAIRS:
        along = dot_c(VEL[q], by_m)
        lam[q] = a * mu[q] + s * mu[o] + (by_rho + along)
        lam[o] = a * mu[o] + s * mu[q] + (by_rho - along)
        same = same + (mu[q] * f[q] + mu[o] * f[o])
        cross = cross + (mu[q] * f[o] + mu[o] * f[q])
    total = rho * (big_a + big_b[0] * u[0] + big_b[1] * u[1] + big_b[2] * u[2] + quad)
    by_s = cross - ((1.0 - OMEGA) * same + OMEGA * total)
    return lam, by_s


def scratch_list(rows, cols, n_ar):
    f32 = jnp.float32
    padded = rows + 16
    names = {
        "f0": pltpu.VMEM((19, 1, rows, cols), f32),
        "sol": pltpu.VMEM((1, rows, cols), f32),
        "lab": pltpu.VMEM((1, rows, cols), jnp.int32),
        "coef": pltpu.VMEM((3, rows, cols), f32),
        "mom0": pltpu.VMEM((4, rows, cols), f32),
        "mom1": pltpu.VMEM((4, rows, cols), f32),
        "f1": pltpu.VMEM((19, rows, cols), f32),
        "ds": pltpu.VMEM((rows, cols), f32),
        "acc": pltpu.VMEM((ROWS, cols), f32),
        "in_sem": pltpu.SemaphoreType.DMA((3,)),
        "ssem": pltpu.SemaphoreType.DMA((4, 14)),
        "rsem": pltpu.SemaphoreType.DMA((4, 14)),
        "part": pltpu.VMEM((6, padded, cols), f32),
        "grad": pltpu.VMEM((4, padded, cols), f32),
    }
    for r, fields, edge in ((0, 5, 3), (1, 4, 2), (2, 3, 2), (3, 5, 3)):
        names[f"up{r}"] = pltpu.VMEM((fields, rows, cols), f32)
        names[f"dn{r}"] = pltpu.VMEM((fields, rows, cols), f32)
        names[f"rup{r}"] = pltpu.VMEM((fields, padded, cols), f32)
        names[f"rdn{r}"] = pltpu.VMEM((fields, padded, cols), f32)
        for name in ("yu", "yd", "ryu", "ryd"):
            names[f"{name}{r}"] = pltpu.VMEM((edge, cols), f32)
        for i in range(4):
            names[f"dg{r}{i}"] = pltpu.VMEM((1, cols), f32)
            names[f"rdg{r}{i}"] = pltpu.VMEM((1, cols), f32)
    for r in (0, 3):
        names[f"flat{r}"] = pltpu.VMEM((9, padded, cols), f32)
    for stage, count in enumerate(n_ar):
        names[f"ar{stage}"] = pltpu.VMEM((1, 128), f32)
        names[f"ras{stage}"] = pltpu.SemaphoreType.DMA((count,))
        names[f"rar{stage}"] = pltpu.SemaphoreType.DMA((count,))
        for i in range(count):
            names[f"arr{stage}_{i}"] = pltpu.VMEM((1, 128), f32)
    return names


def kernel(names, sizes, pop_ref, sol_ref, lab_ref, lam_ref, sens_ref, en_ref, *refs):
    S = dict(zip(names, refs))
    n_gz, n_gy, n_x, n_z, n_core = sizes
    rows, cols = S["ds"].shape
    chunks = rows // ROWS
    order = [0, chunks - 1, *range(1, chunks - 1)]
    last = TOP + rows
    gz = lax.axis_index("gz")
    gy = lax.axis_index("gy")

    loads = [
        pltpu.make_async_copy(pop_ref, S["f0"], S["in_sem"].at[0]),
        pltpu.make_async_copy(sol_ref, S["sol"], S["in_sem"].at[1]),
        pltpu.make_async_copy(lab_ref, S["lab"], S["in_sem"].at[2]),
    ]
    for load in loads:
        load.start()

    def at(dz, dy):
        return (lax.rem(gz + dz + n_gz, n_gz), lax.rem(gy + dy + n_gy, n_gy))

    core = lax.rem(gz, n_core)
    zpos = lax.rem(gz // n_core, n_z)
    xpos = gz // (n_core * n_z)

    def place(dx, dz, dcore, dy):
        x = lax.rem(xpos + dx, n_x)
        z = lax.rem(zpos + dz, n_z)
        c = lax.rem(core + dcore, n_core)
        return ((x * n_z + z) * n_core + c, lax.rem(gy + dy, n_gy))

    stages = [
        [place(0, dz, dc, 0) for dz in range(n_z) for dc in range(n_core) if (dz, dc) != (0, 0)],
        [place(dx, 0, 0, dy) for dx in range(n_x) for dy in range(n_gy) if (dx, dy) != (0, 0)],
    ]
    near = [at(dz, dy) for dz, dy in ((1, 0), (-1, 0), (0, 1), (0, -1), (1, 1), (1, -1), (-1, 1), (-1, -1))]
    barrier = pltpu.get_barrier_semaphore()
    greeted = near + [d for stage in stages for d in stage]
    for device in greeted:
        pl.semaphore_signal(barrier, inc=1, device_id=device, device_id_type=MESH)

    def send(src, dst, r, i, device):
        copy = pltpu.make_async_remote_copy(
            src_ref=src,
            dst_ref=dst,
            send_sem=S["ssem"].at[r, i],
            recv_sem=S["rsem"].at[r, i],
            device_id=device,
            device_id_type=MESH,
        )
        copy.start()
        started[r][i] = copy

    started = [{}, {}, {}, {}]

    def send_bulk(r, k):
        src, dst = pl.ds(k * ROWS, ROWS), pl.ds(TOP + k * ROWS, ROWS)
        send(S[f"up{r}"].at[:, src, :], S[f"rup{r}"].at[:, dst, :], r, k, at(1, 0))
        send(S[f"dn{r}"].at[:, src, :], S[f"rdn{r}"].at[:, dst, :], r, chunks + k, at(-1, 0))

    def send_edges(r):
        base = 2 * chunks
        send(S[f"yu{r}"], S[f"ryu{r}"], r, base, at(0, 1))
        send(S[f"yd{r}"], S[f"ryd{r}"], r, base + 1, at(0, -1))
        for i, (dz, dy) in enumerate(((1, 1), (1, -1), (-1, 1), (-1, -1))):
            send(S[f"dg{r}{i}"], S[f"rdg{r}{i}"], r, base + 2 + i, at(dz, dy))

    def send_chunk(r, k):
        if k == chunks - 1:
            send_edges(r)
        send_bulk(r, k)

    landed = set()

    def receive_part(r, i):
        if (r, i) not in landed:
            landed.add((r, i))
            started[r][i].wait_recv()

    def receive(r, k):
        for j in (k - 1, k, k + 1):
            if 0 <= j < chunks:
                receive_part(r, j)
                receive_part(r, chunks + j)
        first = (r, 2 * chunks) not in landed
        for i in range(6):
            receive_part(r, 2 * chunks + i)
        return first

    def interior(k):
        return pl.ds(TOP + k * ROWS, ROWS)

    def moved(k, dy):
        return pl.ds(TOP + k * ROWS - dy, ROWS)

    def emit_populations(r, k, values, sense):
        here = pl.ds(k * ROWS, ROWS)
        for name, table in (("up", UP), ("dn", DOWN)):
            for i, d in enumerate(table):
                q = INDEX[tuple(sense * e for e in d)]
                value = roll_x(values[q], d[0])
                S[f"{name}{r}"][i, here, :] = value
                slot = {("up", 1): 0, ("up", -1): 1, ("dn", 1): 2, ("dn", -1): 3}.get((name, d[1]))
                if d[1] == 1 and k == chunks - 1:
                    S[f"dg{r}{slot}"][...] = value[ROWS - 1 :, :]
                if d[1] == -1 and k == 0:
                    S[f"dg{r}{slot}"][...] = value[:1, :]
        for i, d in enumerate(FLAT):
            q = INDEX[tuple(sense * e for e in d)]
            value = roll_x(values[q], d[0])
            S[f"flat{r}"][i, interior(k), :] = value
            if d[1] == 1 and k == chunks - 1:
                j = FLAT_UP.index(d)
                S[f"yu{r}"][j : j + 1, :] = value[ROWS - 1 :, :]
            if d[1] == -1 and k == 0:
                j = FLAT_DOWN.index(d)
                S[f"yd{r}"][j : j + 1, :] = value[:1, :]

    def place_edges(r):
        for i, name, row in ((0, "rup", TOP - 1), (1, "rup", last), (2, "rdn", TOP - 1), (3, "rdn", last)):
            slot = 3 if i % 2 == 0 else 4
            S[f"{name}{r}"][slot, pl.ds(row, 1), :] = S[f"rdg{r}{i}"][...]
        for j in range(3):
            S[f"flat{r}"][FLAT.index(FLAT_UP[j]), pl.ds(TOP - 1, 1), :] = S[f"ryu{r}"][j : j + 1, :]
            S[f"flat{r}"][FLAT.index(FLAT_DOWN[j]), pl.ds(last, 1), :] = S[f"ryd{r}"][j : j + 1, :]

    def gather_populations(r, k, sense):
        values = [None] * 19
        for name, table in (("rup", UP), ("rdn", DOWN), ("flat", FLAT)):
            for i, d in enumerate(table):
                q = INDEX[tuple(sense * e for e in d)]
                values[q] = S[f"{name}{r}"][i, moved(k, d[1]), :]
        return values

    def coefficients(k):
        here = pl.ds(k * ROWS, ROWS)
        return [S["coef"][i, here, :] for i in range(3)]

    def inlet(k):
        return jnp.where(S["lab"][0, pl.ds(k * ROWS, ROWS), :] == 3, 1.0, 0.0)

    for load in loads:
        load.wait()
    for k in order:
        here = pl.ds(k * ROWS, ROWS)
        label = S["lab"][0, here, :]
        s = jnp.where(label == 1, S["sol"][0, here, :], jnp.where(label == 2, 1.0, 0.0))
        free = jnp.where(label == 3, 0.0, 1.0 - s)
        b = jnp.where(label == 4, free, OMEGA * free)
        a = jnp.where(label == 4, 0.0, (1.0 - OMEGA) * free)
        for i, value in enumerate((a, b, s)):
            S["coef"][i, here, :] = value
        f = [S["f0"][q, 0, here, :] for q in range(19)]
        rho, u, speed, post = collide(f, a, b, s, inlet(k))
        for i, value in enumerate((rho, *u)):
            S["mom0"][i, here, :] = value
        emit_populations(0, k, post, 1)

    pl.semaphore_wait(barrier, len(greeted))
    send_edges(0)
    for k in order:
        send_bulk(0, k)

    for k in order:
        here = pl.ds(k * ROWS, ROWS)
        if receive(0, k):
            place_edges(0)
        a, b, s = coefficients(k)
        f = gather_populations(0, k, 1)
        for q in range(19):
            S["f1"][q, here, :] = f[q]
        rho, u, speed, post = collide(f, a, b, s, inlet(k))
        for i, value in enumerate((rho, *u)):
            S["mom1"][i, here, :] = value
        flow = rho * speed
        S["ds"][here, :] = -flow
        energy = (1.0 - s) * flow
        S["acc"][...] = energy if k == 0 else S["acc"][...] + energy

        def three(cy, cz):
            mid = post[INDEX[0, cy, cz]]
            right = roll_x(post[INDEX[1, cy, cz]], 1)
            left = roll_x(post[INDEX[-1, cy, cz]], -1)
            return mid + right + left, right - left

        for name, cz, slot in (("up", 1, 0), ("dn", -1, 2)):
            total, along = three(0, cz)
            ahead, behind = post[INDEX[0, 1, cz]], post[INDEX[0, -1, cz]]
            for i, value in enumerate((total, along, ahead, behind)):
                S[f"{name}1"][i, here, :] = value
            if k == chunks - 1:
                S[f"dg1{slot}"][...] = ahead[ROWS - 1 :, :]
            if k == 0:
                S[f"dg1{slot + 1}"][...] = behind[:1, :]
        for j, cy in enumerate((0, 1, -1)):
            total, along = three(cy, 0)
            S["part"][2 * j, interior(k), :] = total
            S["part"][2 * j + 1, interior(k), :] = along
            if cy == 1 and k == chunks - 1:
                S["yu1"][0:1, :] = total[ROWS - 1 :, :]
                S["yu1"][1:2, :] = along[ROWS - 1 :, :]
            if cy == -1 and k == 0:
                S["yd1"][0:1, :] = total[:1, :]
                S["yd1"][1:2, :] = along[:1, :]
        send_chunk(1, k)

    def place_moments():
        for i, name, row in ((0, "rup1", TOP - 1), (1, "rup1", last), (2, "rdn1", TOP - 1), (3, "rdn1", last)):
            S[name][2 + i % 2, pl.ds(row, 1), :] = S[f"rdg1{i}"][...]
        for j in range(2):
            S["part"][2 + j, pl.ds(TOP - 1, 1), :] = S["ryu1"][j : j + 1, :]
            S["part"][4 + j, pl.ds(last, 1), :] = S["ryd1"][j : j + 1, :]

    for k in order:
        here = pl.ds(k * ROWS, ROWS)
        if receive(1, k):
            place_moments()
        s = S["coef"][2, here, :]
        above, below = {}, {}
        for table, name in ((above, "rup1"), (below, "rdn1")):
            table["sum"] = S[name][0, interior(k), :]
            table["x"] = S[name][1, interior(k), :]
            table["ahead"] = S[name][2, moved(k, 1), :]
            table["behind"] = S[name][3, moved(k, -1), :]
            table["all"] = table["sum"] + (table["ahead"] + table["behind"])
        mid, mid_x = S["part"][0, interior(k), :], S["part"][1, interior(k), :]
        ahead, ahead_x = S["part"][2, moved(k, 1), :], S["part"][3, moved(k, 1), :]
        behind, behind_x = S["part"][4, moved(k, -1), :], S["part"][5, moved(k, -1), :]
        rho = above["all"] + below["all"] + (mid + (ahead + behind))
        inv = 1.0 / rho
        ux = (above["x"] + below["x"] + (mid_x + (ahead_x + behind_x))) * inv
        uy = ((above["ahead"] - above["behind"]) + (below["ahead"] - below["behind"]) + (ahead - behind)) * inv
        uz = (above["all"] - below["all"]) * inv
        speed = ux * ux + uy * uy + uz * uz
        flow = rho * speed
        S["ds"][here, :] = S["ds"][here, :] - flow
        S["acc"][...] = S["acc"][...] + (1.0 - s) * flow
        e = (1.0 - s) * speed
        twice = 2.0 * (1.0 - s)
        x, y, z = twice * ux, twice * uy, twice * uz
        for name, w, slot in (("up", -z - e, 0), ("dn", z - e, 2)):
            for i, value in enumerate((x, y, w)):
                S[f"{name}2"][i, here, :] = value
            if k == chunks - 1:
                S[f"dg2{slot}"][...] = (w - y)[ROWS - 1 :, :]
            if k == 0:
                S[f"dg2{slot + 1}"][...] = (w + y)[:1, :]
        for i, value in enumerate((x, y - e, -y - e, e)):
            S["grad"][i, interior(k), :] = value
        if k == chunks - 1:
            S["yu2"][0:1, :] = x[ROWS - 1 :, :]
            S["yu2"][1:2, :] = (-y - e)[ROWS - 1 :, :]
        if k == 0:
            S["yd2"][0:1, :] = x[:1, :]
            S["yd2"][1:2, :] = (y - e)[:1, :]
        send_chunk(2, k)

    sums = []

    def reduce_send(stage, value):
        S[f"ar{stage}"][...] = value
        for i, device in enumerate(stages[stage]):
            copy = pltpu.make_async_remote_copy(
                src_ref=S[f"ar{stage}"],
                dst_ref=S[f"arr{stage}_{i}"],
                send_sem=S[f"ras{stage}"].at[i],
                recv_sem=S[f"rar{stage}"].at[i],
                device_id=device,
                device_id_type=MESH,
            )
            copy.start()
            sums.append((stage, copy))

    def reduce_receive(stage):
        value = S[f"ar{stage}"][...]
        for which, copy in sums:
            if which == stage:
                copy.wait_recv()
        for i in range(len(stages[stage])):
            value = value + S[f"arr{stage}_{i}"][...]
        return value

    acc = S["acc"][...]
    acc = functools.reduce(lambda p, q: p + q, [acc[:, i : i + 128] for i in range(0, cols, 128)])
    reduce_send(0, jnp.sum(acc, axis=0, keepdims=True))

    zero_row = jnp.zeros((1, cols), jnp.float32)
    def place_gradients():
        for i, name, row in ((0, "rup2", TOP - 1), (1, "rup2", last), (2, "rdn2", TOP - 1), (3, "rdn2", last)):
            S[name][2, pl.ds(row, 1), :] = S[f"rdg2{i}"][...]
            S[name][1, pl.ds(row, 1), :] = zero_row
        for j, slot in ((0, 0), (1, 2)):
            S["grad"][slot, pl.ds(TOP - 1, 1), :] = S["ryu2"][j : j + 1, :]
        for j, slot in ((0, 0), (1, 1)):
            S["grad"][slot, pl.ds(last, 1), :] = S["ryd2"][j : j + 1, :]

    for k in order:
        here = pl.ds(k * ROWS, ROWS)
        if receive(2, k):
            place_gradients()
        if k == order[1]:
            reduce_send(1, reduce_receive(0))
        a, b, s = coefficients(k)
        mu = [None] * 19
        for name, cz in (("rup2", -1), ("rdn2", 1)):
            x, w = S[name][0, interior(k), :], S[name][2, interior(k), :]
            mu[INDEX[0, 0, cz]] = w
            mu[INDEX[1, 0, cz]] = roll_x(w + x, -1)
            mu[INDEX[-1, 0, cz]] = roll_x(w - x, 1)
            mu[INDEX[0, 1, cz]] = S[name][2, moved(k, -1), :] + S[name][1, moved(k, -1), :]
            mu[INDEX[0, -1, cz]] = S[name][2, moved(k, 1), :] - S[name][1, moved(k, 1), :]
        for cy, slot in ((0, 3), (1, 1), (-1, 2)):
            x, w = S["grad"][0, moved(k, -cy), :], S["grad"][slot, moved(k, -cy), :]
            w = -w if cy == 0 else w
            mu[INDEX[0, cy, 0]] = w
            mu[INDEX[1, cy, 0]] = roll_x(w + x, -1)
            mu[INDEX[-1, cy, 0]] = roll_x(w - x, 1)
        f = [S["f1"][q, here, :] for q in range(19)]
        rho, u = S["mom1"][0, here, :], [S["mom1"][i, here, :] for i in (1, 2, 3)]
        speed = u[0] * u[0] + u[1] * u[1] + u[2] * u[2]
        lam, by_s = collide_adjoint(mu, f, rho, u, speed, a, b, s)
        S["ds"][here, :] = S["ds"][here, :] + by_s
        twice = 2.0 * (1.0 - s)
        twice_u = [twice * u[i] for i in range(3)]
        e = (1.0 - s) * speed
        lam[0] = lam[0] - e
        for q, o in PAIRS:
            along = dot_c(VEL[q], twice_u)
            lam[q] = lam[q] + (along - e)
            lam[o] = lam[o] - (along + e)
        emit_populations(3, k, lam, -1)
        send_chunk(3, k)

    for k in order:
        here = pl.ds(k * ROWS, ROWS)
        if receive(3, k):
            place_edges(3)
        a, b, s = coefficients(k)
        mu = gather_populations(3, k, -1)
        f = [S["f0"][q, 0, here, :] for q in range(19)]
        rho, u = S["mom0"][0, here, :], [S["mom0"][i, here, :] for i in (1, 2, 3)]
        speed = u[0] * u[0] + u[1] * u[1] + u[2] * u[2]
        lam, by_s = collide_adjoint(mu, f, rho, u, speed, a, b, s)
        for q in range(19):
            lam_ref[q, 0, here, :] = lam[q]
        sens_ref[0, here, :] = jnp.where(S["lab"][0, here, :] == 1, S["ds"][here, :] + by_s, 0.0)
    total = jnp.sum(reduce_receive(1), axis=1, keepdims=True)
    en_ref[...] = jnp.broadcast_to(total, en_ref.shape)
    for copies in started:
        for copy in copies.values():
            copy.wait_send()
    for stage, copy in sums:
        copy.wait_send()


def finish(scale, lam_ref, sens_ref, en_ref, out_sens, out_lam, lam, sens, sems):
    inv = 1.0 / (en_ref[...] * scale)
    rows = sens.shape[1]
    stores = [
        pltpu.make_async_copy(lam.at[pl.ds(q, 1)], out_lam.at[pl.ds(q, 1)], sems.at[q]) for q in range(19)
    ] + [pltpu.make_async_copy(sens, out_sens, sems.at[19])]
    for q in range(19):
        for k in range(rows // ROWS):
            here = pl.ds(k * ROWS, ROWS)
            lam[q, 0, here, :] = lam_ref[q, 0, here, :] * inv
        stores[q].start()
    for k in range(rows // ROWS):
        here = pl.ds(k * ROWS, ROWS)
        sens[0, here, :] = sens_ref[0, here, :] * inv
    stores[19].start()
    for store in stores:
        store.wait()


def on_device(sizes, populations, solid_fraction, labels):
    rows, cols = solid_fraction.shape[1:]
    n_gz, n_gy, n_x, n_z, n_core = sizes
    names = scratch_list(rows, cols, (n_core * n_z - 1, n_x * n_gy - 1))
    f32 = jnp.float32
    in_hbm = pl.BlockSpec(memory_space=pltpu.HBM)
    in_vmem = pl.BlockSpec(memory_space=pltpu.VMEM)
    lam_type = jax.ShapeDtypeStruct(populations.shape, f32)
    sens_type = jax.ShapeDtypeStruct(solid_fraction.shape, f32)
    limit = 24 * 1024 * 1024
    lam, sens, total = pl.pallas_call(
        functools.partial(kernel, tuple(names), sizes),
        out_shape=(lam_type, sens_type, jax.ShapeDtypeStruct((ROWS, cols), f32)),
        in_specs=[in_hbm] * 3,
        out_specs=(in_vmem,) * 3,
        scratch_shapes=list(names.values()),
        compiler_params=pltpu.CompilerParams(collective_id=0, has_side_effects=True, vmem_limit_bytes=limit),
        name="lattice",
    )(*[pltpu.with_memory_space_constraint(v, pltpu.HBM) for v in (populations, solid_fraction, labels)])
    scale = 1.0 / (STEPS * n_gz * n_gy * rows * cols)
    return pl.pallas_call(
        functools.partial(finish, scale),
        out_shape=(sens_type, lam_type),
        in_specs=[in_vmem] * 3,
        out_specs=(in_hbm,) * 2,
        scratch_shapes=[
            pltpu.VMEM(populations.shape, f32),
            pltpu.VMEM(solid_fraction.shape, f32),
            pltpu.SemaphoreType.DMA((20,)),
        ],
        compiler_params=pltpu.CompilerParams(vmem_limit_bytes=4 * 1024 * 1024),
        name="finish",
    )(lam, sens, total)


def solution(mesh):
    n_gz, n_gy = mesh.shape["gz"], mesh.shape["gy"]
    n_core = 2
    n_z = 8 if n_gz % 16 == 0 else n_gz // 2
    n_x = n_gz // (n_core * n_z)
    in_specs = (P(None, "gz", "gy", None), P("gz", "gy", None), P("gz", "gy", None))
    out_specs = (P("gz", "gy", None), P(None, "gz", "gy", None))
    return jax.shard_map(
        functools.partial(on_device, (n_gz, n_gy, n_x, n_z, n_core)),
        mesh=mesh,
        in_specs=in_specs,
        out_specs=out_specs,
        check_vma=False,
    )
```

```python
import functools
import types

import jax
import jax.numpy as jnp
from jax import lax
from jax.experimental import pallas as pl
from jax.experimental.pallas import tpu as pltpu
from jax.sharding import PartitionSpec as P

STEPS = 2
OMEGA = 0.9
INLET_SPEED = 0.05
ROWS = 8
TOP = 8
MESH = pl.DeviceIdType.MESH
LANES = 128
EDGE_ROWS = ((0, 4), (1, 8), (2, 2), (3, 4))
GROUPS = [(r, g) for r in (0, 2, 3, 4) for g in ("A", "B", "E")]
GROUPS += [(1, side + g) for side in ("f", "n") for g in ("A", "B", "E")] + [(5, "A"), (6, "A"), (7, "A")]


def velocity_table():
    velocities = [(0, 0, 0)]
    for axis in range(3):
        for sign in (1, -1):
            vector = [0, 0, 0]
            vector[axis] = sign
            velocities.append(tuple(vector))
    for first in range(3):
        for second in range(first + 1, 3):
            for sign_a in (1, -1):
                for sign_b in (1, -1):
                    vector = [0, 0, 0]
                    vector[first] = sign_a
                    vector[second] = sign_b
                    velocities.append(tuple(vector))
    weights = [1.0 / 3.0] + [1.0 / 18.0] * 6 + [1.0 / 36.0] * 12
    opposite = [velocities.index(tuple((-e for e in vector))) for vector in velocities]
    return (velocities, weights, opposite)


VEL, WEIGHT, OPP = velocity_table()
INDEX = {v: q for q, v in enumerate(VEL)}
PAIRS = [(q, OPP[q]) for q in range(19) if q < OPP[q]]
UP = [(0, 0, 1), (1, 0, 1), (-1, 0, 1), (0, 1, 1), (0, -1, 1)]
DOWN = [(0, 0, -1), (1, 0, -1), (-1, 0, -1), (0, 1, -1), (0, -1, -1)]
FLAT = [v for v in VEL if v[2] == 0]
FLAT_UP = [(0, 1, 0), (1, 1, 0), (-1, 1, 0)]
FLAT_DOWN = [(0, -1, 0), (1, -1, 0), (-1, -1, 0)]


def inlet_value(q):
    along = VEL[q][2] * INLET_SPEED
    return WEIGHT[q] * (1.0 + 3.0 * along + 4.5 * along * along - 1.5 * INLET_SPEED * INLET_SPEED)


def roll_x(value, shift):
    if shift == 0:
        return value
    return pltpu.roll(value, shift % value.shape[1], 1)


def signed(terms):
    total = None
    for sign, value in terms:
        if sign == 0:
            continue
        if total is None:
            total = value if sign > 0 else -value
        else:
            total = total + value if sign > 0 else total - value
    return total


def dot_c(c, vector):
    return signed([(c[i], vector[i]) for i in range(3)])


def collide(f, a, b, s, k):
    rho = functools.reduce(lambda p, q: p + q, f)
    m = [signed([(VEL[q][i], f[q]) for q in range(19)]) for i in range(3)]
    inv = 1.0 / rho
    u = [m[i] * inv for i in range(3)]
    speed = u[0] * u[0] + u[1] * u[1] + u[2] * u[2]
    brho = b * rho
    base = brho * (1.0 - 1.5 * speed)
    post = [None] * 19
    post[0] = (a + s) * f[0] + WEIGHT[0] * base + k * inlet_value(0)
    for q, o in PAIRS:
        w = WEIGHT[q]
        along = dot_c(VEL[q], u)
        even = w * base + (4.5 * w) * (brho * along) * along
        odd = (3.0 * w) * (brho * along)
        post[q] = a * f[q] + s * f[o] + (even + odd) + k * inlet_value(q)
        post[o] = a * f[o] + s * f[q] + (even - odd) + k * inlet_value(o)
    return rho, u, speed, post


def collide_adjoint(mu, f, rho, u, speed, a, b, s):
    plus = {q: mu[q] + mu[o] for q, o in PAIRS}
    minus = {q: mu[q] - mu[o] for q, o in PAIRS}

    def weighted(table, first, second=None):
        axial, diagonal = [], []
        for q, o in PAIRS:
            c = VEL[q]
            sign = c[first] if second is None else c[first] * c[second]
            (axial if WEIGHT[q] == WEIGHT[1] else diagonal).append((sign, table[q]))
        one, two = signed(axial), signed(diagonal)
        two = two * WEIGHT[7]
        return two if one is None else one * WEIGHT[1] + two

    axial = functools.reduce(lambda p, q: p + q, [plus[q] for q, o in PAIRS if WEIGHT[q] == WEIGHT[1]])
    diagonal = functools.reduce(lambda p, q: p + q, [plus[q] for q, o in PAIRS if WEIGHT[q] != WEIGHT[1]])
    big_a = WEIGHT[0] * mu[0] + WEIGHT[1] * axial + WEIGHT[7] * diagonal
    big_b = [3.0 * weighted(minus, i) for i in range(3)]
    big_c = {}
    for i in range(3):
        for j in range(i, 3):
            big_c[i, j] = big_c[j, i] = 4.5 * weighted(plus, i, j)
    cu = [sum(big_c[i, j] * u[j] for j in range(3)) for i in range(3)]
    quad = cu[0] * u[0] + cu[1] * u[1] + cu[2] * u[2] - 1.5 * speed * big_a
    by_rho = b * (big_a - quad)
    by_m = [b * (big_b[i] + 2.0 * cu[i] - 3.0 * big_a * u[i]) for i in range(3)]
    lam = [None] * 19
    lam[0] = (a + s) * mu[0] + by_rho
    same = mu[0] * f[0]
    cross = same
    for q, o in PAIRS:
        along = dot_c(VEL[q], by_m)
        lam[q] = a * mu[q] + s * mu[o] + (by_rho + along)
        lam[o] = a * mu[o] + s * mu[q] + (by_rho - along)
        same = same + (mu[q] * f[q] + mu[o] * f[o])
        cross = cross + (mu[q] * f[o] + mu[o] * f[q])
    total = rho * (big_a + big_b[0] * u[0] + big_b[1] * u[1] + big_b[2] * u[2] + quad)
    by_s = cross - ((1.0 - OMEGA) * same + OMEGA * total)
    return lam, by_s


def scratch_tree(rows, cols, n_ar):
    def vmem(*shape):
        return pltpu.VMEM(shape, jnp.float32)

    padded = rows + 16
    dma = pltpu.SemaphoreType.DMA
    return dict(
        f0=vmem(19, 1, rows, cols),
        sol=vmem(1, rows, cols),
        lab=pltpu.VMEM((1, rows, cols), jnp.int32),
        coef=vmem(3, rows, cols),
        mom0=vmem(4, rows, cols),
        mom1=vmem(4, rows, cols),
        f1=vmem(19, rows, cols),
        ds=vmem(rows, cols),
        acc=vmem(ROWS, cols),
        in_sem=dma((1,)),
        ssem=dma((8,)),
        rsem=dma((len(GROUPS),)),
        some=vmem(3 * 19 * rows * cols // LANES, 1, LANES),
        part=vmem(6, padded, cols),
        grad=vmem(4, padded, cols),
        out1=vmem(2, 4, padded, cols),
        in1=vmem(2, 4, padded, cols),
        side=vmem(2, 3, padded, cols),
        mine=vmem(3, rows, cols),
        rest=vmem(4, rows, cols),
        far_rest=vmem(4, rows, cols),
        far_s=vmem(rows, cols),
        s_hi=vmem(1, cols),
        s_lo=vmem(1, cols),
        far_s_hi=vmem(1, cols),
        far_s_lo=vmem(1, cols),
        rest_hi=vmem(4, cols),
        rest_lo=vmem(4, cols),
        far_rest_hi=vmem(4, cols),
        far_rest_lo=vmem(4, cols),
        yu={r: vmem(n, cols) for r, n in EDGE_ROWS},
        yd={r: vmem(n, cols) for r, n in EDGE_ROWS},
        ryu={r: vmem(n, cols) for r, n in EDGE_ROWS},
        ryd={r: vmem(n, cols) for r, n in EDGE_ROWS},
        up={r: vmem(5, rows, cols) for r in (0, 3)},
        dn={r: vmem(5, rows, cols) for r in (0, 3)},
        rup={r: vmem(5, padded, cols) for r in (0, 3)},
        rdn={r: vmem(5, padded, cols) for r in (0, 3)},
        flat={r: vmem(9, padded, cols) for r in (0, 3)},
        dg=[[vmem(1, cols) for i in range(4)] for r in range(4)],
        rdg=[[vmem(1, cols) for i in range(4)] for r in range(4)],
        ar=[vmem(1, LANES) for count in n_ar],
        arr=[[vmem(1, LANES) for i in range(count)] for count in n_ar],
    )


def kernel(tree, sizes, pop_ref, sol_ref, lab_ref, lam_ref, sens_ref, en_ref, *refs):
    S = types.SimpleNamespace(**jax.tree.unflatten(tree, refs))
    n_gz, n_gy, n_x, n_z, n_core = sizes
    rows, cols = S.ds.shape
    chunks = rows // ROWS
    order = [0, chunks - 1, *range(1, chunks - 1)]
    last = TOP + rows
    gz = lax.axis_index("gz")
    gy = lax.axis_index("gy")

    def size(ref):
        return functools.reduce(lambda p, q: p * q, ref.shape) // LANES

    def wait_bytes(count, sem):
        some = S.some.at[pl.ds(0, count)]
        pltpu.make_async_copy(some, some, sem).wait()

    loads = ((pop_ref, S.f0), (sol_ref, S.sol), (lab_ref, S.lab))
    for src, dst in loads:
        pltpu.make_async_copy(src, dst, S.in_sem.at[0]).start()

    def at(dz, dy):
        return (lax.rem(gz + dz + n_gz, n_gz), lax.rem(gy + dy + n_gy, n_gy))

    core = lax.rem(gz, n_core)
    zpos = lax.rem(gz // n_core, n_z)
    xpos = gz // (n_core * n_z)

    def place(dx, dz, dcore, dy):
        x = lax.rem(xpos + dx, n_x)
        z = lax.rem(zpos + dz, n_z)
        c = lax.rem(core + dcore, n_core)
        return ((x * n_z + z) * n_core + c, lax.rem(gy + dy, n_gy))

    stages = [
        [place(0, dz, dc, 0) for dz in range(n_z) for dc in range(n_core) if (dz, dc) != (0, 0)],
        [place(dx, 0, 0, dy) for dx in range(n_x) for dy in range(n_gy) if (dx, dy) != (0, 0)],
    ]
    near = [at(dz, dy) for dz, dy in ((1, 0), (-1, 0), (0, 1), (0, -1), (1, 1), (1, -1), (-1, 1), (-1, -1))]
    barrier = pltpu.get_barrier_semaphore()
    greeted = near + stages[0] + [place(dx, 0, 0, 0) for dx in range(1, n_x)]
    for device in greeted:
        pl.semaphore_signal(barrier, inc=1, device_id=device, device_id_type=MESH)

    sent_bytes, group_bytes = {}, {}

    def group_of(r, i):
        if i >= base:
            name = "E"
        else:
            name = "B" if i % chunks == order[-1] and r != 5 else "A"
        if r == 1:
            near_side = i - base not in (2, 3) if i >= base else i >= chunks
            name = ("n" if near_side else "f") + name
        return (r, name)

    def send(src, dst, r, i, device):
        group = group_of(r, i)
        pltpu.make_async_remote_copy(
            src_ref=src,
            dst_ref=dst,
            send_sem=S.ssem.at[r],
            recv_sem=S.rsem.at[GROUPS.index(group)],
            device_id=device,
            device_id_type=MESH,
        ).start()
        sent_bytes[r] = sent_bytes.get(r, 0) + size(src)
        group_bytes[group] = group_bytes.get(group, 0) + size(src)

    far, near_z = 2 * core - 1, 1 - 2 * core
    upward, downward = 1 - core, core
    base = 2 * chunks
    DIAGONAL = ((1, 1), (1, -1), (-1, 1), (-1, -1))
    FAR_DIAGONAL = ((far, 1), (far, -1), (near_z, 1), (near_z, -1))

    def send_bulk(r, k):
        src, dst = pl.ds(k * ROWS, ROWS), pl.ds(TOP + k * ROWS, ROWS)
        if r in (0, 3):
            send(S.up[r].at[:, src, :], S.rup[r].at[:, dst, :], r, k, at(1, 0))
            send(S.dn[r].at[:, src, :], S.rdn[r].at[:, dst, :], r, chunks + k, at(-1, 0))
        if r == 1:
            send(S.out1.at[1, :, dst, :], S.in1.at[1, :, dst, :], 1, chunks + k, at(near_z, 0))
            send(S.out1.at[0, :, dst, :], S.in1.at[0, :, dst, :], 1, k, at(far, 0))
        if r == 2:
            send(S.mine.at[:, src, :], S.side.at[1, :, dst, :], 2, chunks + k, at(near_z, 0))
        if r == 4:
            send(S.rest.at[:, src, :], S.far_rest.at[:, src, :], 4, k, at(far, 0))

    def send_edges(r):
        if r == 4:
            send(S.rest_hi, S.far_rest_hi, 4, base + 2, at(far, 1))
            send(S.rest_lo, S.far_rest_lo, 4, base + 3, at(far, -1))
            return
        send(S.yu[r], S.ryu[r], r, base, at(0, 1))
        send(S.yd[r], S.ryd[r], r, base + 1, at(0, -1))
        for i, (dz, dy) in enumerate(DIAGONAL if r in (0, 3) else FAR_DIAGONAL):
            if r != 2 or i >= 2:
                send(S.dg[r][i], S.rdg[r][i], r, base + 2 + i, at(dz, dy))

    def send_chunk(r, k):
        if k == chunks - 1:
            send_edges(r)
        send_bulk(r, k)

    def sent(*rounds):
        for r in rounds:
            wait_bytes(sent_bytes[r], S.ssem.at[r])

    landed = set()

    def receive_group(r, name):
        if (r, name) not in landed:
            landed.add((r, name))
            wait_bytes(group_bytes[r, name], S.rsem.at[GROUPS.index((r, name))])

    def receive(r, k, side="", reach=1):
        receive_group(r, side + "A")
        if abs(k - order[-1]) <= reach:
            receive_group(r, side + "B")
        receive_group(r, side + "E")
        return k == order[0]

    def interior(k):
        return pl.ds(TOP + k * ROWS, ROWS)

    def moved(k, dy):
        return pl.ds(TOP + k * ROWS - dy, ROWS)

    def emit_populations(r, k, values, sense):
        here = pl.ds(k * ROWS, ROWS)
        for moving, table in ((S.up, UP), (S.dn, DOWN)):
            for i, d in enumerate(table):
                q = INDEX[tuple(sense * e for e in d)]
                value = roll_x(values[q], d[0])
                moving[r][i, here, :] = value
                slot = DIAGONAL.index((d[2], d[1])) if d[1] else None
                if d[1] == 1 and k == chunks - 1:
                    S.dg[r][slot][...] = value[ROWS - 1 :, :]
                if d[1] == -1 and k == 0:
                    S.dg[r][slot][...] = value[:1, :]
        for i, d in enumerate(FLAT):
            q = INDEX[tuple(sense * e for e in d)]
            value = roll_x(values[q], d[0])
            S.flat[r][i, interior(k), :] = value
            if d[1] == 1 and k == chunks - 1:
                j = FLAT_UP.index(d)
                S.yu[r][j : j + 1, :] = value[ROWS - 1 :, :]
            if d[1] == -1 and k == 0:
                j = FLAT_DOWN.index(d)
                S.yd[r][j : j + 1, :] = value[:1, :]

    def place_edges(r):
        for i, arrived, row in ((0, S.rup, TOP - 1), (1, S.rup, last), (2, S.rdn, TOP - 1), (3, S.rdn, last)):
            slot = 3 if i % 2 == 0 else 4
            arrived[r][slot, pl.ds(row, 1), :] = S.rdg[r][i][...]
        for j in range(3):
            S.flat[r][FLAT.index(FLAT_UP[j]), pl.ds(TOP - 1, 1), :] = S.ryu[r][j : j + 1, :]
            S.flat[r][FLAT.index(FLAT_DOWN[j]), pl.ds(last, 1), :] = S.ryd[r][j : j + 1, :]

    def gather_populations(r, k, sense):
        values = [None] * 19
        for arrived, table in ((S.rup, UP), (S.rdn, DOWN), (S.flat, FLAT)):
            for i, d in enumerate(table):
                q = INDEX[tuple(sense * e for e in d)]
                values[q] = arrived[r][i, moved(k, d[1]), :]
        return values

    def coefficients(k):
        here = pl.ds(k * ROWS, ROWS)
        return [S.coef[i, here, :] for i in range(3)]

    def inlet(k):
        return jnp.where(S.lab[0, pl.ds(k * ROWS, ROWS), :] == 3, 1.0, 0.0)

    wait_bytes(sum(size(dst) for src, dst in loads), S.in_sem.at[0])
    for k in order:
        here = pl.ds(k * ROWS, ROWS)
        label = S.lab[0, here, :]
        s = jnp.where(label == 1, S.sol[0, here, :], jnp.where(label == 2, 1.0, 0.0))
        free = jnp.where(label == 3, 0.0, 1.0 - s)
        b = jnp.where(label == 4, free, OMEGA * free)
        a = jnp.where(label == 4, 0.0, (1.0 - OMEGA) * free)
        for i, value in enumerate((a, b, s)):
            S.coef[i, here, :] = value
        f = [S.f0[q, 0, here, :] for q in range(19)]
        rho, u, speed, post = collide(f, a, b, s, inlet(k))
        for i, value in enumerate((rho, *u)):
            S.mom0[i, here, :] = value
        emit_populations(0, k, post, 1)

    pl.semaphore_wait(barrier, len(greeted))
    send_edges(0)
    for k in order:
        send_bulk(0, k)
    S.s_hi[...] = S.coef[2, pl.ds(rows - 1, 1), :]
    S.s_lo[...] = S.coef[2, pl.ds(0, 1), :]
    send(S.s_hi, S.far_s_hi, 5, 1, at(far, 1))
    send(S.s_lo, S.far_s_lo, 5, 2, at(far, -1))
    send(S.coef.at[2], S.far_s, 5, 0, at(far, 0))

    for k in order:
        here = pl.ds(k * ROWS, ROWS)
        if receive(0, k):
            place_edges(0)
        a, b, s = coefficients(k)
        f = gather_populations(0, k, 1)
        for q in range(19):
            S.f1[q, here, :] = f[q]
        rho, u, speed, post = collide(f, a, b, s, inlet(k))
        for i, value in enumerate((rho, *u)):
            S.mom1[i, here, :] = value
        flow = rho * speed
        S.ds[here, :] = -flow
        energy = (1.0 - s) * flow
        S.acc[...] = energy if k == 0 else S.acc[...] + energy

        def three(cy, cz):
            mid = post[INDEX[0, cy, cz]]
            right = roll_x(post[INDEX[1, cy, cz]], 1)
            left = roll_x(post[INDEX[-1, cy, cz]], -1)
            return mid + right + left, right - left

        for slot, cz in ((upward, 1), (downward, -1)):
            total, along = three(0, cz)
            for i, value in enumerate((total, along, post[INDEX[0, 1, cz]], post[INDEX[0, -1, cz]])):
                S.out1[slot, i, interior(k), :] = value
        if k == chunks - 1:
            end = pl.ds(last - 1, 1)
            for j, (i, row) in enumerate(((0, end), (1, end), (2, pl.ds(last - 2, 1)), (2, end))):
                S.yu[1][2 + j : 3 + j, :] = S.out1[0, i, row, :]
            S.dg[1][0][...] = S.out1[0, 2, end, :]
            S.dg[1][2][...] = S.out1[1, 2, end, :]
        if k == 0:
            end = pl.ds(TOP, 1)
            for j, (i, row) in enumerate(((0, end), (1, end), (3, pl.ds(TOP + 1, 1)), (3, end))):
                S.yd[1][2 + j : 3 + j, :] = S.out1[0, i, row, :]
            S.dg[1][1][...] = S.out1[0, 3, end, :]
            S.dg[1][3][...] = S.out1[1, 3, end, :]
        for j, cy in enumerate((0, 1, -1)):
            total, along = three(cy, 0)
            S.part[2 * j, interior(k), :] = total
            S.part[2 * j + 1, interior(k), :] = along
            if cy == 1 and k == chunks - 1:
                S.yu[1][0:1, :] = total[ROWS - 1 :, :]
                S.yu[1][1:2, :] = along[ROWS - 1 :, :]
            if cy == -1 and k == 0:
                S.yd[1][0:1, :] = total[:1, :]
                S.yd[1][1:2, :] = along[:1, :]
        send_chunk(1, k)

    sent(0, 5)

    def place_halo(side, i):
        S.in1[side, 2, pl.ds(TOP - 1, 1), :] = S.rdg[1][i][...]
        S.in1[side, 3, pl.ds(last, 1), :] = S.rdg[1][i + 1][...]

    for k in order:
        here = pl.ds(k * ROWS, ROWS)
        if receive(1, k, "n"):
            place_halo(1, 2)
            for j in range(2):
                S.part[2 + j, pl.ds(TOP - 1, 1), :] = S.ryu[1][j : j + 1, :]
                S.part[4 + j, pl.ds(last, 1), :] = S.ryd[1][j : j + 1, :]
            S.out1[0, 2, pl.ds(TOP - 1, 1), :] = S.ryu[1][5:6, :]
            S.out1[0, 3, pl.ds(last, 1), :] = S.ryd[1][5:6, :]
        near_x = S.in1[1, 1, interior(k), :]
        near_a, near_b = S.in1[1, 2, moved(k, 1), :], S.in1[1, 3, moved(k, -1), :]
        mass = S.in1[1, 0, interior(k), :] + (near_a + near_b)
        mid, mid_x = S.part[0, interior(k), :], S.part[1, interior(k), :]
        ahead, ahead_x = S.part[2, moved(k, 1), :], S.part[3, moved(k, 1), :]
        behind, behind_x = S.part[4, moved(k, -1), :], S.part[5, moved(k, -1), :]
        rest = (
            mass + (mid + (ahead + behind)),
            near_x + (mid_x + (ahead_x + behind_x)),
            (near_a - near_b) + (ahead - behind),
            mass,
        )
        for i, value in enumerate(rest):
            S.rest[i, here, :] = value
            if k == chunks - 1:
                S.rest_hi[i : i + 1, :] = value[ROWS - 1 :, :]
            if k == 0:
                S.rest_lo[i : i + 1, :] = value[:1, :]
        send_chunk(4, k)

    def finish_moments(rest, total, along, ahead, behind, s):
        mass = total + (ahead + behind)
        rho = rest[0] + mass
        inv = 1.0 / rho
        u = [(rest[1] + along) * inv, (rest[2] + (ahead - behind)) * inv, (mass - rest[3]) * inv]
        speed = u[0] * u[0] + u[1] * u[1] + u[2] * u[2]
        free = 1.0 - s
        twice = 2.0 * free
        return rho, speed, [twice * v for v in u], free

    for k in order:
        here = pl.ds(k * ROWS, ROWS)
        if receive(1, k, "f"):
            place_halo(0, 0)
        rho, speed, (x, y, z), free = finish_moments(
            [S.rest[i, here, :] for i in range(4)],
            S.in1[0, 0, interior(k), :],
            S.in1[0, 1, interior(k), :],
            S.in1[0, 2, moved(k, 1), :],
            S.in1[0, 3, moved(k, -1), :],
            S.coef[2, here, :],
        )
        flow = rho * speed
        S.ds[here, :] = S.ds[here, :] - flow
        S.acc[...] = S.acc[...] + free * flow
        e = free * speed
        w = -z - e
        for i, value in enumerate((x, y, w)):
            S.mine[i, here, :] = value
        for i, value in enumerate((x, y - e, -y - e, e)):
            S.grad[i, interior(k), :] = value
        if k == chunks - 1:
            S.dg[2][2][...] = (w - y)[ROWS - 1 :, :]
            S.yu[2][0:1, :] = x[ROWS - 1 :, :]
            S.yu[2][1:2, :] = (-y - e)[ROWS - 1 :, :]
        if k == 0:
            S.dg[2][3][...] = (w + y)[:1, :]
            S.yd[2][0:1, :] = x[:1, :]
            S.yd[2][1:2, :] = (y - e)[:1, :]
        send_chunk(2, k)

    def reduce_send(stage, value):
        S.ar[stage][...] = value
        for i, device in enumerate(stages[stage]):
            pltpu.make_async_remote_copy(
                src_ref=S.ar[stage],
                dst_ref=S.arr[stage][i],
                send_sem=S.ssem.at[6 + stage],
                recv_sem=S.rsem.at[GROUPS.index((6 + stage, "A"))],
                device_id=device,
                device_id_type=MESH,
            ).start()
        sent_bytes[6 + stage] = len(stages[stage])

    def reduce_receive(stage):
        wait_bytes(len(stages[stage]), S.rsem.at[GROUPS.index((6 + stage, "A"))])
        value = S.ar[stage][...]
        for i in range(len(stages[stage])):
            value = value + S.arr[stage][i][...]
        return value

    acc = S.acc[...]
    acc = functools.reduce(lambda p, q: p + q, [acc[:, i : i + 128] for i in range(0, cols, 128)])
    reduce_send(0, jnp.sum(acc, axis=0, keepdims=True))

    zero_row = jnp.zeros((1, cols), jnp.float32)
    sent(1)

    def far_plane(rest, total, along, ahead, behind, s):
        rho, speed, (x, y, z), free = finish_moments(rest, total, along, ahead, behind, s)
        return x, y, z - free * speed

    for k in order:
        here = pl.ds(k * ROWS, ROWS)
        receive_group(5, "A")
        if receive(4, k, "", 0):
            low, high = pl.ds(TOP - 1, 1), pl.ds(last, 1)
            x, y, w = far_plane(
                [S.far_rest_hi[i : i + 1, :] for i in range(4)],
                S.ryu[1][2:3, :],
                S.ryu[1][3:4, :],
                S.ryu[1][4:5, :],
                S.out1[0, 3, pl.ds(TOP, 1), :],
                S.far_s_hi[...],
            )
            S.side[0, 1, low, :] = y
            S.side[0, 2, low, :] = w
            x, y, w = far_plane(
                [S.far_rest_lo[i : i + 1, :] for i in range(4)],
                S.ryd[1][2:3, :],
                S.ryd[1][3:4, :],
                S.out1[0, 2, pl.ds(last - 1, 1), :],
                S.ryd[1][4:5, :],
                S.far_s_lo[...],
            )
            S.side[0, 1, high, :] = y
            S.side[0, 2, high, :] = w
        value = far_plane(
            [S.far_rest[i, here, :] for i in range(4)],
            S.out1[0, 0, interior(k), :],
            S.out1[0, 1, interior(k), :],
            S.out1[0, 2, moved(k, 1), :],
            S.out1[0, 3, moved(k, -1), :],
            S.far_s[here, :],
        )
        for i in range(3):
            S.side[0, i, interior(k), :] = value[i]

    for k in order:
        here = pl.ds(k * ROWS, ROWS)
        if receive(2, k):
            for i, row in ((2, TOP - 1), (3, last)):
                S.side[1, 2, pl.ds(row, 1), :] = S.rdg[2][i][...]
                S.side[1, 1, pl.ds(row, 1), :] = zero_row
            for j, slot in ((0, 0), (1, 2)):
                S.grad[slot, pl.ds(TOP - 1, 1), :] = S.ryu[2][j : j + 1, :]
            for j, slot in ((0, 0), (1, 1)):
                S.grad[slot, pl.ds(last, 1), :] = S.ryd[2][j : j + 1, :]
        a, b, s = coefficients(k)
        mu = [None] * 19
        for slot, cz in ((upward, 1), (downward, -1)):
            x, w = S.side[slot, 0, interior(k), :], S.side[slot, 2, interior(k), :]
            mu[INDEX[0, 0, cz]] = w
            mu[INDEX[1, 0, cz]] = roll_x(w + x, -1)
            mu[INDEX[-1, 0, cz]] = roll_x(w - x, 1)
            mu[INDEX[0, 1, cz]] = S.side[slot, 2, moved(k, -1), :] + S.side[slot, 1, moved(k, -1), :]
            mu[INDEX[0, -1, cz]] = S.side[slot, 2, moved(k, 1), :] - S.side[slot, 1, moved(k, 1), :]
        for cy, slot in ((0, 3), (1, 1), (-1, 2)):
            x, w = S.grad[0, moved(k, -cy), :], S.grad[slot, moved(k, -cy), :]
            w = -w if cy == 0 else w
            mu[INDEX[0, cy, 0]] = w
            mu[INDEX[1, cy, 0]] = roll_x(w + x, -1)
            mu[INDEX[-1, cy, 0]] = roll_x(w - x, 1)
        f = [S.f1[q, here, :] for q in range(19)]
        rho, u = S.mom1[0, here, :], [S.mom1[i, here, :] for i in (1, 2, 3)]
        speed = u[0] * u[0] + u[1] * u[1] + u[2] * u[2]
        lam, by_s = collide_adjoint(mu, f, rho, u, speed, a, b, s)
        S.ds[here, :] = S.ds[here, :] + by_s
        twice = 2.0 * (1.0 - s)
        twice_u = [twice * u[i] for i in range(3)]
        e = (1.0 - s) * speed
        lam[0] = lam[0] - e
        for q, o in PAIRS:
            along = dot_c(VEL[q], twice_u)
            lam[q] = lam[q] + (along - e)
            lam[o] = lam[o] - (along + e)
        emit_populations(3, k, lam, -1)
        send_chunk(3, k)

    reduce_send(1, reduce_receive(0))
    sent(4, 2, 3, 6, 7)

    for k in order:
        here = pl.ds(k * ROWS, ROWS)
        if receive(3, k):
            place_edges(3)
        a, b, s = coefficients(k)
        mu = gather_populations(3, k, -1)
        f = [S.f0[q, 0, here, :] for q in range(19)]
        rho, u = S.mom0[0, here, :], [S.mom0[i, here, :] for i in (1, 2, 3)]
        speed = u[0] * u[0] + u[1] * u[1] + u[2] * u[2]
        lam, by_s = collide_adjoint(mu, f, rho, u, speed, a, b, s)
        for q in range(19):
            lam_ref[q, 0, here, :] = lam[q]
        sens_ref[0, here, :] = jnp.where(S.lab[0, here, :] == 1, S.ds[here, :] + by_s, 0.0)
    total = jnp.sum(reduce_receive(1), axis=1, keepdims=True)
    en_ref[...] = jnp.broadcast_to(total, en_ref.shape)


def finish(scale, lam_ref, sens_ref, en_ref, out_sens, out_lam, lam, sens, some, sems):
    inv = 1.0 / (en_ref[...] * scale)
    rows = sens.shape[1]
    for q in range(19):
        for k in range(rows // ROWS):
            here = pl.ds(k * ROWS, ROWS)
            lam[q, 0, here, :] = lam_ref[q, 0, here, :] * inv
        pltpu.make_async_copy(lam.at[pl.ds(q, 1)], out_lam.at[pl.ds(q, 1)], sems.at[0]).start()
    for k in range(rows // ROWS):
        here = pl.ds(k * ROWS, ROWS)
        sens[0, here, :] = sens_ref[0, here, :] * inv
    pltpu.make_async_copy(sens, out_sens, sems.at[0]).start()
    pltpu.make_async_copy(some, some, sems.at[0]).wait()


def on_device(sizes, populations, solid_fraction, labels):
    rows, cols = solid_fraction.shape[1:]
    n_gz, n_gy, n_x, n_z, n_core = sizes
    leaves, tree = jax.tree.flatten(scratch_tree(rows, cols, (n_core * n_z - 1, n_x * n_gy - 1)))
    f32 = jnp.float32
    in_hbm = pl.BlockSpec(memory_space=pltpu.HBM)
    in_vmem = pl.BlockSpec(memory_space=pltpu.VMEM)
    lam_type = jax.ShapeDtypeStruct(populations.shape, f32)
    sens_type = jax.ShapeDtypeStruct(solid_fraction.shape, f32)
    limit = 24 * 1024 * 1024
    lam, sens, total = pl.pallas_call(
        functools.partial(kernel, tree, sizes),
        out_shape=(lam_type, sens_type, jax.ShapeDtypeStruct((ROWS, cols), f32)),
        in_specs=[in_hbm] * 3,
        out_specs=(in_vmem,) * 3,
        scratch_shapes=leaves,
        compiler_params=pltpu.CompilerParams(collective_id=0, has_side_effects=True, vmem_limit_bytes=limit),
        name="lattice",
    )(*[pltpu.with_memory_space_constraint(v, pltpu.HBM) for v in (populations, solid_fraction, labels)])
    scale = 1.0 / (STEPS * n_gz * n_gy * rows * cols)
    return pl.pallas_call(
        functools.partial(finish, scale),
        out_shape=(sens_type, lam_type),
        in_specs=[in_vmem] * 3,
        out_specs=(in_hbm,) * 2,
        scratch_shapes=[
            pltpu.VMEM(populations.shape, f32),
            pltpu.VMEM(solid_fraction.shape, f32),
            pltpu.VMEM((20 * rows * cols // LANES, 1, LANES), f32),
            pltpu.SemaphoreType.DMA((1,)),
        ],
        compiler_params=pltpu.CompilerParams(vmem_limit_bytes=4 * 1024 * 1024),
        name="finish",
    )(lam, sens, total)


def solution(mesh):
    n_gz, n_gy = mesh.shape["gz"], mesh.shape["gy"]
    n_core = 2
    n_z = 8 if n_gz % 16 == 0 else n_gz // 2
    n_x = n_gz // (n_core * n_z)
    in_specs = (P(None, "gz", "gy", None), P("gz", "gy", None), P("gz", "gy", None))
    out_specs = (P("gz", "gy", None), P(None, "gz", "gy", None))
    return jax.shard_map(
        functools.partial(on_device, (n_gz, n_gy, n_x, n_z, n_core)),
        mesh=mesh,
        in_specs=in_specs,
        out_specs=out_specs,
        check_vma=False,
    )
```

```python
import functools
import types

import jax
import jax.numpy as jnp
from jax import lax
from jax.experimental import pallas as pl
from jax.experimental.pallas import tpu as pltpu
from jax.sharding import PartitionSpec as P

STEPS = 2
OMEGA = 0.9
INLET_SPEED = 0.05
ROWS = 8
TOP = 8
MESH = pl.DeviceIdType.MESH
LANES = 128
EDGE_ROWS = ((0, 4), (1, 8), (2, 2), (3, 4))
GROUPS = [(r, g) for r in (0, 2, 3, 4) for g in ("A", "B", "E")]
GROUPS += [(1, side + g) for side in ("f", "n") for g in ("A", "B", "E")] + [(5, "A"), (6, "A"), (7, "A")]


def velocity_table():
    velocities = [(0, 0, 0)]
    for axis in range(3):
        for sign in (1, -1):
            vector = [0, 0, 0]
            vector[axis] = sign
            velocities.append(tuple(vector))
    for first in range(3):
        for second in range(first + 1, 3):
            for sign_a in (1, -1):
                for sign_b in (1, -1):
                    vector = [0, 0, 0]
                    vector[first] = sign_a
                    vector[second] = sign_b
                    velocities.append(tuple(vector))
    weights = [1.0 / 3.0] + [1.0 / 18.0] * 6 + [1.0 / 36.0] * 12
    opposite = [velocities.index(tuple((-e for e in vector))) for vector in velocities]
    return (velocities, weights, opposite)


VEL, WEIGHT, OPP = velocity_table()
INDEX = {v: q for q, v in enumerate(VEL)}
PAIRS = [(q, OPP[q]) for q in range(19) if q < OPP[q]]
UP = [(0, 0, 1), (1, 0, 1), (-1, 0, 1), (0, 1, 1), (0, -1, 1)]
DOWN = [(0, 0, -1), (1, 0, -1), (-1, 0, -1), (0, 1, -1), (0, -1, -1)]
FLAT = [v for v in VEL if v[2] == 0]
FLAT_UP = [(0, 1, 0), (1, 1, 0), (-1, 1, 0)]
FLAT_DOWN = [(0, -1, 0), (1, -1, 0), (-1, -1, 0)]


def inlet_value(q):
    along = VEL[q][2] * INLET_SPEED
    return WEIGHT[q] * (1.0 + 3.0 * along + 4.5 * along * along - 1.5 * INLET_SPEED * INLET_SPEED)


def roll_x(value, shift):
    if shift == 0:
        return value
    return pltpu.roll(value, shift % value.shape[1], 1)


def signed(terms):
    total = None
    for sign, value in terms:
        if sign == 0:
            continue
        if total is None:
            total = value if sign > 0 else -value
        else:
            total = total + value if sign > 0 else total - value
    return total


def dot_c(c, vector):
    return signed([(c[i], vector[i]) for i in range(3)])


def pair_moments(plus, minus, rest):
    total = rest + functools.reduce(lambda p, q: p + q, list(plus.values()))
    return total, [signed([(VEL[q][i], minus[q]) for q, o in PAIRS]) for i in range(3)]


def collide(f, a, b, s, k):
    plus = {q: f[q] + f[o] for q, o in PAIRS}
    minus = {q: f[q] - f[o] for q, o in PAIRS}
    rho, m = pair_moments(plus, minus, f[0])
    inv = 1.0 / rho
    u = [m[i] * inv for i in range(3)]
    speed = u[0] * u[0] + u[1] * u[1] + u[2] * u[2]
    brho = b * rho
    base = brho * (1.0 - 1.5 * speed)
    both, half_sum, half_diff = a + s, 0.5 * (a + s), 0.5 * (a - s)
    bases = {w: w * base for w in set(WEIGHT)}
    level = {w: bases[w] + k * inlet_value(q) for w, q in ((WEIGHT[0], 0), (WEIGHT[1], 1), (WEIGHT[7], 7))}
    post = [None] * 19
    post[0] = both * f[0] + level[WEIGHT[0]]
    for q, o in PAIRS:
        w = WEIGHT[q]
        along = dot_c(VEL[q], u)
        flow = brho * along
        even = half_sum * plus[q] + (4.5 * w) * (flow * along)
        odd = half_diff * minus[q] + (3.0 * w) * flow
        if VEL[q][2] == 0:
            even = even + level[w]
        else:
            even = even + (bases[w] + k * (0.5 * (inlet_value(q) + inlet_value(o))))
            odd = odd + k * (0.5 * (inlet_value(q) - inlet_value(o)))
        post[q] = even + odd
        post[o] = even - odd
    return rho, u, speed, post


def collide_adjoint(mu, f, rho, u, speed, a, b, s, extra=None):
    plus = {q: mu[q] + mu[o] for q, o in PAIRS}
    minus = {q: mu[q] - mu[o] for q, o in PAIRS}

    def weighted(table, first, second=None):
        axial, diagonal = [], []
        for q, o in PAIRS:
            c = VEL[q]
            sign = c[first] if second is None else c[first] * c[second]
            (axial if WEIGHT[q] == WEIGHT[1] else diagonal).append((sign, table[q]))
        one, two = signed(axial), signed(diagonal)
        two = two * WEIGHT[7]
        return two if one is None else one * WEIGHT[1] + two

    axial = functools.reduce(lambda p, q: p + q, [plus[q] for q, o in PAIRS if WEIGHT[q] == WEIGHT[1]])
    diagonal = functools.reduce(lambda p, q: p + q, [plus[q] for q, o in PAIRS if WEIGHT[q] != WEIGHT[1]])
    big_a = WEIGHT[0] * mu[0] + WEIGHT[1] * axial + WEIGHT[7] * diagonal
    big_b = [3.0 * weighted(minus, i) for i in range(3)]
    big_c = {}
    for i in range(3):
        for j in range(i, 3):
            big_c[i, j] = big_c[j, i] = 4.5 * weighted(plus, i, j)
    cu = [big_c[i, 0] * u[0] + big_c[i, 1] * u[1] + big_c[i, 2] * u[2] for i in range(3)]
    quad = cu[0] * u[0] + cu[1] * u[1] + cu[2] * u[2] - 1.5 * speed * big_a
    by_rho = b * (big_a - quad)
    triple = 3.0 * big_a
    by_m = [b * (big_b[i] + 2.0 * cu[i] - triple * u[i]) for i in range(3)]
    if extra is not None:
        by_rho = by_rho + extra[0]
        by_m = [by_m[i] + extra[1][i] for i in range(3)]
    both, half_sum, half_diff = a + s, 0.5 * (a + s), 0.5 * (a - s)
    lam = [None] * 19
    lam[0] = both * mu[0] + by_rho
    sums, differences = [], []
    for q, o in PAIRS:
        even = half_sum * plus[q] + by_rho
        odd = half_diff * minus[q] + dot_c(VEL[q], by_m)
        lam[q] = even + odd
        lam[o] = even - odd
        sums.append(plus[q] * (f[q] + f[o]))
        differences.append(minus[q] * (f[q] - f[o]))
    all_sums = functools.reduce(lambda p, q: p + q, sums)
    all_differences = functools.reduce(lambda p, q: p + q, differences)
    middle = mu[0] * f[0]
    total = rho * (big_a + big_b[0] * u[0] + big_b[1] * u[1] + big_b[2] * u[2] + quad)
    by_s = OMEGA * (middle + 0.5 * all_sums - total) - (1.0 - 0.5 * OMEGA) * all_differences
    return lam, by_s


def scratch_tree(rows, cols, n_ar):
    def vmem(*shape):
        return pltpu.VMEM(shape, jnp.float32)

    padded = rows + 16
    dma = pltpu.SemaphoreType.DMA
    return dict(
        f0=vmem(19, 1, rows, cols),
        sol=vmem(1, rows, cols),
        lab=pltpu.VMEM((1, rows, cols), jnp.int32),
        coef=vmem(3, rows, cols),
        mom0=vmem(4, rows, cols),
        mom1=vmem(4, rows, cols),
        f1=vmem(19, rows, cols),
        ds=vmem(rows, cols),
        acc=vmem(ROWS, cols),
        in_sem=dma((1,)),
        ssem=dma((8,)),
        rsem=dma((len(GROUPS),)),
        some=vmem(3 * 19 * rows * cols // LANES, 1, LANES),
        part=vmem(6, padded, cols),
        grad=vmem(4, padded, cols),
        out1=vmem(2, 4, padded, cols),
        in1=vmem(2, 4, padded, cols),
        side=vmem(2, 3, padded, cols),
        mine=vmem(3, rows, cols),
        rest=vmem(4, rows, cols),
        far_rest=vmem(4, rows, cols),
        far_s=vmem(rows, cols),
        s_hi=vmem(1, cols),
        s_lo=vmem(1, cols),
        far_s_hi=vmem(1, cols),
        far_s_lo=vmem(1, cols),
        rest_hi=vmem(4, cols),
        rest_lo=vmem(4, cols),
        far_rest_hi=vmem(4, cols),
        far_rest_lo=vmem(4, cols),
        yu={r: vmem(n, cols) for r, n in EDGE_ROWS},
        yd={r: vmem(n, cols) for r, n in EDGE_ROWS},
        ryu={r: vmem(n, cols) for r, n in EDGE_ROWS},
        ryd={r: vmem(n, cols) for r, n in EDGE_ROWS},
        out={r: vmem(2, 5, rows, cols) for r in (0, 3)},
        arrived={r: vmem(2, 5, padded, cols) for r in (0, 3)},
        flat={r: vmem(9, padded, cols) for r in (0, 3)},
        dg=[[vmem(1, cols) for i in range(4)] for r in range(4)],
        rdg=[[vmem(1, cols) for i in range(4)] for r in range(4)],
        ar=[vmem(1, LANES) for count in n_ar],
        arr=[[vmem(1, LANES) for i in range(count)] for count in n_ar],
    )


def kernel(tree, sizes, pop_ref, sol_ref, lab_ref, lam_ref, sens_ref, en_ref, *refs):
    S = types.SimpleNamespace(**jax.tree.unflatten(tree, refs))
    n_gz, n_gy, n_x, n_z, n_core = sizes
    rows, cols = S.ds.shape
    chunks = rows // ROWS
    order = [chunks - 1, 0, *range(chunks - 2, 0, -1)]
    last = TOP + rows
    gz = lax.axis_index("gz")
    gy = lax.axis_index("gy")

    def size(ref):
        return functools.reduce(lambda p, q: p * q, ref.shape) // LANES

    def wait_bytes(count, sem):
        some = S.some.at[pl.ds(0, count)]
        pltpu.make_async_copy(some, some, sem).wait()

    loads = ((pop_ref, S.f0), (sol_ref, S.sol), (lab_ref, S.lab))
    for src, dst in loads:
        pltpu.make_async_copy(src, dst, S.in_sem.at[0]).start()

    def at(dz, dy):
        return (lax.rem(gz + dz + n_gz, n_gz), lax.rem(gy + dy + n_gy, n_gy))

    core = lax.rem(gz, n_core)
    zpos = lax.rem(gz // n_core, n_z)
    xpos = gz // (n_core * n_z)

    def place(dx, dz, dcore, dy):
        x = lax.rem(xpos + dx, n_x)
        z = lax.rem(zpos + dz, n_z)
        c = lax.rem(core + dcore, n_core)
        return ((x * n_z + z) * n_core + c, lax.rem(gy + dy, n_gy))

    stages = [
        [place(0, dz, dc, 0) for dz in range(n_z) for dc in range(n_core) if (dz, dc) != (0, 0)],
        [place(dx, 0, 0, dy) for dx in range(n_x) for dy in range(n_gy) if (dx, dy) != (0, 0)],
    ]
    near = [at(dz, dy) for dz, dy in ((1, 0), (-1, 0), (0, 1), (0, -1), (1, 1), (1, -1), (-1, 1), (-1, -1))]
    barrier = pltpu.get_barrier_semaphore()
    greeted = near + stages[0] + [place(dx, 0, 0, 0) for dx in range(1, n_x)]
    for device in greeted:
        pl.semaphore_signal(barrier, inc=1, device_id=device, device_id_type=MESH)

    sent_bytes, group_bytes = {}, {}

    def group_of(r, i):
        if i >= base:
            name = "E"
        else:
            name = "B" if i % chunks == order[-1] and r != 5 else "A"
        if r == 1:
            near_side = i - base not in (2, 3) if i >= base else i >= chunks
            name = ("n" if near_side else "f") + name
        return (r, name)

    def send(src, dst, r, i, device):
        group = group_of(r, i)
        pltpu.make_async_remote_copy(
            src_ref=src,
            dst_ref=dst,
            send_sem=S.ssem.at[r],
            recv_sem=S.rsem.at[GROUPS.index(group)],
            device_id=device,
            device_id_type=MESH,
        ).start()
        sent_bytes[r] = sent_bytes.get(r, 0) + size(src)
        group_bytes[group] = group_bytes.get(group, 0) + size(src)

    far, near_z = 2 * core - 1, 1 - 2 * core
    upward, downward = 1 - core, core
    base = 2 * chunks
    DIAGONAL = ((1, 1), (1, -1), (-1, 1), (-1, -1))
    FAR_DIAGONAL = ((far, 1), (far, -1), (near_z, 1), (near_z, -1))

    def send_bulk(r, k):
        src, dst = pl.ds(k * ROWS, ROWS), pl.ds(TOP + k * ROWS, ROWS)
        if r in (0, 3):
            send(S.out[r].at[0, :, src, :], S.arrived[r].at[0, :, dst, :], r, k, at(far, 0))
            send(S.out[r].at[1, :, src, :], S.arrived[r].at[1, :, dst, :], r, chunks + k, at(near_z, 0))
        if r == 1:
            send(S.out1.at[0, :, dst, :], S.in1.at[0, :, dst, :], 1, k, at(far, 0))
            send(S.out1.at[1, :, dst, :], S.in1.at[1, :, dst, :], 1, chunks + k, at(near_z, 0))
        if r == 2:
            send(S.mine.at[:, src, :], S.side.at[1, :, dst, :], 2, chunks + k, at(near_z, 0))
        if r == 4:
            send(S.rest.at[:, src, :], S.far_rest.at[:, src, :], 4, k, at(far, 0))

    def send_edges(r, end):
        high = end == 1
        if r == 4:
            src, dst = (S.rest_hi, S.far_rest_hi) if high else (S.rest_lo, S.far_rest_lo)
            send(src, dst, 4, base + (2 if high else 3), at(far, end))
            return
        src, dst = (S.yu, S.ryu) if high else (S.yd, S.ryd)
        send(src[r], dst[r], r, base + (0 if high else 1), at(0, end))
        for i, (dz, dy) in enumerate(DIAGONAL if r in (0, 3) else FAR_DIAGONAL):
            if dy == end and (r != 2 or i >= 2):
                send(S.dg[r][i], S.rdg[r][i], r, base + 2 + i, at(dz, dy))

    def send_chunk(r, k):
        if k == chunks - 1:
            send_edges(r, 1)
        if k == 0:
            send_edges(r, -1)
        send_bulk(r, k)

    def sent(*rounds):
        for r in rounds:
            wait_bytes(sent_bytes[r], S.ssem.at[r])

    landed = set()

    def receive_group(r, name):
        if (r, name) not in landed:
            landed.add((r, name))
            wait_bytes(group_bytes[r, name], S.rsem.at[GROUPS.index((r, name))])

    def receive(r, k, side="", reach=1):
        receive_group(r, side + "A")
        if abs(k - order[-1]) <= reach:
            receive_group(r, side + "B")
        receive_group(r, side + "E")
        return k == order[0]

    def interior(k):
        return pl.ds(TOP + k * ROWS, ROWS)

    def moved(k, dy):
        return pl.ds(TOP + k * ROWS - dy, ROWS)

    def emit_populations(r, k, values, sense):
        here = pl.ds(k * ROWS, ROWS)
        for side, table in ((upward, UP), (downward, DOWN)):
            for i, d in enumerate(table):
                q = INDEX[tuple(sense * e for e in d)]
                value = roll_x(values[q], d[0])
                S.out[r][side, i, here, :] = value
                slot = DIAGONAL.index((d[2], d[1])) if d[1] else None
                if d[1] == 1 and k == chunks - 1:
                    S.dg[r][slot][...] = value[ROWS - 1 :, :]
                if d[1] == -1 and k == 0:
                    S.dg[r][slot][...] = value[:1, :]
        for i, d in enumerate(FLAT):
            q = INDEX[tuple(sense * e for e in d)]
            value = roll_x(values[q], d[0])
            S.flat[r][i, interior(k), :] = value
            if d[1] == 1 and k == chunks - 1:
                j = FLAT_UP.index(d)
                S.yu[r][j : j + 1, :] = value[ROWS - 1 :, :]
            if d[1] == -1 and k == 0:
                j = FLAT_DOWN.index(d)
                S.yd[r][j : j + 1, :] = value[:1, :]

    def place_edges(r):
        for i, side, row in ((0, downward, TOP - 1), (1, downward, last), (2, upward, TOP - 1), (3, upward, last)):
            slot = 3 if i % 2 == 0 else 4
            S.arrived[r][side, slot, pl.ds(row, 1), :] = S.rdg[r][i][...]
        for j in range(3):
            S.flat[r][FLAT.index(FLAT_UP[j]), pl.ds(TOP - 1, 1), :] = S.ryu[r][j : j + 1, :]
            S.flat[r][FLAT.index(FLAT_DOWN[j]), pl.ds(last, 1), :] = S.ryd[r][j : j + 1, :]

    def gather_populations(r, k, sense):
        values = [None] * 19
        for i, d in enumerate(FLAT):
            values[INDEX[tuple(sense * e for e in d)]] = S.flat[r][i, moved(k, d[1]), :]
        for side, table in ((downward, UP), (upward, DOWN)):
            for i, d in enumerate(table):
                values[INDEX[tuple(sense * e for e in d)]] = S.arrived[r][side, i, moved(k, d[1]), :]
        return values

    def coefficients(k):
        here = pl.ds(k * ROWS, ROWS)
        return [S.coef[i, here, :] for i in range(3)]

    def inlet(k):
        return jnp.where(S.lab[0, pl.ds(k * ROWS, ROWS), :] == 3, 1.0, 0.0)

    wait_bytes(sum(size(dst) for src, dst in loads), S.in_sem.at[0])
    for k in order:
        here = pl.ds(k * ROWS, ROWS)
        label = S.lab[0, here, :]
        s = jnp.where(label == 1, S.sol[0, here, :], jnp.where(label == 2, 1.0, 0.0))
        free = jnp.where(label == 3, 0.0, 1.0 - s)
        b = jnp.where(label == 4, free, OMEGA * free)
        a = jnp.where(label == 4, 0.0, (1.0 - OMEGA) * free)
        for i, value in enumerate((a, b, s)):
            S.coef[i, here, :] = value
        f = [S.f0[q, 0, here, :] for q in range(19)]
        rho, u, speed, post = collide(f, a, b, s, inlet(k))
        for i, value in enumerate((rho, *u)):
            S.mom0[i, here, :] = value
        emit_populations(0, k, post, 1)

    pl.semaphore_wait(barrier, len(greeted))
    send_edges(0, 1)
    send_edges(0, -1)
    for k in order:
        send_bulk(0, k)
    S.s_hi[...] = S.coef[2, pl.ds(rows - 1, 1), :]
    S.s_lo[...] = S.coef[2, pl.ds(0, 1), :]
    send(S.s_hi, S.far_s_hi, 5, 1, at(far, 1))
    send(S.s_lo, S.far_s_lo, 5, 2, at(far, -1))
    send(S.coef.at[2], S.far_s, 5, 0, at(far, 0))

    for k in order:
        here = pl.ds(k * ROWS, ROWS)
        if receive(0, k):
            place_edges(0)
        a, b, s = coefficients(k)
        f = gather_populations(0, k, 1)
        for q in range(19):
            S.f1[q, here, :] = f[q]
        rho, u, speed, post = collide(f, a, b, s, inlet(k))
        for i, value in enumerate((rho, *u)):
            S.mom1[i, here, :] = value
        flow = rho * speed
        S.ds[here, :] = -flow
        energy = (1.0 - s) * flow
        S.acc[...] = energy if k == order[0] else S.acc[...] + energy

        def three(cy, cz):
            mid = post[INDEX[0, cy, cz]]
            right = roll_x(post[INDEX[1, cy, cz]], 1)
            left = roll_x(post[INDEX[-1, cy, cz]], -1)
            return mid + right + left, right - left

        for slot, cz in ((upward, 1), (downward, -1)):
            total, along = three(0, cz)
            for i, value in enumerate((total, along, post[INDEX[0, 1, cz]], post[INDEX[0, -1, cz]])):
                S.out1[slot, i, interior(k), :] = value
        if k == chunks - 1:
            end = pl.ds(last - 1, 1)
            for j, (i, row) in enumerate(((0, end), (1, end), (2, pl.ds(last - 2, 1)), (2, end))):
                S.yu[1][2 + j : 3 + j, :] = S.out1[0, i, row, :]
            S.dg[1][0][...] = S.out1[0, 2, end, :]
            S.dg[1][2][...] = S.out1[1, 2, end, :]
        if k == 0:
            end = pl.ds(TOP, 1)
            for j, (i, row) in enumerate(((0, end), (1, end), (3, pl.ds(TOP + 1, 1)), (3, end))):
                S.yd[1][2 + j : 3 + j, :] = S.out1[0, i, row, :]
            S.dg[1][1][...] = S.out1[0, 3, end, :]
            S.dg[1][3][...] = S.out1[1, 3, end, :]
        for j, cy in enumerate((0, 1, -1)):
            total, along = three(cy, 0)
            S.part[2 * j, interior(k), :] = total
            S.part[2 * j + 1, interior(k), :] = along
            if cy == 1 and k == chunks - 1:
                S.yu[1][0:1, :] = total[ROWS - 1 :, :]
                S.yu[1][1:2, :] = along[ROWS - 1 :, :]
            if cy == -1 and k == 0:
                S.yd[1][0:1, :] = total[:1, :]
                S.yd[1][1:2, :] = along[:1, :]
        send_chunk(1, k)

    sent(0, 5)

    def place_halo(side, i):
        S.in1[side, 2, pl.ds(TOP - 1, 1), :] = S.rdg[1][i][...]
        S.in1[side, 3, pl.ds(last, 1), :] = S.rdg[1][i + 1][...]

    for k in order:
        here = pl.ds(k * ROWS, ROWS)
        if receive(1, k, "n"):
            place_halo(1, 2)
            for j in range(2):
                S.part[2 + j, pl.ds(TOP - 1, 1), :] = S.ryu[1][j : j + 1, :]
                S.part[4 + j, pl.ds(last, 1), :] = S.ryd[1][j : j + 1, :]
            S.out1[0, 2, pl.ds(TOP - 1, 1), :] = S.ryu[1][5:6, :]
            S.out1[0, 3, pl.ds(last, 1), :] = S.ryd[1][5:6, :]
        near_x = S.in1[1, 1, interior(k), :]
        near_a, near_b = S.in1[1, 2, moved(k, 1), :], S.in1[1, 3, moved(k, -1), :]
        mass = S.in1[1, 0, interior(k), :] + (near_a + near_b)
        mid, mid_x = S.part[0, interior(k), :], S.part[1, interior(k), :]
        ahead, ahead_x = S.part[2, moved(k, 1), :], S.part[3, moved(k, 1), :]
        behind, behind_x = S.part[4, moved(k, -1), :], S.part[5, moved(k, -1), :]
        rest = (
            mass + (mid + (ahead + behind)),
            near_x + (mid_x + (ahead_x + behind_x)),
            (near_a - near_b) + (ahead - behind),
            mass,
        )
        for i, value in enumerate(rest):
            S.rest[i, here, :] = value
            if k == chunks - 1:
                S.rest_hi[i : i + 1, :] = value[ROWS - 1 :, :]
            if k == 0:
                S.rest_lo[i : i + 1, :] = value[:1, :]
        send_chunk(4, k)

    def finish_moments(rest, total, along, ahead, behind, s):
        mass = total + (ahead + behind)
        rho = rest[0] + mass
        inv = 1.0 / rho
        u = [(rest[1] + along) * inv, (rest[2] + (ahead - behind)) * inv, (mass - rest[3]) * inv]
        speed = u[0] * u[0] + u[1] * u[1] + u[2] * u[2]
        free = 1.0 - s
        twice = 2.0 * free
        return rho, speed, [twice * v for v in u], free

    for k in order:
        here = pl.ds(k * ROWS, ROWS)
        if receive(1, k, "f"):
            place_halo(0, 0)
        rho, speed, (x, y, z), free = finish_moments(
            [S.rest[i, here, :] for i in range(4)],
            S.in1[0, 0, interior(k), :],
            S.in1[0, 1, interior(k), :],
            S.in1[0, 2, moved(k, 1), :],
            S.in1[0, 3, moved(k, -1), :],
            S.coef[2, here, :],
        )
        flow = rho * speed
        S.ds[here, :] = S.ds[here, :] - flow
        S.acc[...] = S.acc[...] + free * flow
        e = free * speed
        w = -z - e
        for i, value in enumerate((x, y, w)):
            S.mine[i, here, :] = value
        for i, value in enumerate((x, y - e, -y - e, e)):
            S.grad[i, interior(k), :] = value
        if k == chunks - 1:
            S.dg[2][2][...] = (w - y)[ROWS - 1 :, :]
            S.yu[2][0:1, :] = x[ROWS - 1 :, :]
            S.yu[2][1:2, :] = (-y - e)[ROWS - 1 :, :]
        if k == 0:
            S.dg[2][3][...] = (w + y)[:1, :]
            S.yd[2][0:1, :] = x[:1, :]
            S.yd[2][1:2, :] = (y - e)[:1, :]
        send_chunk(2, k)

    def reduce_send(stage, value):
        S.ar[stage][...] = value
        for i, device in enumerate(stages[stage]):
            pltpu.make_async_remote_copy(
                src_ref=S.ar[stage],
                dst_ref=S.arr[stage][i],
                send_sem=S.ssem.at[6 + stage],
                recv_sem=S.rsem.at[GROUPS.index((6 + stage, "A"))],
                device_id=device,
                device_id_type=MESH,
            ).start()
        sent_bytes[6 + stage] = len(stages[stage])

    def reduce_receive(stage):
        wait_bytes(len(stages[stage]), S.rsem.at[GROUPS.index((6 + stage, "A"))])
        value = S.ar[stage][...]
        for i in range(len(stages[stage])):
            value = value + S.arr[stage][i][...]
        return value

    acc = S.acc[...]
    acc = functools.reduce(lambda p, q: p + q, [acc[:, i : i + 128] for i in range(0, cols, 128)])
    reduce_send(0, jnp.sum(acc, axis=0, keepdims=True))

    zero_row = jnp.zeros((1, cols), jnp.float32)
    sent(1)

    def far_plane(rest, total, along, ahead, behind, s):
        rho, speed, (x, y, z), free = finish_moments(rest, total, along, ahead, behind, s)
        return x, y, z - free * speed

    for k in order:
        here = pl.ds(k * ROWS, ROWS)
        receive_group(5, "A")
        if receive(4, k, "", 0):
            low, high = pl.ds(TOP - 1, 1), pl.ds(last, 1)
            x, y, w = far_plane(
                [S.far_rest_hi[i : i + 1, :] for i in range(4)],
                S.ryu[1][2:3, :],
                S.ryu[1][3:4, :],
                S.ryu[1][4:5, :],
                S.out1[0, 3, pl.ds(TOP, 1), :],
                S.far_s_hi[...],
            )
            S.side[0, 1, low, :] = y
            S.side[0, 2, low, :] = w
            x, y, w = far_plane(
                [S.far_rest_lo[i : i + 1, :] for i in range(4)],
                S.ryd[1][2:3, :],
                S.ryd[1][3:4, :],
                S.out1[0, 2, pl.ds(last - 1, 1), :],
                S.ryd[1][4:5, :],
                S.far_s_lo[...],
            )
            S.side[0, 1, high, :] = y
            S.side[0, 2, high, :] = w
        value = far_plane(
            [S.far_rest[i, here, :] for i in range(4)],
            S.out1[0, 0, interior(k), :],
            S.out1[0, 1, interior(k), :],
            S.out1[0, 2, moved(k, 1), :],
            S.out1[0, 3, moved(k, -1), :],
            S.far_s[here, :],
        )
        for i in range(3):
            S.side[0, i, interior(k), :] = value[i]

    for k in order:
        here = pl.ds(k * ROWS, ROWS)
        if receive(2, k):
            for i, row in ((2, TOP - 1), (3, last)):
                S.side[1, 2, pl.ds(row, 1), :] = S.rdg[2][i][...]
                S.side[1, 1, pl.ds(row, 1), :] = zero_row
            for j, slot in ((0, 0), (1, 2)):
                S.grad[slot, pl.ds(TOP - 1, 1), :] = S.ryu[2][j : j + 1, :]
            for j, slot in ((0, 0), (1, 1)):
                S.grad[slot, pl.ds(last, 1), :] = S.ryd[2][j : j + 1, :]
        a, b, s = coefficients(k)
        mu = [None] * 19
        for slot, cz in ((upward, 1), (downward, -1)):
            x, w = S.side[slot, 0, interior(k), :], S.side[slot, 2, interior(k), :]
            mu[INDEX[0, 0, cz]] = w
            mu[INDEX[1, 0, cz]] = roll_x(w + x, -1)
            mu[INDEX[-1, 0, cz]] = roll_x(w - x, 1)
            mu[INDEX[0, 1, cz]] = S.side[slot, 2, moved(k, -1), :] + S.side[slot, 1, moved(k, -1), :]
            mu[INDEX[0, -1, cz]] = S.side[slot, 2, moved(k, 1), :] - S.side[slot, 1, moved(k, 1), :]
        for cy, slot in ((0, 3), (1, 1), (-1, 2)):
            x, w = S.grad[0, moved(k, -cy), :], S.grad[slot, moved(k, -cy), :]
            w = -w if cy == 0 else w
            mu[INDEX[0, cy, 0]] = w
            mu[INDEX[1, cy, 0]] = roll_x(w + x, -1)
            mu[INDEX[-1, cy, 0]] = roll_x(w - x, 1)
        f = [S.f1[q, here, :] for q in range(19)]
        rho, u = S.mom1[0, here, :], [S.mom1[i, here, :] for i in (1, 2, 3)]
        speed = u[0] * u[0] + u[1] * u[1] + u[2] * u[2]
        free = 1.0 - s
        twice = 2.0 * free
        extra = (-(free * speed), [twice * u[i] for i in range(3)])
        lam, by_s = collide_adjoint(mu, f, rho, u, speed, a, b, s, extra)
        S.ds[here, :] = S.ds[here, :] + by_s
        emit_populations(3, k, lam, -1)
        send_chunk(3, k)

    reduce_send(1, reduce_receive(0))
    sent(4, 2, 3, 6, 7)

    for k in order:
        here = pl.ds(k * ROWS, ROWS)
        if receive(3, k):
            place_edges(3)
        a, b, s = coefficients(k)
        mu = gather_populations(3, k, -1)
        f = [S.f0[q, 0, here, :] for q in range(19)]
        rho, u = S.mom0[0, here, :], [S.mom0[i, here, :] for i in (1, 2, 3)]
        speed = u[0] * u[0] + u[1] * u[1] + u[2] * u[2]
        lam, by_s = collide_adjoint(mu, f, rho, u, speed, a, b, s)
        for q in range(19):
            lam_ref[q, 0, here, :] = lam[q]
        sens_ref[0, here, :] = jnp.where(S.lab[0, here, :] == 1, S.ds[here, :] + by_s, 0.0)
    total = jnp.sum(reduce_receive(1), axis=1, keepdims=True)
    en_ref[...] = jnp.broadcast_to(total, en_ref.shape)


def finish(scale, lam_ref, sens_ref, en_ref, out_sens, out_lam, lam, sens, some, sems):
    inv = 1.0 / (en_ref[...] * scale)
    rows = sens.shape[1]
    for q in range(19):
        for k in range(rows // ROWS):
            here = pl.ds(k * ROWS, ROWS)
            lam[q, 0, here, :] = lam_ref[q, 0, here, :] * inv
        pltpu.make_async_copy(lam.at[pl.ds(q, 1)], out_lam.at[pl.ds(q, 1)], sems.at[0]).start()
    for k in range(rows // ROWS):
        here = pl.ds(k * ROWS, ROWS)
        sens[0, here, :] = sens_ref[0, here, :] * inv
    pltpu.make_async_copy(sens, out_sens, sems.at[0]).start()
    pltpu.make_async_copy(some, some, sems.at[0]).wait()


def on_device(sizes, populations, solid_fraction, labels):
    rows, cols = solid_fraction.shape[1:]
    n_gz, n_gy, n_x, n_z, n_core = sizes
    leaves, tree = jax.tree.flatten(scratch_tree(rows, cols, (n_core * n_z - 1, n_x * n_gy - 1)))
    f32 = jnp.float32
    in_hbm = pl.BlockSpec(memory_space=pltpu.HBM)
    in_vmem = pl.BlockSpec(memory_space=pltpu.VMEM)
    lam_type = jax.ShapeDtypeStruct(populations.shape, f32)
    sens_type = jax.ShapeDtypeStruct(solid_fraction.shape, f32)
    limit = 24 * 1024 * 1024
    lam, sens, total = pl.pallas_call(
        functools.partial(kernel, tree, sizes),
        out_shape=(lam_type, sens_type, jax.ShapeDtypeStruct((ROWS, cols), f32)),
        in_specs=[in_hbm] * 3,
        out_specs=(in_vmem,) * 3,
        scratch_shapes=leaves,
        compiler_params=pltpu.CompilerParams(collective_id=0, has_side_effects=True, vmem_limit_bytes=limit),
        name="lattice",
    )(*[pltpu.with_memory_space_constraint(v, pltpu.HBM) for v in (populations, solid_fraction, labels)])
    scale = 1.0 / (STEPS * n_gz * n_gy * rows * cols)
    return pl.pallas_call(
        functools.partial(finish, scale),
        out_shape=(sens_type, lam_type),
        in_specs=[in_vmem] * 3,
        out_specs=(in_hbm,) * 2,
        scratch_shapes=[
            pltpu.VMEM(populations.shape, f32),
            pltpu.VMEM(solid_fraction.shape, f32),
            pltpu.VMEM((20 * rows * cols // LANES, 1, LANES), f32),
            pltpu.SemaphoreType.DMA((1,)),
        ],
        compiler_params=pltpu.CompilerParams(vmem_limit_bytes=4 * 1024 * 1024),
        name="finish",
    )(lam, sens, total)


def solution(mesh):
    n_gz, n_gy = mesh.shape["gz"], mesh.shape["gy"]
    n_core = 2
    n_z = 8 if n_gz % 16 == 0 else n_gz // 2
    n_x = n_gz // (n_core * n_z)
    in_specs = (P(None, "gz", "gy", None), P("gz", "gy", None), P("gz", "gy", None))
    out_specs = (P("gz", "gy", None), P(None, "gz", "gy", None))
    return jax.shard_map(
        functools.partial(on_device, (n_gz, n_gy, n_x, n_z, n_core)),
        mesh=mesh,
        in_specs=in_specs,
        out_specs=out_specs,
        check_vma=False,
    )
```

```python
import functools
import types

import jax
import jax.numpy as jnp
from jax import lax
from jax.experimental import pallas as pl
from jax.experimental.pallas import tpu as pltpu
from jax.sharding import PartitionSpec as P

STEPS = 2
OMEGA = 0.9
INLET_SPEED = 0.05
ROWS = 8
TOP = 8
MESH = pl.DeviceIdType.MESH
LANES = 128
EDGE_ROWS = ((0, 4), (1, 8), (2, 2), (3, 4))
GROUPS = [(r, g) for r in (0, 2, 3, 4) for g in ("A", "B", "E")]
GROUPS += [(1, side + g) for side in ("f", "n") for g in ("A", "B", "E")] + [(5, "A"), (6, "A"), (7, "A")]


def velocity_table():
    velocities = [(0, 0, 0)]
    for axis in range(3):
        for sign in (1, -1):
            vector = [0, 0, 0]
            vector[axis] = sign
            velocities.append(tuple(vector))
    for first in range(3):
        for second in range(first + 1, 3):
            for sign_a in (1, -1):
                for sign_b in (1, -1):
                    vector = [0, 0, 0]
                    vector[first] = sign_a
                    vector[second] = sign_b
                    velocities.append(tuple(vector))
    weights = [1.0 / 3.0] + [1.0 / 18.0] * 6 + [1.0 / 36.0] * 12
    opposite = [velocities.index(tuple((-e for e in vector))) for vector in velocities]
    return (velocities, weights, opposite)


VEL, WEIGHT, OPP = velocity_table()
INDEX = {v: q for q, v in enumerate(VEL)}
PAIRS = [(q, OPP[q]) for q in range(19) if q < OPP[q]]
UP = [(0, 0, 1), (1, 0, 1), (-1, 0, 1), (0, 1, 1), (0, -1, 1)]
DOWN = [(0, 0, -1), (1, 0, -1), (-1, 0, -1), (0, 1, -1), (0, -1, -1)]
FLAT = [v for v in VEL if v[2] == 0]
FLAT_UP = [(0, 1, 0), (1, 1, 0), (-1, 1, 0)]
FLAT_DOWN = [(0, -1, 0), (1, -1, 0), (-1, -1, 0)]


def inlet_value(q):
    along = VEL[q][2] * INLET_SPEED
    return WEIGHT[q] * (1.0 + 3.0 * along + 4.5 * along * along - 1.5 * INLET_SPEED * INLET_SPEED)


def roll_x(value, shift):
    if shift == 0:
        return value
    return pltpu.roll(value, shift % value.shape[1], 1)


def signed(terms):
    total = None
    for sign, value in terms:
        if sign == 0:
            continue
        if total is None:
            total = value if sign > 0 else -value
        else:
            total = total + value if sign > 0 else total - value
    return total


def dot_c(c, vector):
    return signed([(c[i], vector[i]) for i in range(3)])


def pair_moments(plus, minus, rest):
    total = rest + functools.reduce(lambda p, q: p + q, list(plus.values()))
    return total, [signed([(VEL[q][i], minus[q]) for q, o in PAIRS]) for i in range(3)]


def collide(f, a, b, s, k):
    plus = {q: f[q] + f[o] for q, o in PAIRS}
    minus = {q: f[q] - f[o] for q, o in PAIRS}
    rho, m = pair_moments(plus, minus, f[0])
    inv = 1.0 / rho
    u = [m[i] * inv for i in range(3)]
    speed = u[0] * u[0] + u[1] * u[1] + u[2] * u[2]
    brho = b * rho
    base = brho * (1.0 - 1.5 * speed)
    both, half_sum, half_diff = a + s, 0.5 * (a + s), 0.5 * (a - s)
    bases = {w: w * base for w in set(WEIGHT)}
    level = {w: bases[w] + k * inlet_value(q) for w, q in ((WEIGHT[0], 0), (WEIGHT[1], 1), (WEIGHT[7], 7))}
    post = [None] * 19
    post[0] = both * f[0] + level[WEIGHT[0]]
    for q, o in PAIRS:
        w = WEIGHT[q]
        along = dot_c(VEL[q], u)
        flow = brho * along
        even = half_sum * plus[q] + (4.5 * w) * (flow * along)
        odd = half_diff * minus[q] + (3.0 * w) * flow
        if VEL[q][2] == 0:
            even = even + level[w]
        else:
            even = even + (bases[w] + k * (0.5 * (inlet_value(q) + inlet_value(o))))
            odd = odd + k * (0.5 * (inlet_value(q) - inlet_value(o)))
        post[q] = even + odd
        post[o] = even - odd
    return rho, u, speed, post


def collide_adjoint(mu, f, rho, u, speed, a, b, s, extra=None):
    plus = {q: mu[q] + mu[o] for q, o in PAIRS}
    minus = {q: mu[q] - mu[o] for q, o in PAIRS}

    def weighted(table, first, second=None):
        axial, diagonal = [], []
        for q, o in PAIRS:
            c = VEL[q]
            sign = c[first] if second is None else c[first] * c[second]
            (axial if WEIGHT[q] == WEIGHT[1] else diagonal).append((sign, table[q]))
        one, two = signed(axial), signed(diagonal)
        two = two * WEIGHT[7]
        return two if one is None else one * WEIGHT[1] + two

    axial = functools.reduce(lambda p, q: p + q, [plus[q] for q, o in PAIRS if WEIGHT[q] == WEIGHT[1]])
    diagonal = functools.reduce(lambda p, q: p + q, [plus[q] for q, o in PAIRS if WEIGHT[q] != WEIGHT[1]])
    big_a = WEIGHT[0] * mu[0] + WEIGHT[1] * axial + WEIGHT[7] * diagonal
    big_b = [3.0 * weighted(minus, i) for i in range(3)]
    big_c = {}
    for i in range(3):
        for j in range(i, 3):
            big_c[i, j] = big_c[j, i] = 4.5 * weighted(plus, i, j)
    cu = [big_c[i, 0] * u[0] + big_c[i, 1] * u[1] + big_c[i, 2] * u[2] for i in range(3)]
    quad = cu[0] * u[0] + cu[1] * u[1] + cu[2] * u[2] - 1.5 * speed * big_a
    by_rho = b * (big_a - quad)
    triple = 3.0 * big_a
    by_m = [b * (big_b[i] + 2.0 * cu[i] - triple * u[i]) for i in range(3)]
    if extra is not None:
        by_rho = by_rho + extra[0]
        by_m = [by_m[i] + extra[1][i] for i in range(3)]
    both, half_sum, half_diff = a + s, 0.5 * (a + s), 0.5 * (a - s)
    lam = [None] * 19
    lam[0] = both * mu[0] + by_rho
    sums, differences = [], []
    for q, o in PAIRS:
        even = half_sum * plus[q] + by_rho
        odd = half_diff * minus[q] + dot_c(VEL[q], by_m)
        lam[q] = even + odd
        lam[o] = even - odd
        sums.append(plus[q] * (f[q] + f[o]))
        differences.append(minus[q] * (f[q] - f[o]))
    all_sums = functools.reduce(lambda p, q: p + q, sums)
    all_differences = functools.reduce(lambda p, q: p + q, differences)
    middle = mu[0] * f[0]
    total = rho * (big_a + big_b[0] * u[0] + big_b[1] * u[1] + big_b[2] * u[2] + quad)
    by_s = OMEGA * (middle + 0.5 * all_sums - total) - (1.0 - 0.5 * OMEGA) * all_differences
    return lam, by_s


def scratch_tree(rows, cols, n_ar):
    def vmem(*shape):
        return pltpu.VMEM(shape, jnp.float32)

    padded = rows + 16
    dma = pltpu.SemaphoreType.DMA
    return dict(
        f0=vmem(19, 1, rows, cols),
        sol=vmem(1, rows, cols),
        lab=pltpu.VMEM((1, rows, cols), jnp.int32),
        coef=vmem(3, rows, cols),
        mom0=vmem(4, rows, cols),
        mom1=vmem(4, rows, cols),
        f1=vmem(19, rows, cols),
        ds=vmem(rows, cols),
        acc=vmem(ROWS, cols),
        in_sem=dma((1,)),
        ssem=dma((8,)),
        rsem=dma((len(GROUPS),)),
        some=vmem(3 * 19 * rows * cols // LANES, 1, LANES),
        part=vmem(6, padded, cols),
        grad=vmem(4, padded, cols),
        out1=vmem(2, 4, padded, cols),
        in1=vmem(2, 4, padded, cols),
        side=vmem(2, 3, padded, cols),
        mine=vmem(3, rows, cols),
        rest=vmem(4, rows, cols),
        far_rest=vmem(4, rows, cols),
        far_s=vmem(rows, cols),
        s_hi=vmem(1, cols),
        s_lo=vmem(1, cols),
        far_s_hi=vmem(1, cols),
        far_s_lo=vmem(1, cols),
        rest_hi=vmem(4, cols),
        rest_lo=vmem(4, cols),
        far_rest_hi=vmem(4, cols),
        far_rest_lo=vmem(4, cols),
        yu={r: vmem(n, cols) for r, n in EDGE_ROWS},
        yd={r: vmem(n, cols) for r, n in EDGE_ROWS},
        ryu={r: vmem(n, cols) for r, n in EDGE_ROWS},
        ryd={r: vmem(n, cols) for r, n in EDGE_ROWS},
        out={r: vmem(2, 5, rows, cols) for r in (0, 3)},
        arrived={r: vmem(2, 5, padded, cols) for r in (0, 3)},
        flat={r: vmem(9, padded, cols) for r in (0, 3)},
        dg=[[vmem(1, cols) for i in range(4)] for r in range(4)],
        rdg=[[vmem(1, cols) for i in range(4)] for r in range(4)],
        ar=[vmem(1, LANES) for count in n_ar],
        arr=[[vmem(1, LANES) for i in range(count)] for count in n_ar],
    )


def kernel(tree, sizes, pop_ref, sol_ref, lab_ref, lam_ref, sens_ref, en_ref, *refs):
    S = types.SimpleNamespace(**jax.tree.unflatten(tree, refs))
    n_gz, n_gy, n_x, n_z, n_core = sizes
    rows, cols = S.ds.shape
    chunks = rows // ROWS
    order = [chunks - 1, 0, *range(chunks - 2, 0, -1)]
    late_order = [*range(1, chunks - 1), chunks - 1, 0]
    last = TOP + rows
    gz = lax.axis_index("gz")
    gy = lax.axis_index("gy")

    def size(ref):
        return functools.reduce(lambda p, q: p * q, ref.shape) // LANES

    def wait_bytes(count, sem):
        some = S.some.at[pl.ds(0, count)]
        pltpu.make_async_copy(some, some, sem).wait()

    loads = ((pop_ref, S.f0), (sol_ref, S.sol), (lab_ref, S.lab))
    for src, dst in loads:
        pltpu.make_async_copy(src, dst, S.in_sem.at[0]).start()

    def at(dz, dy):
        return (lax.rem(gz + dz + n_gz, n_gz), lax.rem(gy + dy + n_gy, n_gy))

    core = lax.rem(gz, n_core)
    zpos = lax.rem(gz // n_core, n_z)
    xpos = gz // (n_core * n_z)

    def place(dx, dz, dcore, dy):
        x = lax.rem(xpos + dx, n_x)
        z = lax.rem(zpos + dz, n_z)
        c = lax.rem(core + dcore, n_core)
        return ((x * n_z + z) * n_core + c, lax.rem(gy + dy, n_gy))

    stages = [
        [place(0, dz, dc, 0) for dz in range(n_z) for dc in range(n_core) if (dz, dc) != (0, 0)],
        [place(dx, 0, 0, dy) for dx in range(n_x) for dy in range(n_gy) if (dx, dy) != (0, 0)],
    ]
    near = [at(dz, dy) for dz, dy in ((1, 0), (-1, 0), (0, 1), (0, -1), (1, 1), (1, -1), (-1, 1), (-1, -1))]
    barrier = pltpu.get_barrier_semaphore()
    greeted = near + stages[0] + [place(dx, 0, 0, 0) for dx in range(1, n_x)]
    for device in greeted:
        pl.semaphore_signal(barrier, inc=1, device_id=device, device_id_type=MESH)

    sent_bytes, group_bytes = {}, {}

    def group_of(r, i):
        if i >= base:
            name = "E"
        else:
            name = "B" if i % chunks == order[-1] and r != 5 else "A"
        if r == 4 and i < base:
            name = "B" if i in (0, chunks - 1) else "A"
        if r == 1:
            near_side = i - base not in (2, 3) if i >= base else i >= chunks
            name = ("n" if near_side else "f") + name
        return (r, name)

    def send(src, dst, r, i, device):
        group = group_of(r, i)
        pltpu.make_async_remote_copy(
            src_ref=src,
            dst_ref=dst,
            send_sem=S.ssem.at[r],
            recv_sem=S.rsem.at[GROUPS.index(group)],
            device_id=device,
            device_id_type=MESH,
        ).start()
        sent_bytes[r] = sent_bytes.get(r, 0) + size(src)
        group_bytes[group] = group_bytes.get(group, 0) + size(src)

    far, near_z = 2 * core - 1, 1 - 2 * core
    upward, downward = 1 - core, core
    base = 2 * chunks
    DIAGONAL = ((1, 1), (1, -1), (-1, 1), (-1, -1))
    FAR_DIAGONAL = ((far, 1), (far, -1), (near_z, 1), (near_z, -1))

    def send_bulk(r, k):
        src, dst = pl.ds(k * ROWS, ROWS), pl.ds(TOP + k * ROWS, ROWS)
        if r in (0, 3):
            send(S.out[r].at[0, :, src, :], S.arrived[r].at[0, :, dst, :], r, k, at(far, 0))
            send(S.out[r].at[1, :, src, :], S.arrived[r].at[1, :, dst, :], r, chunks + k, at(near_z, 0))
        if r == 1:
            send(S.out1.at[0, :, dst, :], S.in1.at[0, :, dst, :], 1, k, at(far, 0))
            send(S.out1.at[1, :, dst, :], S.in1.at[1, :, dst, :], 1, chunks + k, at(near_z, 0))
        if r == 2:
            send(S.mine.at[:, src, :], S.side.at[1, :, dst, :], 2, chunks + k, at(near_z, 0))
        if r == 4:
            send(S.rest.at[:, src, :], S.far_rest.at[:, src, :], 4, k, at(far, 0))

    def send_edges(r, end):
        high = end == 1
        if r == 4:
            src, dst = (S.rest_hi, S.far_rest_hi) if high else (S.rest_lo, S.far_rest_lo)
            send(src, dst, 4, base + (2 if high else 3), at(far, end))
            return
        src, dst = (S.yu, S.ryu) if high else (S.yd, S.ryd)
        send(src[r], dst[r], r, base + (0 if high else 1), at(0, end))
        for i, (dz, dy) in enumerate(DIAGONAL if r in (0, 3) else FAR_DIAGONAL):
            if dy == end and (r != 2 or i >= 2):
                send(S.dg[r][i], S.rdg[r][i], r, base + 2 + i, at(dz, dy))

    def send_chunk(r, k):
        if k == chunks - 1:
            send_edges(r, 1)
        if k == 0:
            send_edges(r, -1)
        send_bulk(r, k)

    def sent(*rounds):
        for r in rounds:
            wait_bytes(sent_bytes[r], S.ssem.at[r])

    landed = set()

    def receive_group(r, name):
        if (r, name) not in landed:
            landed.add((r, name))
            wait_bytes(group_bytes[r, name], S.rsem.at[GROUPS.index((r, name))])

    def receive(r, k, side=""):
        receive_group(r, side + "A")
        if abs(k - order[-1]) <= 1:
            receive_group(r, side + "B")
        receive_group(r, side + "E")
        return k == order[0]

    def receive_late(r, k, side=""):
        receive_group(r, side + "A")
        receive_group(r, side + "B")
        first = k == late_order[-2]
        if first:
            receive_group(r, side + "E")
        return first

    def interior(k):
        return pl.ds(TOP + k * ROWS, ROWS)

    def moved(k, dy):
        return pl.ds(TOP + k * ROWS - dy, ROWS)

    def emit_populations(r, k, values, sense):
        here = pl.ds(k * ROWS, ROWS)
        for side, table in ((upward, UP), (downward, DOWN)):
            for i, d in enumerate(table):
                q = INDEX[tuple(sense * e for e in d)]
                value = roll_x(values[q], d[0])
                S.out[r][side, i, here, :] = value
                slot = DIAGONAL.index((d[2], d[1])) if d[1] else None
                if d[1] == 1 and k == chunks - 1:
                    S.dg[r][slot][...] = value[ROWS - 1 :, :]
                if d[1] == -1 and k == 0:
                    S.dg[r][slot][...] = value[:1, :]
        for i, d in enumerate(FLAT):
            q = INDEX[tuple(sense * e for e in d)]
            value = roll_x(values[q], d[0])
            S.flat[r][i, interior(k), :] = value
            if d[1] == 1 and k == chunks - 1:
                j = FLAT_UP.index(d)
                S.yu[r][j : j + 1, :] = value[ROWS - 1 :, :]
            if d[1] == -1 and k == 0:
                j = FLAT_DOWN.index(d)
                S.yd[r][j : j + 1, :] = value[:1, :]

    def place_edges(r):
        for i, side, row in ((0, downward, TOP - 1), (1, downward, last), (2, upward, TOP - 1), (3, upward, last)):
            slot = 3 if i % 2 == 0 else 4
            S.arrived[r][side, slot, pl.ds(row, 1), :] = S.rdg[r][i][...]
        for j in range(3):
            S.flat[r][FLAT.index(FLAT_UP[j]), pl.ds(TOP - 1, 1), :] = S.ryu[r][j : j + 1, :]
            S.flat[r][FLAT.index(FLAT_DOWN[j]), pl.ds(last, 1), :] = S.ryd[r][j : j + 1, :]

    def gather_populations(r, k, sense):
        values = [None] * 19
        for i, d in enumerate(FLAT):
            values[INDEX[tuple(sense * e for e in d)]] = S.flat[r][i, moved(k, d[1]), :]
        for side, table in ((downward, UP), (upward, DOWN)):
            for i, d in enumerate(table):
                values[INDEX[tuple(sense * e for e in d)]] = S.arrived[r][side, i, moved(k, d[1]), :]
        return values

    def coefficients(k):
        here = pl.ds(k * ROWS, ROWS)
        return [S.coef[i, here, :] for i in range(3)]

    def inlet(k):
        return jnp.where(S.lab[0, pl.ds(k * ROWS, ROWS), :] == 3, 1.0, 0.0)

    wait_bytes(sum(size(dst) for src, dst in loads), S.in_sem.at[0])
    for k in order:
        here = pl.ds(k * ROWS, ROWS)
        label = S.lab[0, here, :]
        s = jnp.where(label == 1, S.sol[0, here, :], jnp.where(label == 2, 1.0, 0.0))
        free = jnp.where(label == 3, 0.0, 1.0 - s)
        b = jnp.where(label == 4, free, OMEGA * free)
        a = jnp.where(label == 4, 0.0, (1.0 - OMEGA) * free)
        for i, value in enumerate((a, b, s)):
            S.coef[i, here, :] = value
        f = [S.f0[q, 0, here, :] for q in range(19)]
        rho, u, speed, post = collide(f, a, b, s, inlet(k))
        for i, value in enumerate((rho, *u)):
            S.mom0[i, here, :] = value
        emit_populations(0, k, post, 1)

    pl.semaphore_wait(barrier, len(greeted))
    send_edges(0, 1)
    send_edges(0, -1)
    for k in order:
        send_bulk(0, k)
    S.s_hi[...] = S.coef[2, pl.ds(rows - 1, 1), :]
    S.s_lo[...] = S.coef[2, pl.ds(0, 1), :]
    send(S.s_hi, S.far_s_hi, 5, 1, at(far, 1))
    send(S.s_lo, S.far_s_lo, 5, 2, at(far, -1))
    send(S.coef.at[2], S.far_s, 5, 0, at(far, 0))

    for k in order:
        here = pl.ds(k * ROWS, ROWS)
        if receive(0, k):
            place_edges(0)
        a, b, s = coefficients(k)
        f = gather_populations(0, k, 1)
        for q in range(19):
            S.f1[q, here, :] = f[q]
        rho, u, speed, post = collide(f, a, b, s, inlet(k))
        for i, value in enumerate((rho, *u)):
            S.mom1[i, here, :] = value
        flow = rho * speed
        S.ds[here, :] = -flow
        energy = (1.0 - s) * flow
        S.acc[...] = energy if k == order[0] else S.acc[...] + energy

        def three(cy, cz):
            mid = post[INDEX[0, cy, cz]]
            right = roll_x(post[INDEX[1, cy, cz]], 1)
            left = roll_x(post[INDEX[-1, cy, cz]], -1)
            return mid + right + left, right - left

        for slot, cz in ((upward, 1), (downward, -1)):
            total, along = three(0, cz)
            for i, value in enumerate((total, along, post[INDEX[0, 1, cz]], post[INDEX[0, -1, cz]])):
                S.out1[slot, i, interior(k), :] = value
        if k == chunks - 1:
            end = pl.ds(last - 1, 1)
            for j, (i, row) in enumerate(((0, end), (1, end), (2, pl.ds(last - 2, 1)), (2, end))):
                S.yu[1][2 + j : 3 + j, :] = S.out1[0, i, row, :]
            S.dg[1][0][...] = S.out1[0, 2, end, :]
            S.dg[1][2][...] = S.out1[1, 2, end, :]
        if k == 0:
            end = pl.ds(TOP, 1)
            for j, (i, row) in enumerate(((0, end), (1, end), (3, pl.ds(TOP + 1, 1)), (3, end))):
                S.yd[1][2 + j : 3 + j, :] = S.out1[0, i, row, :]
            S.dg[1][1][...] = S.out1[0, 3, end, :]
            S.dg[1][3][...] = S.out1[1, 3, end, :]
        for j, cy in enumerate((0, 1, -1)):
            total, along = three(cy, 0)
            S.part[2 * j, interior(k), :] = total
            S.part[2 * j + 1, interior(k), :] = along
            if cy == 1 and k == chunks - 1:
                S.yu[1][0:1, :] = total[ROWS - 1 :, :]
                S.yu[1][1:2, :] = along[ROWS - 1 :, :]
            if cy == -1 and k == 0:
                S.yd[1][0:1, :] = total[:1, :]
                S.yd[1][1:2, :] = along[:1, :]
        send_chunk(1, k)

    sent(0, 5)

    def place_halo(side, i):
        S.in1[side, 2, pl.ds(TOP - 1, 1), :] = S.rdg[1][i][...]
        S.in1[side, 3, pl.ds(last, 1), :] = S.rdg[1][i + 1][...]

    for k in late_order:
        here = pl.ds(k * ROWS, ROWS)
        if receive_late(1, k, "n"):
            place_halo(1, 2)
            for j in range(2):
                S.part[2 + j, pl.ds(TOP - 1, 1), :] = S.ryu[1][j : j + 1, :]
                S.part[4 + j, pl.ds(last, 1), :] = S.ryd[1][j : j + 1, :]
            S.out1[0, 2, pl.ds(TOP - 1, 1), :] = S.ryu[1][5:6, :]
            S.out1[0, 3, pl.ds(last, 1), :] = S.ryd[1][5:6, :]
        near_x = S.in1[1, 1, interior(k), :]
        near_a, near_b = S.in1[1, 2, moved(k, 1), :], S.in1[1, 3, moved(k, -1), :]
        mass = S.in1[1, 0, interior(k), :] + (near_a + near_b)
        mid, mid_x = S.part[0, interior(k), :], S.part[1, interior(k), :]
        ahead, ahead_x = S.part[2, moved(k, 1), :], S.part[3, moved(k, 1), :]
        behind, behind_x = S.part[4, moved(k, -1), :], S.part[5, moved(k, -1), :]
        rest = (
            mass + (mid + (ahead + behind)),
            near_x + (mid_x + (ahead_x + behind_x)),
            (near_a - near_b) + (ahead - behind),
            mass,
        )
        for i, value in enumerate(rest):
            S.rest[i, here, :] = value
            if k == chunks - 1:
                S.rest_hi[i : i + 1, :] = value[ROWS - 1 :, :]
            if k == 0:
                S.rest_lo[i : i + 1, :] = value[:1, :]
        send_chunk(4, k)

    def finish_moments(rest, total, along, ahead, behind, s):
        mass = total + (ahead + behind)
        rho = rest[0] + mass
        inv = 1.0 / rho
        u = [(rest[1] + along) * inv, (rest[2] + (ahead - behind)) * inv, (mass - rest[3]) * inv]
        speed = u[0] * u[0] + u[1] * u[1] + u[2] * u[2]
        free = 1.0 - s
        twice = 2.0 * free
        return rho, speed, [twice * v for v in u], free

    for k in order:
        here = pl.ds(k * ROWS, ROWS)
        if receive(1, k, "f"):
            place_halo(0, 0)
        rho, speed, (x, y, z), free = finish_moments(
            [S.rest[i, here, :] for i in range(4)],
            S.in1[0, 0, interior(k), :],
            S.in1[0, 1, interior(k), :],
            S.in1[0, 2, moved(k, 1), :],
            S.in1[0, 3, moved(k, -1), :],
            S.coef[2, here, :],
        )
        flow = rho * speed
        S.ds[here, :] = S.ds[here, :] - flow
        S.acc[...] = S.acc[...] + free * flow
        e = free * speed
        w = -z - e
        for i, value in enumerate((x, y, w)):
            S.mine[i, here, :] = value
        for i, value in enumerate((x, y - e, -y - e, e)):
            S.grad[i, interior(k), :] = value
        if k == chunks - 1:
            S.dg[2][2][...] = (w - y)[ROWS - 1 :, :]
            S.yu[2][0:1, :] = x[ROWS - 1 :, :]
            S.yu[2][1:2, :] = (-y - e)[ROWS - 1 :, :]
        if k == 0:
            S.dg[2][3][...] = (w + y)[:1, :]
            S.yd[2][0:1, :] = x[:1, :]
            S.yd[2][1:2, :] = (y - e)[:1, :]
        send_chunk(2, k)

    def reduce_send(stage, value):
        S.ar[stage][...] = value
        for i, device in enumerate(stages[stage]):
            pltpu.make_async_remote_copy(
                src_ref=S.ar[stage],
                dst_ref=S.arr[stage][i],
                send_sem=S.ssem.at[6 + stage],
                recv_sem=S.rsem.at[GROUPS.index((6 + stage, "A"))],
                device_id=device,
                device_id_type=MESH,
            ).start()
        sent_bytes[6 + stage] = len(stages[stage])

    def reduce_receive(stage):
        wait_bytes(len(stages[stage]), S.rsem.at[GROUPS.index((6 + stage, "A"))])
        value = S.ar[stage][...]
        for i in range(len(stages[stage])):
            value = value + S.arr[stage][i][...]
        return value

    acc = S.acc[...]
    acc = functools.reduce(lambda p, q: p + q, [acc[:, i : i + 128] for i in range(0, cols, 128)])
    reduce_send(0, jnp.sum(acc, axis=0, keepdims=True))

    zero_row = jnp.zeros((1, cols), jnp.float32)
    sent(1)

    def far_plane(rest, total, along, ahead, behind, s):
        rho, speed, (x, y, z), free = finish_moments(rest, total, along, ahead, behind, s)
        return x, y, z - free * speed

    for k in late_order:
        here = pl.ds(k * ROWS, ROWS)
        receive_group(5, "A")
        receive_group(4, "A")
        if k == late_order[-2]:
            receive_group(4, "B")
            receive_group(4, "E")
            low, high = pl.ds(TOP - 1, 1), pl.ds(last, 1)
            x, y, w = far_plane(
                [S.far_rest_hi[i : i + 1, :] for i in range(4)],
                S.ryu[1][2:3, :],
                S.ryu[1][3:4, :],
                S.ryu[1][4:5, :],
                S.out1[0, 3, pl.ds(TOP, 1), :],
                S.far_s_hi[...],
            )
            S.side[0, 1, low, :] = y
            S.side[0, 2, low, :] = w
            x, y, w = far_plane(
                [S.far_rest_lo[i : i + 1, :] for i in range(4)],
                S.ryd[1][2:3, :],
                S.ryd[1][3:4, :],
                S.out1[0, 2, pl.ds(last - 1, 1), :],
                S.ryd[1][4:5, :],
                S.far_s_lo[...],
            )
            S.side[0, 1, high, :] = y
            S.side[0, 2, high, :] = w
        value = far_plane(
            [S.far_rest[i, here, :] for i in range(4)],
            S.out1[0, 0, interior(k), :],
            S.out1[0, 1, interior(k), :],
            S.out1[0, 2, moved(k, 1), :],
            S.out1[0, 3, moved(k, -1), :],
            S.far_s[here, :],
        )
        for i in range(3):
            S.side[0, i, interior(k), :] = value[i]

    for k in order:
        here = pl.ds(k * ROWS, ROWS)
        if receive(2, k):
            for i, row in ((2, TOP - 1), (3, last)):
                S.side[1, 2, pl.ds(row, 1), :] = S.rdg[2][i][...]
                S.side[1, 1, pl.ds(row, 1), :] = zero_row
            for j, slot in ((0, 0), (1, 2)):
                S.grad[slot, pl.ds(TOP - 1, 1), :] = S.ryu[2][j : j + 1, :]
            for j, slot in ((0, 0), (1, 1)):
                S.grad[slot, pl.ds(last, 1), :] = S.ryd[2][j : j + 1, :]
        a, b, s = coefficients(k)
        mu = [None] * 19
        for slot, cz in ((upward, 1), (downward, -1)):
            x, w = S.side[slot, 0, interior(k), :], S.side[slot, 2, interior(k), :]
            mu[INDEX[0, 0, cz]] = w
            mu[INDEX[1, 0, cz]] = roll_x(w + x, -1)
            mu[INDEX[-1, 0, cz]] = roll_x(w - x, 1)
            mu[INDEX[0, 1, cz]] = S.side[slot, 2, moved(k, -1), :] + S.side[slot, 1, moved(k, -1), :]
            mu[INDEX[0, -1, cz]] = S.side[slot, 2, moved(k, 1), :] - S.side[slot, 1, moved(k, 1), :]
        for cy, slot in ((0, 3), (1, 1), (-1, 2)):
            x, w = S.grad[0, moved(k, -cy), :], S.grad[slot, moved(k, -cy), :]
            w = -w if cy == 0 else w
            mu[INDEX[0, cy, 0]] = w
            mu[INDEX[1, cy, 0]] = roll_x(w + x, -1)
            mu[INDEX[-1, cy, 0]] = roll_x(w - x, 1)
        f = [S.f1[q, here, :] for q in range(19)]
        rho, u = S.mom1[0, here, :], [S.mom1[i, here, :] for i in (1, 2, 3)]
        speed = u[0] * u[0] + u[1] * u[1] + u[2] * u[2]
        free = 1.0 - s
        twice = 2.0 * free
        extra = (-(free * speed), [twice * u[i] for i in range(3)])
        lam, by_s = collide_adjoint(mu, f, rho, u, speed, a, b, s, extra)
        S.ds[here, :] = S.ds[here, :] + by_s
        emit_populations(3, k, lam, -1)
        send_chunk(3, k)

    reduce_send(1, reduce_receive(0))
    sent(4, 2, 3, 6, 7)

    for k in late_order:
        here = pl.ds(k * ROWS, ROWS)
        if receive_late(3, k):
            place_edges(3)
        a, b, s = coefficients(k)
        mu = gather_populations(3, k, -1)
        f = [S.f0[q, 0, here, :] for q in range(19)]
        rho, u = S.mom0[0, here, :], [S.mom0[i, here, :] for i in (1, 2, 3)]
        speed = u[0] * u[0] + u[1] * u[1] + u[2] * u[2]
        lam, by_s = collide_adjoint(mu, f, rho, u, speed, a, b, s)
        for q in range(19):
            lam_ref[q, 0, here, :] = lam[q]
        sens_ref[0, here, :] = jnp.where(S.lab[0, here, :] == 1, S.ds[here, :] + by_s, 0.0)
    total = jnp.sum(reduce_receive(1), axis=1, keepdims=True)
    en_ref[...] = jnp.broadcast_to(total, en_ref.shape)


def finish(scale, lam_ref, sens_ref, en_ref, out_sens, out_lam, lam, sens, some, sems):
    inv = 1.0 / (en_ref[...] * scale)
    rows = sens.shape[1]
    for q in range(19):
        for k in range(rows // ROWS):
            here = pl.ds(k * ROWS, ROWS)
            lam[q, 0, here, :] = lam_ref[q, 0, here, :] * inv
        pltpu.make_async_copy(lam.at[pl.ds(q, 1)], out_lam.at[pl.ds(q, 1)], sems.at[0]).start()
    for k in range(rows // ROWS):
        here = pl.ds(k * ROWS, ROWS)
        sens[0, here, :] = sens_ref[0, here, :] * inv
    pltpu.make_async_copy(sens, out_sens, sems.at[0]).start()
    pltpu.make_async_copy(some, some, sems.at[0]).wait()


def on_device(sizes, populations, solid_fraction, labels):
    rows, cols = solid_fraction.shape[1:]
    n_gz, n_gy, n_x, n_z, n_core = sizes
    leaves, tree = jax.tree.flatten(scratch_tree(rows, cols, (n_core * n_z - 1, n_x * n_gy - 1)))
    f32 = jnp.float32
    in_hbm = pl.BlockSpec(memory_space=pltpu.HBM)
    in_vmem = pl.BlockSpec(memory_space=pltpu.VMEM)
    lam_type = jax.ShapeDtypeStruct(populations.shape, f32)
    sens_type = jax.ShapeDtypeStruct(solid_fraction.shape, f32)
    limit = 24 * 1024 * 1024
    lam, sens, total = pl.pallas_call(
        functools.partial(kernel, tree, sizes),
        out_shape=(lam_type, sens_type, jax.ShapeDtypeStruct((ROWS, cols), f32)),
        in_specs=[in_hbm] * 3,
        out_specs=(in_vmem,) * 3,
        scratch_shapes=leaves,
        compiler_params=pltpu.CompilerParams(collective_id=0, has_side_effects=True, vmem_limit_bytes=limit),
        name="lattice",
    )(*[pltpu.with_memory_space_constraint(v, pltpu.HBM) for v in (populations, solid_fraction, labels)])
    scale = 1.0 / (STEPS * n_gz * n_gy * rows * cols)
    return pl.pallas_call(
        functools.partial(finish, scale),
        out_shape=(sens_type, lam_type),
        in_specs=[in_vmem] * 3,
        out_specs=(in_hbm,) * 2,
        scratch_shapes=[
            pltpu.VMEM(populations.shape, f32),
            pltpu.VMEM(solid_fraction.shape, f32),
            pltpu.VMEM((20 * rows * cols // LANES, 1, LANES), f32),
            pltpu.SemaphoreType.DMA((1,)),
        ],
        compiler_params=pltpu.CompilerParams(vmem_limit_bytes=4 * 1024 * 1024),
        name="finish",
    )(lam, sens, total)


def solution(mesh):
    n_gz, n_gy = mesh.shape["gz"], mesh.shape["gy"]
    n_core = 2
    n_z = 8 if n_gz % 16 == 0 else n_gz // 2
    n_x = n_gz // (n_core * n_z)
    in_specs = (P(None, "gz", "gy", None), P("gz", "gy", None), P("gz", "gy", None))
    out_specs = (P("gz", "gy", None), P(None, "gz", "gy", None))
    return jax.shard_map(
        functools.partial(on_device, (n_gz, n_gy, n_x, n_z, n_core)),
        mesh=mesh,
        in_specs=in_specs,
        out_specs=out_specs,
        check_vma=False,
    )
```

```python
import functools
import types

import jax
import jax.numpy as jnp
from jax import lax
from jax.experimental import pallas as pl
from jax.experimental.pallas import tpu as pltpu
from jax.sharding import PartitionSpec as P

STEPS = 2
OMEGA = 0.9
INLET_SPEED = 0.05
ROWS = 8
TOP = 8
MESH = pl.DeviceIdType.MESH
LANES = 128
EDGE_ROWS = ((0, 4), (1, 8), (2, 2), (3, 4))
GROUPS = [(r, g) for r in (0, 2, 3, 4) for g in ("A", "B", "E")]
GROUPS += [(1, side + g) for side in ("f", "n") for g in ("A", "B", "E")] + [(5, "A"), (6, "A"), (7, "A")]


def velocity_table():
    velocities = [(0, 0, 0)]
    for axis in range(3):
        for sign in (1, -1):
            vector = [0, 0, 0]
            vector[axis] = sign
            velocities.append(tuple(vector))
    for first in range(3):
        for second in range(first + 1, 3):
            for sign_a in (1, -1):
                for sign_b in (1, -1):
                    vector = [0, 0, 0]
                    vector[first] = sign_a
                    vector[second] = sign_b
                    velocities.append(tuple(vector))
    weights = [1.0 / 3.0] + [1.0 / 18.0] * 6 + [1.0 / 36.0] * 12
    opposite = [velocities.index(tuple((-e for e in vector))) for vector in velocities]
    return (velocities, weights, opposite)


VEL, WEIGHT, OPP = velocity_table()
INDEX = {v: q for q, v in enumerate(VEL)}
PAIRS = [(q, OPP[q]) for q in range(19) if q < OPP[q]]
UP = [(0, 0, 1), (1, 0, 1), (-1, 0, 1), (0, 1, 1), (0, -1, 1)]
DOWN = [(0, 0, -1), (1, 0, -1), (-1, 0, -1), (0, 1, -1), (0, -1, -1)]
FLAT = [v for v in VEL if v[2] == 0]
FLAT_UP = [(0, 1, 0), (1, 1, 0), (-1, 1, 0)]
FLAT_DOWN = [(0, -1, 0), (1, -1, 0), (-1, -1, 0)]


def inlet_value(q):
    along = VEL[q][2] * INLET_SPEED
    return WEIGHT[q] * (1.0 + 3.0 * along + 4.5 * along * along - 1.5 * INLET_SPEED * INLET_SPEED)


def roll_x(value, shift):
    if shift == 0:
        return value
    return pltpu.roll(value, shift % value.shape[1], 1)


def signed(terms):
    total = None
    for sign, value in terms:
        if sign == 0:
            continue
        if total is None:
            total = value if sign > 0 else -value
        else:
            total = total + value if sign > 0 else total - value
    return total


def dot_c(c, vector):
    return signed([(c[i], vector[i]) for i in range(3)])


def pair_moments(plus, minus, rest):
    total = rest + functools.reduce(lambda p, q: p + q, list(plus.values()))
    return total, [signed([(VEL[q][i], minus[q]) for q, o in PAIRS]) for i in range(3)]


def collide(f, a, b, s, k):
    plus = {q: f[q] + f[o] for q, o in PAIRS}
    minus = {q: f[q] - f[o] for q, o in PAIRS}
    rho, m = pair_moments(plus, minus, f[0])
    inv = 1.0 / rho
    u = [m[i] * inv for i in range(3)]
    speed = u[0] * u[0] + u[1] * u[1] + u[2] * u[2]
    brho = b * rho
    base = brho * (1.0 - 1.5 * speed)
    both, half_sum, half_diff = a + s, 0.5 * (a + s), 0.5 * (a - s)
    bases = {w: w * base for w in set(WEIGHT)}
    level = {w: bases[w] + k * inlet_value(q) for w, q in ((WEIGHT[0], 0), (WEIGHT[1], 1), (WEIGHT[7], 7))}
    post = [None] * 19
    post[0] = both * f[0] + level[WEIGHT[0]]
    for q, o in PAIRS:
        w = WEIGHT[q]
        along = dot_c(VEL[q], u)
        flow = brho * along
        even = half_sum * plus[q] + (4.5 * w) * (flow * along)
        odd = half_diff * minus[q] + (3.0 * w) * flow
        if VEL[q][2] == 0:
            even = even + level[w]
        else:
            even = even + (bases[w] + k * (0.5 * (inlet_value(q) + inlet_value(o))))
            odd = odd + k * (0.5 * (inlet_value(q) - inlet_value(o)))
        post[q] = even + odd
        post[o] = even - odd
    return rho, u, speed, post


def collide_adjoint(mu, f, rho, u, speed, a, b, s, extra=None):
    plus = {q: mu[q] + mu[o] for q, o in PAIRS}
    minus = {q: mu[q] - mu[o] for q, o in PAIRS}

    def weighted(table, first, second=None):
        axial, diagonal = [], []
        for q, o in PAIRS:
            c = VEL[q]
            sign = c[first] if second is None else c[first] * c[second]
            (axial if WEIGHT[q] == WEIGHT[1] else diagonal).append((sign, table[q]))
        one, two = signed(axial), signed(diagonal)
        two = two * WEIGHT[7]
        return two if one is None else one * WEIGHT[1] + two

    axial = functools.reduce(lambda p, q: p + q, [plus[q] for q, o in PAIRS if WEIGHT[q] == WEIGHT[1]])
    diagonal = functools.reduce(lambda p, q: p + q, [plus[q] for q, o in PAIRS if WEIGHT[q] != WEIGHT[1]])
    big_a = WEIGHT[0] * mu[0] + WEIGHT[1] * axial + WEIGHT[7] * diagonal
    big_b = [3.0 * weighted(minus, i) for i in range(3)]
    big_c = {}
    for i in range(3):
        for j in range(i, 3):
            big_c[i, j] = big_c[j, i] = 4.5 * weighted(plus, i, j)
    cu = [big_c[i, 0] * u[0] + big_c[i, 1] * u[1] + big_c[i, 2] * u[2] for i in range(3)]
    quad = cu[0] * u[0] + cu[1] * u[1] + cu[2] * u[2] - 1.5 * speed * big_a
    by_rho = b * (big_a - quad)
    triple = 3.0 * big_a
    by_m = [b * (big_b[i] + 2.0 * cu[i] - triple * u[i]) for i in range(3)]
    if extra is not None:
        by_rho = by_rho + extra[0]
        by_m = [by_m[i] + extra[1][i] for i in range(3)]
    both, half_sum, half_diff = a + s, 0.5 * (a + s), 0.5 * (a - s)
    lam = [None] * 19
    lam[0] = both * mu[0] + by_rho
    sums, differences = [], []
    for q, o in PAIRS:
        even = half_sum * plus[q] + by_rho
        odd = half_diff * minus[q] + dot_c(VEL[q], by_m)
        lam[q] = even + odd
        lam[o] = even - odd
        sums.append(plus[q] * (f[q] + f[o]))
        differences.append(minus[q] * (f[q] - f[o]))
    all_sums = functools.reduce(lambda p, q: p + q, sums)
    all_differences = functools.reduce(lambda p, q: p + q, differences)
    middle = mu[0] * f[0]
    total = rho * (big_a + big_b[0] * u[0] + big_b[1] * u[1] + big_b[2] * u[2] + quad)
    by_s = OMEGA * (middle + 0.5 * all_sums - total) - (1.0 - 0.5 * OMEGA) * all_differences
    return lam, by_s


def scratch_tree(rows, cols, n_ar):
    def vmem(*shape):
        return pltpu.VMEM(shape, jnp.float32)

    padded = rows + 16
    dma = pltpu.SemaphoreType.DMA
    return dict(
        f0=vmem(19, 1, rows, cols),
        sol=vmem(1, rows, cols),
        lab=pltpu.VMEM((1, rows, cols), jnp.int32),
        coef=vmem(3, rows, cols),
        mom0=vmem(4, rows, cols),
        mom1=vmem(4, rows, cols),
        f1=vmem(19, rows, cols),
        ds=vmem(rows, cols),
        acc=vmem(ROWS, cols),
        in_sem=dma((1,)),
        ssem=dma((8,)),
        rsem=dma((len(GROUPS),)),
        some=vmem(3 * 19 * rows * cols // LANES, 1, LANES),
        part=vmem(6, padded, cols),
        grad=vmem(4, padded, cols),
        out1=vmem(2, 4, padded, cols),
        in1=vmem(2, 4, padded, cols),
        side=vmem(2, 3, padded, cols),
        mine=vmem(3, rows, cols),
        rest=vmem(4, rows, cols),
        far_rest=vmem(4, rows, cols),
        far_s=vmem(rows, cols),
        s_hi=vmem(1, cols),
        s_lo=vmem(1, cols),
        far_s_hi=vmem(1, cols),
        far_s_lo=vmem(1, cols),
        rest_hi=vmem(4, cols),
        rest_lo=vmem(4, cols),
        far_rest_hi=vmem(4, cols),
        far_rest_lo=vmem(4, cols),
        yu={r: vmem(n, cols) for r, n in EDGE_ROWS},
        yd={r: vmem(n, cols) for r, n in EDGE_ROWS},
        ryu={r: vmem(n, cols) for r, n in EDGE_ROWS},
        ryd={r: vmem(n, cols) for r, n in EDGE_ROWS},
        out={r: vmem(2, 5, rows, cols) for r in (0, 3)},
        arrived={r: vmem(2, 5, padded, cols) for r in (0, 3)},
        flat={r: vmem(9, padded, cols) for r in (0, 3)},
        dg=[[vmem(1, cols) for i in range(4)] for r in range(4)],
        rdg=[[vmem(1, cols) for i in range(4)] for r in range(4)],
        ar=[vmem(1, LANES) for count in n_ar],
        arr=[[vmem(1, LANES) for i in range(count)] for count in n_ar],
    )


def kernel(tree, sizes, pop_ref, sol_ref, lab_ref, lam_ref, sens_ref, en_ref, *refs):
    S = types.SimpleNamespace(**jax.tree.unflatten(tree, refs))
    n_gz, n_gy, n_x, n_z, n_core = sizes
    rows, cols = S.ds.shape
    chunks = rows // ROWS
    order = [chunks - 1, 0, *range(chunks - 2, 0, -1)]
    late_order = [*range(1, chunks - 1), chunks - 1, 0]
    last = TOP + rows
    gz = lax.axis_index("gz")
    gy = lax.axis_index("gy")

    def size(ref):
        return functools.reduce(lambda p, q: p * q, ref.shape) // LANES

    def wait_bytes(count, sem):
        some = S.some.at[pl.ds(0, count)]
        pltpu.make_async_copy(some, some, sem).wait()

    loads = ((pop_ref, S.f0), (sol_ref, S.sol), (lab_ref, S.lab))
    for src, dst in loads:
        pltpu.make_async_copy(src, dst, S.in_sem.at[0]).start()

    def at(dz, dy):
        return (lax.rem(gz + dz + n_gz, n_gz), lax.rem(gy + dy + n_gy, n_gy))

    core = lax.rem(gz, n_core)
    zpos = lax.rem(gz // n_core, n_z)
    xpos = gz // (n_core * n_z)

    def place(dx, dz, dcore, dy):
        x = lax.rem(xpos + dx, n_x)
        z = lax.rem(zpos + dz, n_z)
        c = lax.rem(core + dcore, n_core)
        return ((x * n_z + z) * n_core + c, lax.rem(gy + dy, n_gy))

    stages = [
        [place(0, dz, dc, 0) for dz in range(n_z) for dc in range(n_core) if (dz, dc) != (0, 0)],
        [place(dx, 0, 0, dy) for dx in range(n_x) for dy in range(n_gy) if (dx, dy) != (0, 0)],
    ]
    near = [at(dz, dy) for dz, dy in ((1, 0), (-1, 0), (0, 1), (0, -1), (1, 1), (1, -1), (-1, 1), (-1, -1))]
    barrier = pltpu.get_barrier_semaphore()
    greeted = near + stages[0] + [place(dx, 0, 0, 0) for dx in range(1, n_x)]
    for device in greeted:
        pl.semaphore_signal(barrier, inc=1, device_id=device, device_id_type=MESH)

    sent_bytes, group_bytes = {}, {}

    def group_of(r, i):
        if i >= base:
            name = "E"
        else:
            name = "B" if i % chunks == order[-1] and r != 5 else "A"
        if r == 4 and i < base:
            name = "B" if i in (0, chunks - 1) else "A"
        if r == 1:
            near_side = i - base not in (2, 3) if i >= base else i >= chunks
            name = ("n" if near_side else "f") + name
        return (r, name)

    def send(src, dst, r, i, device):
        group = group_of(r, i)
        pltpu.make_async_remote_copy(
            src_ref=src,
            dst_ref=dst,
            send_sem=S.ssem.at[r],
            recv_sem=S.rsem.at[GROUPS.index(group)],
            device_id=device,
            device_id_type=MESH,
        ).start()
        sent_bytes[r] = sent_bytes.get(r, 0) + size(src)
        group_bytes[group] = group_bytes.get(group, 0) + size(src)

    far, near_z = 2 * core - 1, 1 - 2 * core
    upward, downward = 1 - core, core
    base = 2 * chunks
    DIAGONAL = ((1, 1), (1, -1), (-1, 1), (-1, -1))
    FAR_DIAGONAL = ((far, 1), (far, -1), (near_z, 1), (near_z, -1))

    def send_bulk(r, k):
        src, dst = pl.ds(k * ROWS, ROWS), pl.ds(TOP + k * ROWS, ROWS)
        if r in (0, 3):
            send(S.out[r].at[0, :, src, :], S.arrived[r].at[0, :, dst, :], r, k, at(far, 0))
            send(S.out[r].at[1, :, src, :], S.arrived[r].at[1, :, dst, :], r, chunks + k, at(near_z, 0))
        if r == 1:
            send(S.out1.at[0, :, dst, :], S.in1.at[0, :, dst, :], 1, k, at(far, 0))
            send(S.out1.at[1, :, dst, :], S.in1.at[1, :, dst, :], 1, chunks + k, at(near_z, 0))
        if r == 2:
            send(S.mine.at[:, src, :], S.side.at[1, :, dst, :], 2, chunks + k, at(near_z, 0))
        if r == 4:
            send(S.rest.at[:, src, :], S.far_rest.at[:, src, :], 4, k, at(far, 0))

    def send_edges(r, end):
        high = end == 1
        if r == 4:
            src, dst = (S.rest_hi, S.far_rest_hi) if high else (S.rest_lo, S.far_rest_lo)
            send(src, dst, 4, base + (2 if high else 3), at(far, end))
            return
        src, dst = (S.yu, S.ryu) if high else (S.yd, S.ryd)
        send(src[r], dst[r], r, base + (0 if high else 1), at(0, end))
        for i, (dz, dy) in enumerate(DIAGONAL if r in (0, 3) else FAR_DIAGONAL):
            if dy == end and (r != 2 or i >= 2):
                send(S.dg[r][i], S.rdg[r][i], r, base + 2 + i, at(dz, dy))

    def send_chunk(r, k):
        if k == chunks - 1:
            send_edges(r, 1)
        if k == 0:
            send_edges(r, -1)
        send_bulk(r, k)

    def sent(*rounds):
        for r in rounds:
            wait_bytes(sent_bytes[r], S.ssem.at[r])

    landed = set()

    def receive_group(r, name):
        if (r, name) not in landed:
            landed.add((r, name))
            wait_bytes(group_bytes[r, name], S.rsem.at[GROUPS.index((r, name))])

    def receive(r, k, side=""):
        receive_group(r, side + "A")
        if abs(k - order[-1]) <= 1:
            receive_group(r, side + "B")
        receive_group(r, side + "E")
        return k == order[0]

    def receive_late(r, k, side=""):
        receive_group(r, side + "A")
        receive_group(r, side + "B")
        first = k == late_order[-2]
        if first:
            receive_group(r, side + "E")
        return first

    def interior(k):
        return pl.ds(TOP + k * ROWS, ROWS)

    def moved(k, dy):
        return pl.ds(TOP + k * ROWS - dy, ROWS)

    def emit_populations(r, k, values, sense):
        here = pl.ds(k * ROWS, ROWS)
        for side, table in ((upward, UP), (downward, DOWN)):
            for i, d in enumerate(table):
                q = INDEX[tuple(sense * e for e in d)]
                value = roll_x(values[q], d[0])
                S.out[r][side, i, here, :] = value
                slot = DIAGONAL.index((d[2], d[1])) if d[1] else None
                if d[1] == 1 and k == chunks - 1:
                    S.dg[r][slot][...] = value[ROWS - 1 :, :]
                if d[1] == -1 and k == 0:
                    S.dg[r][slot][...] = value[:1, :]
        for i, d in enumerate(FLAT):
            q = INDEX[tuple(sense * e for e in d)]
            value = roll_x(values[q], d[0])
            S.flat[r][i, interior(k), :] = value
            if d[1] == 1 and k == chunks - 1:
                j = FLAT_UP.index(d)
                S.yu[r][j : j + 1, :] = value[ROWS - 1 :, :]
            if d[1] == -1 and k == 0:
                j = FLAT_DOWN.index(d)
                S.yd[r][j : j + 1, :] = value[:1, :]

    def place_edges(r):
        for i, side, row in ((0, downward, TOP - 1), (1, downward, last), (2, upward, TOP - 1), (3, upward, last)):
            slot = 3 if i % 2 == 0 else 4
            S.arrived[r][side, slot, pl.ds(row, 1), :] = S.rdg[r][i][...]
        for j in range(3):
            S.flat[r][FLAT.index(FLAT_UP[j]), pl.ds(TOP - 1, 1), :] = S.ryu[r][j : j + 1, :]
            S.flat[r][FLAT.index(FLAT_DOWN[j]), pl.ds(last, 1), :] = S.ryd[r][j : j + 1, :]

    def gather_populations(r, k, sense):
        values = [None] * 19
        for i, d in enumerate(FLAT):
            values[INDEX[tuple(sense * e for e in d)]] = S.flat[r][i, moved(k, d[1]), :]
        for side, table in ((downward, UP), (upward, DOWN)):
            for i, d in enumerate(table):
                values[INDEX[tuple(sense * e for e in d)]] = S.arrived[r][side, i, moved(k, d[1]), :]
        return values

    def coefficients(k):
        here = pl.ds(k * ROWS, ROWS)
        return [S.coef[i, here, :] for i in range(3)]

    def inlet(k):
        return jnp.where(S.lab[0, pl.ds(k * ROWS, ROWS), :] == 3, 1.0, 0.0)

    wait_bytes(sum(size(dst) for src, dst in loads), S.in_sem.at[0])
    for k in order:
        here = pl.ds(k * ROWS, ROWS)
        label = S.lab[0, here, :]
        s = jnp.where(label == 1, S.sol[0, here, :], jnp.where(label == 2, 1.0, 0.0))
        free = jnp.where(label == 3, 0.0, 1.0 - s)
        b = jnp.where(label == 4, free, OMEGA * free)
        a = jnp.where(label == 4, 0.0, (1.0 - OMEGA) * free)
        for i, value in enumerate((a, b, s)):
            S.coef[i, here, :] = value
        f = [S.f0[q, 0, here, :] for q in range(19)]
        rho, u, speed, post = collide(f, a, b, s, inlet(k))
        for i, value in enumerate((rho, *u)):
            S.mom0[i, here, :] = value
        emit_populations(0, k, post, 1)

    pl.semaphore_wait(barrier, len(greeted))
    send_edges(0, 1)
    send_edges(0, -1)
    for k in order:
        send_bulk(0, k)
    S.s_hi[...] = S.coef[2, pl.ds(rows - 1, 1), :]
    S.s_lo[...] = S.coef[2, pl.ds(0, 1), :]
    send(S.s_hi, S.far_s_hi, 5, 1, at(far, 1))
    send(S.s_lo, S.far_s_lo, 5, 2, at(far, -1))
    send(S.coef.at[2], S.far_s, 5, 0, at(far, 0))

    for k in order:
        here = pl.ds(k * ROWS, ROWS)
        if receive(0, k):
            place_edges(0)
        a, b, s = coefficients(k)
        f = gather_populations(0, k, 1)
        for q in range(19):
            S.f1[q, here, :] = f[q]
        rho, u, speed, post = collide(f, a, b, s, inlet(k))
        for i, value in enumerate((rho, *u)):
            S.mom1[i, here, :] = value
        flow = rho * speed
        S.ds[here, :] = -flow
        energy = (1.0 - s) * flow
        S.acc[...] = energy if k == order[0] else S.acc[...] + energy

        def three(cy, cz):
            mid = post[INDEX[0, cy, cz]]
            right = roll_x(post[INDEX[1, cy, cz]], 1)
            left = roll_x(post[INDEX[-1, cy, cz]], -1)
            return mid + right + left, right - left

        for slot, cz in ((upward, 1), (downward, -1)):
            total, along = three(0, cz)
            for i, value in enumerate((total, along, post[INDEX[0, 1, cz]], post[INDEX[0, -1, cz]])):
                S.out1[slot, i, interior(k), :] = value
        if k == chunks - 1:
            end = pl.ds(last - 1, 1)
            for j, (i, row) in enumerate(((0, end), (1, end), (2, pl.ds(last - 2, 1)), (2, end))):
                S.yu[1][2 + j : 3 + j, :] = S.out1[0, i, row, :]
            S.dg[1][0][...] = S.out1[0, 2, end, :]
            S.dg[1][2][...] = S.out1[1, 2, end, :]
        if k == 0:
            end = pl.ds(TOP, 1)
            for j, (i, row) in enumerate(((0, end), (1, end), (3, pl.ds(TOP + 1, 1)), (3, end))):
                S.yd[1][2 + j : 3 + j, :] = S.out1[0, i, row, :]
            S.dg[1][1][...] = S.out1[0, 3, end, :]
            S.dg[1][3][...] = S.out1[1, 3, end, :]
        for j, cy in enumerate((0, 1, -1)):
            total, along = three(cy, 0)
            S.part[2 * j, interior(k), :] = total
            S.part[2 * j + 1, interior(k), :] = along
            if cy == 1 and k == chunks - 1:
                S.yu[1][0:1, :] = total[ROWS - 1 :, :]
                S.yu[1][1:2, :] = along[ROWS - 1 :, :]
            if cy == -1 and k == 0:
                S.yd[1][0:1, :] = total[:1, :]
                S.yd[1][1:2, :] = along[:1, :]
        send_chunk(1, k)

    sent(0, 5)

    def place_halo(side, i):
        S.in1[side, 2, pl.ds(TOP - 1, 1), :] = S.rdg[1][i][...]
        S.in1[side, 3, pl.ds(last, 1), :] = S.rdg[1][i + 1][...]

    for k in late_order:
        here = pl.ds(k * ROWS, ROWS)
        if receive_late(1, k, "n"):
            place_halo(1, 2)
            for j in range(2):
                S.part[2 + j, pl.ds(TOP - 1, 1), :] = S.ryu[1][j : j + 1, :]
                S.part[4 + j, pl.ds(last, 1), :] = S.ryd[1][j : j + 1, :]
            S.out1[0, 2, pl.ds(TOP - 1, 1), :] = S.ryu[1][5:6, :]
            S.out1[0, 3, pl.ds(last, 1), :] = S.ryd[1][5:6, :]
        near_x = S.in1[1, 1, interior(k), :]
        near_a, near_b = S.in1[1, 2, moved(k, 1), :], S.in1[1, 3, moved(k, -1), :]
        mass = S.in1[1, 0, interior(k), :] + (near_a + near_b)
        mid, mid_x = S.part[0, interior(k), :], S.part[1, interior(k), :]
        ahead, ahead_x = S.part[2, moved(k, 1), :], S.part[3, moved(k, 1), :]
        behind, behind_x = S.part[4, moved(k, -1), :], S.part[5, moved(k, -1), :]
        rest = (
            mass + (mid + (ahead + behind)),
            near_x + (mid_x + (ahead_x + behind_x)),
            (near_a - near_b) + (ahead - behind),
            mass,
        )
        for i, value in enumerate(rest):
            S.rest[i, here, :] = value
            if k == chunks - 1:
                S.rest_hi[i : i + 1, :] = value[ROWS - 1 :, :]
            if k == 0:
                S.rest_lo[i : i + 1, :] = value[:1, :]
        send_chunk(4, k)

    def finish_moments(rest, total, along, ahead, behind, s):
        mass = total + (ahead + behind)
        rho = rest[0] + mass
        inv = 1.0 / rho
        u = [(rest[1] + along) * inv, (rest[2] + (ahead - behind)) * inv, (mass - rest[3]) * inv]
        speed = u[0] * u[0] + u[1] * u[1] + u[2] * u[2]
        free = 1.0 - s
        twice = 2.0 * free
        return rho, speed, [twice * v for v in u], free

    for k in late_order:
        here = pl.ds(k * ROWS, ROWS)
        if receive_late(1, k, "f"):
            place_halo(0, 0)
        rho, speed, (x, y, z), free = finish_moments(
            [S.rest[i, here, :] for i in range(4)],
            S.in1[0, 0, interior(k), :],
            S.in1[0, 1, interior(k), :],
            S.in1[0, 2, moved(k, 1), :],
            S.in1[0, 3, moved(k, -1), :],
            S.coef[2, here, :],
        )
        flow = rho * speed
        S.ds[here, :] = S.ds[here, :] - flow
        S.acc[...] = S.acc[...] + free * flow
        e = free * speed
        w = -z - e
        for i, value in enumerate((x, y, w)):
            S.mine[i, here, :] = value
        for i, value in enumerate((x, y - e, -y - e, e)):
            S.grad[i, interior(k), :] = value
        if k == chunks - 1:
            S.dg[2][2][...] = (w - y)[ROWS - 1 :, :]
            S.yu[2][0:1, :] = x[ROWS - 1 :, :]
            S.yu[2][1:2, :] = (-y - e)[ROWS - 1 :, :]
        if k == 0:
            S.dg[2][3][...] = (w + y)[:1, :]
            S.yd[2][0:1, :] = x[:1, :]
            S.yd[2][1:2, :] = (y - e)[:1, :]
        send_chunk(2, k)

    def reduce_send(stage, value):
        S.ar[stage][...] = value
        for i, device in enumerate(stages[stage]):
            pltpu.make_async_remote_copy(
                src_ref=S.ar[stage],
                dst_ref=S.arr[stage][i],
                send_sem=S.ssem.at[6 + stage],
                recv_sem=S.rsem.at[GROUPS.index((6 + stage, "A"))],
                device_id=device,
                device_id_type=MESH,
            ).start()
        sent_bytes[6 + stage] = len(stages[stage])

    def reduce_receive(stage):
        wait_bytes(len(stages[stage]), S.rsem.at[GROUPS.index((6 + stage, "A"))])
        value = S.ar[stage][...]
        for i in range(len(stages[stage])):
            value = value + S.arr[stage][i][...]
        return value

    acc = S.acc[...]
    acc = functools.reduce(lambda p, q: p + q, [acc[:, i : i + 128] for i in range(0, cols, 128)])
    reduce_send(0, jnp.sum(acc, axis=0, keepdims=True))

    zero_row = jnp.zeros((1, cols), jnp.float32)
    sent(1)

    def far_plane(rest, total, along, ahead, behind, s):
        rho, speed, (x, y, z), free = finish_moments(rest, total, along, ahead, behind, s)
        return x, y, z - free * speed

    for k in late_order:
        here = pl.ds(k * ROWS, ROWS)
        receive_group(5, "A")
        receive_group(4, "A")
        if k == late_order[-2]:
            receive_group(4, "B")
            receive_group(4, "E")
            low, high = pl.ds(TOP - 1, 1), pl.ds(last, 1)
            x, y, w = far_plane(
                [S.far_rest_hi[i : i + 1, :] for i in range(4)],
                S.ryu[1][2:3, :],
                S.ryu[1][3:4, :],
                S.ryu[1][4:5, :],
                S.out1[0, 3, pl.ds(TOP, 1), :],
                S.far_s_hi[...],
            )
            S.side[0, 1, low, :] = y
            S.side[0, 2, low, :] = w
            x, y, w = far_plane(
                [S.far_rest_lo[i : i + 1, :] for i in range(4)],
                S.ryd[1][2:3, :],
                S.ryd[1][3:4, :],
                S.out1[0, 2, pl.ds(last - 1, 1), :],
                S.ryd[1][4:5, :],
                S.far_s_lo[...],
            )
            S.side[0, 1, high, :] = y
            S.side[0, 2, high, :] = w
        value = far_plane(
            [S.far_rest[i, here, :] for i in range(4)],
            S.out1[0, 0, interior(k), :],
            S.out1[0, 1, interior(k), :],
            S.out1[0, 2, moved(k, 1), :],
            S.out1[0, 3, moved(k, -1), :],
            S.far_s[here, :],
        )
        for i in range(3):
            S.side[0, i, interior(k), :] = value[i]

    for k in order:
        here = pl.ds(k * ROWS, ROWS)
        if receive(2, k):
            for i, row in ((2, TOP - 1), (3, last)):
                S.side[1, 2, pl.ds(row, 1), :] = S.rdg[2][i][...]
                S.side[1, 1, pl.ds(row, 1), :] = zero_row
            for j, slot in ((0, 0), (1, 2)):
                S.grad[slot, pl.ds(TOP - 1, 1), :] = S.ryu[2][j : j + 1, :]
            for j, slot in ((0, 0), (1, 1)):
                S.grad[slot, pl.ds(last, 1), :] = S.ryd[2][j : j + 1, :]
        a, b, s = coefficients(k)
        mu = [None] * 19
        for slot, cz in ((upward, 1), (downward, -1)):
            x, w = S.side[slot, 0, interior(k), :], S.side[slot, 2, interior(k), :]
            mu[INDEX[0, 0, cz]] = w
            mu[INDEX[1, 0, cz]] = roll_x(w + x, -1)
            mu[INDEX[-1, 0, cz]] = roll_x(w - x, 1)
            mu[INDEX[0, 1, cz]] = S.side[slot, 2, moved(k, -1), :] + S.side[slot, 1, moved(k, -1), :]
            mu[INDEX[0, -1, cz]] = S.side[slot, 2, moved(k, 1), :] - S.side[slot, 1, moved(k, 1), :]
        for cy, slot in ((0, 3), (1, 1), (-1, 2)):
            x, w = S.grad[0, moved(k, -cy), :], S.grad[slot, moved(k, -cy), :]
            w = -w if cy == 0 else w
            mu[INDEX[0, cy, 0]] = w
            mu[INDEX[1, cy, 0]] = roll_x(w + x, -1)
            mu[INDEX[-1, cy, 0]] = roll_x(w - x, 1)
        f = [S.f1[q, here, :] for q in range(19)]
        rho, u = S.mom1[0, here, :], [S.mom1[i, here, :] for i in (1, 2, 3)]
        speed = u[0] * u[0] + u[1] * u[1] + u[2] * u[2]
        free = 1.0 - s
        twice = 2.0 * free
        extra = (-(free * speed), [twice * u[i] for i in range(3)])
        lam, by_s = collide_adjoint(mu, f, rho, u, speed, a, b, s, extra)
        S.ds[here, :] = S.ds[here, :] + by_s
        emit_populations(3, k, lam, -1)
        send_chunk(3, k)

    reduce_send(1, reduce_receive(0))
    sent(4, 2, 3, 6, 7)

    for k in late_order:
        here = pl.ds(k * ROWS, ROWS)
        if receive_late(3, k):
            place_edges(3)
        a, b, s = coefficients(k)
        mu = gather_populations(3, k, -1)
        f = [S.f0[q, 0, here, :] for q in range(19)]
        rho, u = S.mom0[0, here, :], [S.mom0[i, here, :] for i in (1, 2, 3)]
        speed = u[0] * u[0] + u[1] * u[1] + u[2] * u[2]
        lam, by_s = collide_adjoint(mu, f, rho, u, speed, a, b, s)
        for q in range(19):
            lam_ref[q, 0, here, :] = lam[q]
        sens_ref[0, here, :] = jnp.where(S.lab[0, here, :] == 1, S.ds[here, :] + by_s, 0.0)
    total = jnp.sum(reduce_receive(1), axis=1, keepdims=True)
    en_ref[...] = jnp.broadcast_to(total, en_ref.shape)


def finish(scale, lam_ref, sens_ref, en_ref, out_sens, out_lam, lam, sens, some, sems):
    inv = 1.0 / (en_ref[...] * scale)
    rows = sens.shape[1]
    for q in range(19):
        for k in range(rows // ROWS):
            here = pl.ds(k * ROWS, ROWS)
            lam[q, 0, here, :] = lam_ref[q, 0, here, :] * inv
        pltpu.make_async_copy(lam.at[pl.ds(q, 1)], out_lam.at[pl.ds(q, 1)], sems.at[0]).start()
    for k in range(rows // ROWS):
        here = pl.ds(k * ROWS, ROWS)
        sens[0, here, :] = sens_ref[0, here, :] * inv
    pltpu.make_async_copy(sens, out_sens, sems.at[0]).start()
    pltpu.make_async_copy(some, some, sems.at[0]).wait()


def on_device(sizes, populations, solid_fraction, labels):
    rows, cols = solid_fraction.shape[1:]
    n_gz, n_gy, n_x, n_z, n_core = sizes
    leaves, tree = jax.tree.flatten(scratch_tree(rows, cols, (n_core * n_z - 1, n_x * n_gy - 1)))
    f32 = jnp.float32
    in_hbm = pl.BlockSpec(memory_space=pltpu.HBM)
    in_vmem = pl.BlockSpec(memory_space=pltpu.VMEM)
    lam_type = jax.ShapeDtypeStruct(populations.shape, f32)
    sens_type = jax.ShapeDtypeStruct(solid_fraction.shape, f32)
    limit = 24 * 1024 * 1024
    lam, sens, total = pl.pallas_call(
        functools.partial(kernel, tree, sizes),
        out_shape=(lam_type, sens_type, jax.ShapeDtypeStruct((ROWS, cols), f32)),
        in_specs=[in_hbm] * 3,
        out_specs=(in_vmem,) * 3,
        scratch_shapes=leaves,
        compiler_params=pltpu.CompilerParams(collective_id=0, has_side_effects=True, vmem_limit_bytes=limit),
        name="lattice",
    )(*[pltpu.with_memory_space_constraint(v, pltpu.HBM) for v in (populations, solid_fraction, labels)])
    scale = 1.0 / (STEPS * n_gz * n_gy * rows * cols)
    return pl.pallas_call(
        functools.partial(finish, scale),
        out_shape=(sens_type, lam_type),
        in_specs=[in_vmem] * 3,
        out_specs=(in_hbm,) * 2,
        scratch_shapes=[
            pltpu.VMEM(populations.shape, f32),
            pltpu.VMEM(solid_fraction.shape, f32),
            pltpu.VMEM((20 * rows * cols // LANES, 1, LANES), f32),
            pltpu.SemaphoreType.DMA((1,)),
        ],
        compiler_params=pltpu.CompilerParams(vmem_limit_bytes=4 * 1024 * 1024),
        name="finish",
    )(lam, sens, total)


def solution(mesh):
    n_gz, n_gy = mesh.shape["gz"], mesh.shape["gy"]
    n_core = 2
    n_z = 8 if n_gz % 16 == 0 else n_gz // 2
    n_x = n_gz // (n_core * n_z)
    in_specs = (P(None, "gz", "gy", None), P("gz", "gy", None), P("gz", "gy", None))
    out_specs = (P("gz", "gy", None), P(None, "gz", "gy", None))
    return jax.shard_map(
        functools.partial(on_device, (n_gz, n_gy, n_x, n_z, n_core)),
        mesh=mesh,
        in_specs=in_specs,
        out_specs=out_specs,
        check_vma=False,
    )
```

```python
import functools
import types

import jax
import jax.numpy as jnp
from jax import lax
from jax.experimental import pallas as pl
from jax.experimental.pallas import tpu as pltpu
from jax.sharding import PartitionSpec as P

STEPS = 2
OMEGA = 0.9
INLET_SPEED = 0.05
ROWS = 8
TOP = 8
MESH = pl.DeviceIdType.MESH
LANES = 128
EDGE_ROWS = ((0, 4), (1, 8), (2, 2), (3, 4))
GROUPS = [(r, g) for r in (0, 2, 3, 4) for g in ("A", "B", "E")]
GROUPS += [(1, side + g) for side in ("f", "n") for g in ("A", "B", "E")] + [(5, "A"), (6, "A"), (7, "A")]


def velocity_table():
    velocities = [(0, 0, 0)]
    for axis in range(3):
        for sign in (1, -1):
            vector = [0, 0, 0]
            vector[axis] = sign
            velocities.append(tuple(vector))
    for first in range(3):
        for second in range(first + 1, 3):
            for sign_a in (1, -1):
                for sign_b in (1, -1):
                    vector = [0, 0, 0]
                    vector[first] = sign_a
                    vector[second] = sign_b
                    velocities.append(tuple(vector))
    weights = [1.0 / 3.0] + [1.0 / 18.0] * 6 + [1.0 / 36.0] * 12
    opposite = [velocities.index(tuple((-e for e in vector))) for vector in velocities]
    return (velocities, weights, opposite)


VEL, WEIGHT, OPP = velocity_table()
INDEX = {v: q for q, v in enumerate(VEL)}
PAIRS = [(q, OPP[q]) for q in range(19) if q < OPP[q]]
UP = [(0, 0, 1), (1, 0, 1), (-1, 0, 1), (0, 1, 1), (0, -1, 1)]
DOWN = [(0, 0, -1), (1, 0, -1), (-1, 0, -1), (0, 1, -1), (0, -1, -1)]
FLAT = [v for v in VEL if v[2] == 0]
FLAT_UP = [(0, 1, 0), (1, 1, 0), (-1, 1, 0)]
FLAT_DOWN = [(0, -1, 0), (1, -1, 0), (-1, -1, 0)]


def inlet_value(q):
    along = VEL[q][2] * INLET_SPEED
    return WEIGHT[q] * (1.0 + 3.0 * along + 4.5 * along * along - 1.5 * INLET_SPEED * INLET_SPEED)


def roll_x(value, shift):
    if shift == 0:
        return value
    return pltpu.roll(value, shift % value.shape[1], 1)


def signed(terms):
    total = None
    for sign, value in terms:
        if sign == 0:
            continue
        if total is None:
            total = value if sign > 0 else -value
        else:
            total = total + value if sign > 0 else total - value
    return total


def dot_c(c, vector):
    return signed([(c[i], vector[i]) for i in range(3)])


def pair_moments(plus, minus, rest):
    total = rest + functools.reduce(lambda p, q: p + q, list(plus.values()))
    return total, [signed([(VEL[q][i], minus[q]) for q, o in PAIRS]) for i in range(3)]


def collide(f, a, b, s, k):
    plus = {q: f[q] + f[o] for q, o in PAIRS}
    minus = {q: f[q] - f[o] for q, o in PAIRS}
    rho, m = pair_moments(plus, minus, f[0])
    inv = 1.0 / rho
    u = [m[i] * inv for i in range(3)]
    speed = u[0] * u[0] + u[1] * u[1] + u[2] * u[2]
    brho = b * rho
    base = brho * (1.0 - 1.5 * speed)
    both, half_sum, half_diff = a + s, 0.5 * (a + s), 0.5 * (a - s)
    bases = {w: w * base for w in set(WEIGHT)}
    level = {w: bases[w] + k * inlet_value(q) for w, q in ((WEIGHT[0], 0), (WEIGHT[1], 1), (WEIGHT[7], 7))}
    post = [None] * 19
    post[0] = both * f[0] + level[WEIGHT[0]]
    for q, o in PAIRS:
        w = WEIGHT[q]
        along = dot_c(VEL[q], u)
        flow = brho * along
        even = half_sum * plus[q] + (4.5 * w) * (flow * along)
        odd = half_diff * minus[q] + (3.0 * w) * flow
        if VEL[q][2] == 0:
            even = even + level[w]
        else:
            even = even + (bases[w] + k * (0.5 * (inlet_value(q) + inlet_value(o))))
            odd = odd + k * (0.5 * (inlet_value(q) - inlet_value(o)))
        post[q] = even + odd
        post[o] = even - odd
    return rho, u, speed, post


def collide_adjoint(mu, f, rho, u, speed, a, b, s, extra=None):
    plus = {q: mu[q] + mu[o] for q, o in PAIRS}
    minus = {q: mu[q] - mu[o] for q, o in PAIRS}

    def weighted(table, first, second=None):
        axial, diagonal = [], []
        for q, o in PAIRS:
            c = VEL[q]
            sign = c[first] if second is None else c[first] * c[second]
            (axial if WEIGHT[q] == WEIGHT[1] else diagonal).append((sign, table[q]))
        one, two = signed(axial), signed(diagonal)
        two = two * WEIGHT[7]
        return two if one is None else one * WEIGHT[1] + two

    axial = functools.reduce(lambda p, q: p + q, [plus[q] for q, o in PAIRS if WEIGHT[q] == WEIGHT[1]])
    diagonal = functools.reduce(lambda p, q: p + q, [plus[q] for q, o in PAIRS if WEIGHT[q] != WEIGHT[1]])
    big_a = WEIGHT[0] * mu[0] + WEIGHT[1] * axial + WEIGHT[7] * diagonal
    big_b = [3.0 * weighted(minus, i) for i in range(3)]
    big_c = {}
    for i in range(3):
        for j in range(i, 3):
            big_c[i, j] = big_c[j, i] = 4.5 * weighted(plus, i, j)
    cu = [big_c[i, 0] * u[0] + big_c[i, 1] * u[1] + big_c[i, 2] * u[2] for i in range(3)]
    quad = cu[0] * u[0] + cu[1] * u[1] + cu[2] * u[2] - 1.5 * speed * big_a
    by_rho = b * (big_a - quad)
    triple = 3.0 * big_a
    by_m = [b * (big_b[i] + 2.0 * cu[i] - triple * u[i]) for i in range(3)]
    if extra is not None:
        by_rho = by_rho + extra[0]
        by_m = [by_m[i] + extra[1][i] for i in range(3)]
    both, half_sum, half_diff = a + s, 0.5 * (a + s), 0.5 * (a - s)
    lam = [None] * 19
    lam[0] = both * mu[0] + by_rho
    sums, differences = [], []
    for q, o in PAIRS:
        even = half_sum * plus[q] + by_rho
        odd = half_diff * minus[q] + dot_c(VEL[q], by_m)
        lam[q] = even + odd
        lam[o] = even - odd
        sums.append(plus[q] * (f[q] + f[o]))
        differences.append(minus[q] * (f[q] - f[o]))
    all_sums = functools.reduce(lambda p, q: p + q, sums)
    all_differences = functools.reduce(lambda p, q: p + q, differences)
    middle = mu[0] * f[0]
    total = rho * (big_a + big_b[0] * u[0] + big_b[1] * u[1] + big_b[2] * u[2] + quad)
    by_s = OMEGA * (middle + 0.5 * all_sums - total) - (1.0 - 0.5 * OMEGA) * all_differences
    return lam, by_s


def scratch_tree(rows, cols, n_ar):
    def vmem(*shape):
        return pltpu.VMEM(shape, jnp.float32)

    padded = rows + 16
    dma = pltpu.SemaphoreType.DMA
    return dict(
        f0=vmem(19, 1, rows, cols),
        sol=vmem(1, rows, cols),
        lab=pltpu.VMEM((1, rows, cols), jnp.int32),
        coef=vmem(3, rows, cols),
        mom0=vmem(4, rows, cols),
        mom1=vmem(4, rows, cols),
        f1=vmem(19, rows, cols),
        ds=vmem(rows, cols),
        acc=vmem(ROWS, cols),
        in_sem=dma((1,)),
        ssem=dma((8,)),
        rsem=dma((len(GROUPS),)),
        some=vmem(3 * 19 * rows * cols // LANES, 1, LANES),
        part=vmem(6, padded, cols),
        grad=vmem(4, padded, cols),
        out1=vmem(2, 4, padded, cols),
        in1=vmem(2, 4, padded, cols),
        side=vmem(2, 3, padded, cols),
        mine=vmem(3, rows, cols),
        rest=vmem(4, rows, cols),
        far_rest=vmem(4, rows, cols),
        far_s=vmem(rows, cols),
        s_hi=vmem(1, cols),
        s_lo=vmem(1, cols),
        far_s_hi=vmem(1, cols),
        far_s_lo=vmem(1, cols),
        rest_hi=vmem(4, cols),
        rest_lo=vmem(4, cols),
        far_rest_hi=vmem(4, cols),
        far_rest_lo=vmem(4, cols),
        yu={r: vmem(n, cols) for r, n in EDGE_ROWS},
        yd={r: vmem(n, cols) for r, n in EDGE_ROWS},
        ryu={r: vmem(n, cols) for r, n in EDGE_ROWS},
        ryd={r: vmem(n, cols) for r, n in EDGE_ROWS},
        out={r: vmem(2, 5, rows, cols) for r in (0, 3)},
        arrived={r: vmem(2, 5, padded, cols) for r in (0, 3)},
        flat={r: vmem(9, padded, cols) for r in (0, 3)},
        dg=[[vmem(1, cols) for i in range(4)] for r in range(4)],
        rdg=[[vmem(1, cols) for i in range(4)] for r in range(4)],
        ar=[vmem(1, LANES) for count in n_ar],
        arr=[[vmem(1, LANES) for i in range(count)] for count in n_ar],
    )


def kernel(tree, sizes, pop_ref, sol_ref, lab_ref, lam_ref, sens_ref, en_ref, *refs):
    S = types.SimpleNamespace(**jax.tree.unflatten(tree, refs))
    n_gz, n_gy, n_x, n_z, n_core = sizes
    rows, cols = S.ds.shape
    chunks = rows // ROWS
    order = [chunks - 1, 0, *range(chunks - 2, 0, -1)]
    late_order = [*range(1, chunks - 1), chunks - 1, 0]
    last = TOP + rows
    gz = lax.axis_index("gz")
    gy = lax.axis_index("gy")

    def size(ref):
        return functools.reduce(lambda p, q: p * q, ref.shape) // LANES

    def wait_bytes(count, sem):
        some = S.some.at[pl.ds(0, count)]
        pltpu.make_async_copy(some, some, sem).wait()

    def at(dz, dy):
        return (lax.rem(gz + dz + n_gz, n_gz), lax.rem(gy + dy + n_gy, n_gy))

    core = lax.rem(gz, n_core)
    zpos = lax.rem(gz // n_core, n_z)
    xpos = gz // (n_core * n_z)

    def place(dx, dz, dcore, dy):
        x = lax.rem(xpos + dx, n_x)
        z = lax.rem(zpos + dz, n_z)
        c = lax.rem(core + dcore, n_core)
        return ((x * n_z + z) * n_core + c, lax.rem(gy + dy, n_gy))

    stages = [
        [place(0, dz, dc, 0) for dz in range(n_z) for dc in range(n_core) if (dz, dc) != (0, 0)],
        [place(dx, 0, 0, dy) for dx in range(n_x) for dy in range(n_gy) if (dx, dy) != (0, 0)],
    ]
    near = [at(dz, dy) for dz, dy in ((1, 0), (-1, 0), (0, 1), (0, -1), (1, 1), (1, -1), (-1, 1), (-1, -1))]
    barrier = pltpu.get_barrier_semaphore()
    greeted = near + stages[0] + [place(dx, 0, 0, 0) for dx in range(1, n_x)]
    for device in greeted:
        pl.semaphore_signal(barrier, inc=1, device_id=device, device_id_type=MESH)

    loads = ((pop_ref, S.f0), (sol_ref, S.sol), (lab_ref, S.lab))
    for src, dst in loads:
        pltpu.make_async_copy(src, dst, S.in_sem.at[0]).start()

    sent_bytes, group_bytes = {}, {}

    def group_of(r, i):
        if i >= base:
            name = "E"
        else:
            name = "B" if i % chunks == order[-1] and r != 5 else "A"
        if r == 4 and i < base:
            name = "B" if i in (0, chunks - 1) else "A"
        if r == 1:
            near_side = i - base not in (2, 3) if i >= base else i >= chunks
            name = ("n" if near_side else "f") + name
        return (r, name)

    def send(src, dst, r, i, device):
        group = group_of(r, i)
        pltpu.make_async_remote_copy(
            src_ref=src,
            dst_ref=dst,
            send_sem=S.ssem.at[r],
            recv_sem=S.rsem.at[GROUPS.index(group)],
            device_id=device,
            device_id_type=MESH,
        ).start()
        sent_bytes[r] = sent_bytes.get(r, 0) + size(src)
        group_bytes[group] = group_bytes.get(group, 0) + size(src)

    far, near_z = 2 * core - 1, 1 - 2 * core
    upward, downward = 1 - core, core
    base = 2 * chunks
    DIAGONAL = ((1, 1), (1, -1), (-1, 1), (-1, -1))
    FAR_DIAGONAL = ((far, 1), (far, -1), (near_z, 1), (near_z, -1))

    def send_bulk(r, k):
        src, dst = pl.ds(k * ROWS, ROWS), pl.ds(TOP + k * ROWS, ROWS)
        if r in (0, 3):
            send(S.out[r].at[0, :, src, :], S.arrived[r].at[0, :, dst, :], r, k, at(far, 0))
            send(S.out[r].at[1, :, src, :], S.arrived[r].at[1, :, dst, :], r, chunks + k, at(near_z, 0))
        if r == 1:
            send(S.out1.at[0, :, dst, :], S.in1.at[0, :, dst, :], 1, k, at(far, 0))
            send(S.out1.at[1, :, dst, :], S.in1.at[1, :, dst, :], 1, chunks + k, at(near_z, 0))
        if r == 2:
            send(S.mine.at[:, src, :], S.side.at[1, :, dst, :], 2, chunks + k, at(near_z, 0))
        if r == 4:
            send(S.rest.at[:, src, :], S.far_rest.at[:, src, :], 4, k, at(far, 0))

    def send_edges(r, end):
        high = end == 1
        if r == 4:
            src, dst = (S.rest_hi, S.far_rest_hi) if high else (S.rest_lo, S.far_rest_lo)
            send(src, dst, 4, base + (2 if high else 3), at(far, end))
            return
        src, dst = (S.yu, S.ryu) if high else (S.yd, S.ryd)
        send(src[r], dst[r], r, base + (0 if high else 1), at(0, end))
        for i, (dz, dy) in enumerate(DIAGONAL if r in (0, 3) else FAR_DIAGONAL):
            if dy == end and (r != 2 or i >= 2):
                send(S.dg[r][i], S.rdg[r][i], r, base + 2 + i, at(dz, dy))

    def send_chunk(r, k):
        if k == chunks - 1:
            send_edges(r, 1)
        if k == 0:
            send_edges(r, -1)
        send_bulk(r, k)

    def sent(*rounds):
        for r in rounds:
            wait_bytes(sent_bytes[r], S.ssem.at[r])

    landed = set()

    def receive_group(r, name):
        if (r, name) not in landed:
            landed.add((r, name))
            wait_bytes(group_bytes[r, name], S.rsem.at[GROUPS.index((r, name))])

    def receive(r, k, side=""):
        receive_group(r, side + "A")
        if abs(k - order[-1]) <= 1:
            receive_group(r, side + "B")
        receive_group(r, side + "E")
        return k == order[0]

    def receive_late(r, k, side=""):
        receive_group(r, side + "A")
        receive_group(r, side + "B")
        first = k == late_order[-2]
        if first:
            receive_group(r, side + "E")
        return first

    def interior(k):
        return pl.ds(TOP + k * ROWS, ROWS)

    def moved(k, dy):
        return pl.ds(TOP + k * ROWS - dy, ROWS)

    def emit_populations(r, k, values, sense):
        here = pl.ds(k * ROWS, ROWS)
        for side, table in ((upward, UP), (downward, DOWN)):
            for i, d in enumerate(table):
                q = INDEX[tuple(sense * e for e in d)]
                value = roll_x(values[q], d[0])
                S.out[r][side, i, here, :] = value
                slot = DIAGONAL.index((d[2], d[1])) if d[1] else None
                if d[1] == 1 and k == chunks - 1:
                    S.dg[r][slot][...] = value[ROWS - 1 :, :]
                if d[1] == -1 and k == 0:
                    S.dg[r][slot][...] = value[:1, :]
        for i, d in enumerate(FLAT):
            q = INDEX[tuple(sense * e for e in d)]
            value = roll_x(values[q], d[0])
            S.flat[r][i, interior(k), :] = value
            if d[1] == 1 and k == chunks - 1:
                j = FLAT_UP.index(d)
                S.yu[r][j : j + 1, :] = value[ROWS - 1 :, :]
            if d[1] == -1 and k == 0:
                j = FLAT_DOWN.index(d)
                S.yd[r][j : j + 1, :] = value[:1, :]

    def place_edges(r):
        for i, side, row in ((0, downward, TOP - 1), (1, downward, last), (2, upward, TOP - 1), (3, upward, last)):
            slot = 3 if i % 2 == 0 else 4
            S.arrived[r][side, slot, pl.ds(row, 1), :] = S.rdg[r][i][...]
        for j in range(3):
            S.flat[r][FLAT.index(FLAT_UP[j]), pl.ds(TOP - 1, 1), :] = S.ryu[r][j : j + 1, :]
            S.flat[r][FLAT.index(FLAT_DOWN[j]), pl.ds(last, 1), :] = S.ryd[r][j : j + 1, :]

    def gather_populations(r, k, sense):
        values = [None] * 19
        for i, d in enumerate(FLAT):
            values[INDEX[tuple(sense * e for e in d)]] = S.flat[r][i, moved(k, d[1]), :]
        for side, table in ((downward, UP), (upward, DOWN)):
            for i, d in enumerate(table):
                values[INDEX[tuple(sense * e for e in d)]] = S.arrived[r][side, i, moved(k, d[1]), :]
        return values

    def coefficients(k):
        here = pl.ds(k * ROWS, ROWS)
        return [S.coef[i, here, :] for i in range(3)]

    def inlet(k):
        return jnp.where(S.lab[0, pl.ds(k * ROWS, ROWS), :] == 3, 1.0, 0.0)

    wait_bytes(sum(size(dst) for src, dst in loads), S.in_sem.at[0])
    for k in order:
        here = pl.ds(k * ROWS, ROWS)
        label = S.lab[0, here, :]
        s = jnp.where(label == 1, S.sol[0, here, :], jnp.where(label == 2, 1.0, 0.0))
        free = jnp.where(label == 3, 0.0, 1.0 - s)
        b = jnp.where(label == 4, free, OMEGA * free)
        a = jnp.where(label == 4, 0.0, (1.0 - OMEGA) * free)
        for i, value in enumerate((a, b, s)):
            S.coef[i, here, :] = value
        f = [S.f0[q, 0, here, :] for q in range(19)]
        rho, u, speed, post = collide(f, a, b, s, inlet(k))
        for i, value in enumerate((rho, *u)):
            S.mom0[i, here, :] = value
        emit_populations(0, k, post, 1)

    pl.semaphore_wait(barrier, len(greeted))
    send_edges(0, 1)
    send_edges(0, -1)
    for k in order:
        send_bulk(0, k)
    S.s_hi[...] = S.coef[2, pl.ds(rows - 1, 1), :]
    S.s_lo[...] = S.coef[2, pl.ds(0, 1), :]
    send(S.s_hi, S.far_s_hi, 5, 1, at(far, 1))
    send(S.s_lo, S.far_s_lo, 5, 2, at(far, -1))
    send(S.coef.at[2], S.far_s, 5, 0, at(far, 0))

    for k in order:
        here = pl.ds(k * ROWS, ROWS)
        if receive(0, k):
            place_edges(0)
        a, b, s = coefficients(k)
        f = gather_populations(0, k, 1)
        for q in range(19):
            S.f1[q, here, :] = f[q]
        rho, u, speed, post = collide(f, a, b, s, inlet(k))
        for i, value in enumerate((rho, *u)):
            S.mom1[i, here, :] = value
        flow = rho * speed
        S.ds[here, :] = -flow
        energy = (1.0 - s) * flow
        S.acc[...] = energy if k == order[0] else S.acc[...] + energy

        def three(cy, cz):
            mid = post[INDEX[0, cy, cz]]
            right = roll_x(post[INDEX[1, cy, cz]], 1)
            left = roll_x(post[INDEX[-1, cy, cz]], -1)
            return mid + right + left, right - left

        for slot, cz in ((upward, 1), (downward, -1)):
            total, along = three(0, cz)
            for i, value in enumerate((total, along, post[INDEX[0, 1, cz]], post[INDEX[0, -1, cz]])):
                S.out1[slot, i, interior(k), :] = value
        if k == chunks - 1:
            end = pl.ds(last - 1, 1)
            for j, (i, row) in enumerate(((0, end), (1, end), (2, pl.ds(last - 2, 1)), (2, end))):
                S.yu[1][2 + j : 3 + j, :] = S.out1[0, i, row, :]
            S.dg[1][0][...] = S.out1[0, 2, end, :]
            S.dg[1][2][...] = S.out1[1, 2, end, :]
        if k == 0:
            end = pl.ds(TOP, 1)
            for j, (i, row) in enumerate(((0, end), (1, end), (3, pl.ds(TOP + 1, 1)), (3, end))):
                S.yd[1][2 + j : 3 + j, :] = S.out1[0, i, row, :]
            S.dg[1][1][...] = S.out1[0, 3, end, :]
            S.dg[1][3][...] = S.out1[1, 3, end, :]
        for j, cy in enumerate((0, 1, -1)):
            total, along = three(cy, 0)
            S.part[2 * j, interior(k), :] = total
            S.part[2 * j + 1, interior(k), :] = along
            if cy == 1 and k == chunks - 1:
                S.yu[1][0:1, :] = total[ROWS - 1 :, :]
                S.yu[1][1:2, :] = along[ROWS - 1 :, :]
            if cy == -1 and k == 0:
                S.yd[1][0:1, :] = total[:1, :]
                S.yd[1][1:2, :] = along[:1, :]
        send_chunk(1, k)

    sent(0, 5)

    def place_halo(side, i):
        S.in1[side, 2, pl.ds(TOP - 1, 1), :] = S.rdg[1][i][...]
        S.in1[side, 3, pl.ds(last, 1), :] = S.rdg[1][i + 1][...]

    for k in late_order:
        here = pl.ds(k * ROWS, ROWS)
        if receive_late(1, k, "n"):
            place_halo(1, 2)
            for j in range(2):
                S.part[2 + j, pl.ds(TOP - 1, 1), :] = S.ryu[1][j : j + 1, :]
                S.part[4 + j, pl.ds(last, 1), :] = S.ryd[1][j : j + 1, :]
            S.out1[0, 2, pl.ds(TOP - 1, 1), :] = S.ryu[1][5:6, :]
            S.out1[0, 3, pl.ds(last, 1), :] = S.ryd[1][5:6, :]
        near_x = S.in1[1, 1, interior(k), :]
        near_a, near_b = S.in1[1, 2, moved(k, 1), :], S.in1[1, 3, moved(k, -1), :]
        mass = S.in1[1, 0, interior(k), :] + (near_a + near_b)
        mid, mid_x = S.part[0, interior(k), :], S.part[1, interior(k), :]
        ahead, ahead_x = S.part[2, moved(k, 1), :], S.part[3, moved(k, 1), :]
        behind, behind_x = S.part[4, moved(k, -1), :], S.part[5, moved(k, -1), :]
        rest = (
            mass + (mid + (ahead + behind)),
            near_x + (mid_x + (ahead_x + behind_x)),
            (near_a - near_b) + (ahead - behind),
            mass,
        )
        for i, value in enumerate(rest):
            S.rest[i, here, :] = value
            if k == chunks - 1:
                S.rest_hi[i : i + 1, :] = value[ROWS - 1 :, :]
            if k == 0:
                S.rest_lo[i : i + 1, :] = value[:1, :]
        send_chunk(4, k)

    def finish_moments(rest, total, along, ahead, behind, s):
        mass = total + (ahead + behind)
        rho = rest[0] + mass
        inv = 1.0 / rho
        u = [(rest[1] + along) * inv, (rest[2] + (ahead - behind)) * inv, (mass - rest[3]) * inv]
        speed = u[0] * u[0] + u[1] * u[1] + u[2] * u[2]
        free = 1.0 - s
        twice = 2.0 * free
        return rho, speed, [twice * v for v in u], free

    for k in late_order:
        here = pl.ds(k * ROWS, ROWS)
        if receive_late(1, k, "f"):
            place_halo(0, 0)
        rho, speed, (x, y, z), free = finish_moments(
            [S.rest[i, here, :] for i in range(4)],
            S.in1[0, 0, interior(k), :],
            S.in1[0, 1, interior(k), :],
            S.in1[0, 2, moved(k, 1), :],
            S.in1[0, 3, moved(k, -1), :],
            S.coef[2, here, :],
        )
        flow = rho * speed
        S.ds[here, :] = S.ds[here, :] - flow
        S.acc[...] = S.acc[...] + free * flow
        e = free * speed
        w = -z - e
        for i, value in enumerate((x, y, w)):
            S.mine[i, here, :] = value
        for i, value in enumerate((x, y - e, -y - e, e)):
            S.grad[i, interior(k), :] = value
        if k == chunks - 1:
            S.dg[2][2][...] = (w - y)[ROWS - 1 :, :]
            S.yu[2][0:1, :] = x[ROWS - 1 :, :]
            S.yu[2][1:2, :] = (-y - e)[ROWS - 1 :, :]
        if k == 0:
            S.dg[2][3][...] = (w + y)[:1, :]
            S.yd[2][0:1, :] = x[:1, :]
            S.yd[2][1:2, :] = (y - e)[:1, :]
        send_chunk(2, k)

    def reduce_send(stage, value):
        S.ar[stage][...] = value
        for i, device in enumerate(stages[stage]):
            pltpu.make_async_remote_copy(
                src_ref=S.ar[stage],
                dst_ref=S.arr[stage][i],
                send_sem=S.ssem.at[6 + stage],
                recv_sem=S.rsem.at[GROUPS.index((6 + stage, "A"))],
                device_id=device,
                device_id_type=MESH,
            ).start()
        sent_bytes[6 + stage] = len(stages[stage])

    def reduce_receive(stage):
        wait_bytes(len(stages[stage]), S.rsem.at[GROUPS.index((6 + stage, "A"))])
        value = S.ar[stage][...]
        for i in range(len(stages[stage])):
            value = value + S.arr[stage][i][...]
        return value

    acc = S.acc[...]
    acc = functools.reduce(lambda p, q: p + q, [acc[:, i : i + 128] for i in range(0, cols, 128)])
    reduce_send(0, jnp.sum(acc, axis=0, keepdims=True))

    zero_row = jnp.zeros((1, cols), jnp.float32)
    sent(1)

    def far_plane(rest, total, along, ahead, behind, s):
        rho, speed, (x, y, z), free = finish_moments(rest, total, along, ahead, behind, s)
        return x, y, z - free * speed

    for k in late_order:
        here = pl.ds(k * ROWS, ROWS)
        receive_group(5, "A")
        receive_group(4, "A")
        if k == late_order[-2]:
            receive_group(4, "B")
            receive_group(4, "E")
            low, high = pl.ds(TOP - 1, 1), pl.ds(last, 1)
            x, y, w = far_plane(
                [S.far_rest_hi[i : i + 1, :] for i in range(4)],
                S.ryu[1][2:3, :],
                S.ryu[1][3:4, :],
                S.ryu[1][4:5, :],
                S.out1[0, 3, pl.ds(TOP, 1), :],
                S.far_s_hi[...],
            )
            S.side[0, 1, low, :] = y
            S.side[0, 2, low, :] = w
            x, y, w = far_plane(
                [S.far_rest_lo[i : i + 1, :] for i in range(4)],
                S.ryd[1][2:3, :],
                S.ryd[1][3:4, :],
                S.out1[0, 2, pl.ds(last - 1, 1), :],
                S.ryd[1][4:5, :],
                S.far_s_lo[...],
            )
            S.side[0, 1, high, :] = y
            S.side[0, 2, high, :] = w
        value = far_plane(
            [S.far_rest[i, here, :] for i in range(4)],
            S.out1[0, 0, interior(k), :],
            S.out1[0, 1, interior(k), :],
            S.out1[0, 2, moved(k, 1), :],
            S.out1[0, 3, moved(k, -1), :],
            S.far_s[here, :],
        )
        for i in range(3):
            S.side[0, i, interior(k), :] = value[i]

    for k in order:
        here = pl.ds(k * ROWS, ROWS)
        if receive(2, k):
            for i, row in ((2, TOP - 1), (3, last)):
                S.side[1, 2, pl.ds(row, 1), :] = S.rdg[2][i][...]
                S.side[1, 1, pl.ds(row, 1), :] = zero_row
            for j, slot in ((0, 0), (1, 2)):
                S.grad[slot, pl.ds(TOP - 1, 1), :] = S.ryu[2][j : j + 1, :]
            for j, slot in ((0, 0), (1, 1)):
                S.grad[slot, pl.ds(last, 1), :] = S.ryd[2][j : j + 1, :]
        a, b, s = coefficients(k)
        mu = [None] * 19
        for slot, cz in ((upward, 1), (downward, -1)):
            x, w = S.side[slot, 0, interior(k), :], S.side[slot, 2, interior(k), :]
            mu[INDEX[0, 0, cz]] = w
            mu[INDEX[1, 0, cz]] = roll_x(w + x, -1)
            mu[INDEX[-1, 0, cz]] = roll_x(w - x, 1)
            mu[INDEX[0, 1, cz]] = S.side[slot, 2, moved(k, -1), :] + S.side[slot, 1, moved(k, -1), :]
            mu[INDEX[0, -1, cz]] = S.side[slot, 2, moved(k, 1), :] - S.side[slot, 1, moved(k, 1), :]
        for cy, slot in ((0, 3), (1, 1), (-1, 2)):
            x, w = S.grad[0, moved(k, -cy), :], S.grad[slot, moved(k, -cy), :]
            w = -w if cy == 0 else w
            mu[INDEX[0, cy, 0]] = w
            mu[INDEX[1, cy, 0]] = roll_x(w + x, -1)
            mu[INDEX[-1, cy, 0]] = roll_x(w - x, 1)
        f = [S.f1[q, here, :] for q in range(19)]
        rho, u = S.mom1[0, here, :], [S.mom1[i, here, :] for i in (1, 2, 3)]
        speed = u[0] * u[0] + u[1] * u[1] + u[2] * u[2]
        free = 1.0 - s
        twice = 2.0 * free
        extra = (-(free * speed), [twice * u[i] for i in range(3)])
        lam, by_s = collide_adjoint(mu, f, rho, u, speed, a, b, s, extra)
        S.ds[here, :] = S.ds[here, :] + by_s
        emit_populations(3, k, lam, -1)
        send_chunk(3, k)

    reduce_send(1, reduce_receive(0))
    sent(4, 2, 3, 6, 7)

    for k in late_order:
        here = pl.ds(k * ROWS, ROWS)
        if receive_late(3, k):
            place_edges(3)
        a, b, s = coefficients(k)
        mu = gather_populations(3, k, -1)
        f = [S.f0[q, 0, here, :] for q in range(19)]
        rho, u = S.mom0[0, here, :], [S.mom0[i, here, :] for i in (1, 2, 3)]
        speed = u[0] * u[0] + u[1] * u[1] + u[2] * u[2]
        lam, by_s = collide_adjoint(mu, f, rho, u, speed, a, b, s)
        for q in range(19):
            lam_ref[q, 0, here, :] = lam[q]
        sens_ref[0, here, :] = jnp.where(S.lab[0, here, :] == 1, S.ds[here, :] + by_s, 0.0)
    total = jnp.sum(reduce_receive(1), axis=1, keepdims=True)
    en_ref[...] = jnp.broadcast_to(total, en_ref.shape)


def finish(scale, lam_ref, sens_ref, en_ref, out_sens, out_lam, lam, sens, some, sems):
    inv = 1.0 / (en_ref[...] * scale)
    rows = sens.shape[1]
    for q in range(19):
        for k in range(rows // ROWS):
            here = pl.ds(k * ROWS, ROWS)
            lam[q, 0, here, :] = lam_ref[q, 0, here, :] * inv
        pltpu.make_async_copy(lam.at[pl.ds(q, 1)], out_lam.at[pl.ds(q, 1)], sems.at[0]).start()
    for k in range(rows // ROWS):
        here = pl.ds(k * ROWS, ROWS)
        sens[0, here, :] = sens_ref[0, here, :] * inv
    pltpu.make_async_copy(sens, out_sens, sems.at[0]).start()
    pltpu.make_async_copy(some, some, sems.at[0]).wait()


def on_device(sizes, populations, solid_fraction, labels):
    rows, cols = solid_fraction.shape[1:]
    n_gz, n_gy, n_x, n_z, n_core = sizes
    leaves, tree = jax.tree.flatten(scratch_tree(rows, cols, (n_core * n_z - 1, n_x * n_gy - 1)))
    f32 = jnp.float32
    in_hbm = pl.BlockSpec(memory_space=pltpu.HBM)
    in_vmem = pl.BlockSpec(memory_space=pltpu.VMEM)
    lam_type = jax.ShapeDtypeStruct(populations.shape, f32)
    sens_type = jax.ShapeDtypeStruct(solid_fraction.shape, f32)
    limit = 24 * 1024 * 1024
    lam, sens, total = pl.pallas_call(
        functools.partial(kernel, tree, sizes),
        out_shape=(lam_type, sens_type, jax.ShapeDtypeStruct((ROWS, cols), f32)),
        in_specs=[in_hbm] * 3,
        out_specs=(in_vmem,) * 3,
        scratch_shapes=leaves,
        compiler_params=pltpu.CompilerParams(collective_id=0, has_side_effects=True, vmem_limit_bytes=limit),
        name="lattice",
    )(*[pltpu.with_memory_space_constraint(v, pltpu.HBM) for v in (populations, solid_fraction, labels)])
    scale = 1.0 / (STEPS * n_gz * n_gy * rows * cols)
    return pl.pallas_call(
        functools.partial(finish, scale),
        out_shape=(sens_type, lam_type),
        in_specs=[in_vmem] * 3,
        out_specs=(in_hbm,) * 2,
        scratch_shapes=[
            pltpu.VMEM(populations.shape, f32),
            pltpu.VMEM(solid_fraction.shape, f32),
            pltpu.VMEM((20 * rows * cols // LANES, 1, LANES), f32),
            pltpu.SemaphoreType.DMA((1,)),
        ],
        compiler_params=pltpu.CompilerParams(vmem_limit_bytes=4 * 1024 * 1024),
        name="finish",
    )(lam, sens, total)


def solution(mesh):
    n_gz, n_gy = mesh.shape["gz"], mesh.shape["gy"]
    n_core = 2
    n_z = 8 if n_gz % 16 == 0 else n_gz // 2
    n_x = n_gz // (n_core * n_z)
    in_specs = (P(None, "gz", "gy", None), P("gz", "gy", None), P("gz", "gy", None))
    out_specs = (P("gz", "gy", None), P(None, "gz", "gy", None))
    return jax.shard_map(
        functools.partial(on_device, (n_gz, n_gy, n_x, n_z, n_core)),
        mesh=mesh,
        in_specs=in_specs,
        out_specs=out_specs,
        check_vma=False,
    )
```
